128 devices in a mesh: grp: 8 (over z, x_hi), tile: 16 (over x_lo, y, core).
Axes of the slice: x: 4 (x_hi: 2, x_lo: 2; x = x_hi * 2 + x_lo), y: 4, z: 4, core: 2. Of those that a mesh axis runs over, the one named last changes fastest.
Arguments:
- ens_control: float32 [16, 32, 256, 128], P('grp', None, 'tile'), may hold values from -6 to 6
- static_control: float32 [8, 5, 32, 256, 128], P('grp', None, None, 'tile'), may hold values from -6 to 6
- member_perturb: bfloat16 [16, 5, 32, 256, 128], P('grp', None, None, 'tile'), may hold values from -5 to 5
- member_group: int32 [16], P('grp'), may hold values from 0 to 11
- localize_rate: float32 [12], replicated, may hold values from 0.04 to 0.24
- static_rate: float32 [8], P('grp'), may hold values from 0.04 to 0.24
- static_scale: float32 [8, 5, 32], P('grp'), may hold values from 0.2 to 2
- obs_index: int32 [65536], P('tile'), may hold values from 0 to 2047
- obs_frac: float32 [65536], P('tile'), may hold values from 0 to 1
- obs_layer: int32 [65536], P('tile'), may hold values from 0 to 159
- obs_kind: int32 [65536], P('tile'), may hold values from 0 to 7
- obs_precision: float32 [8], replicated, may hold values from 0.5 to 8
Outputs:
- hv_ensemble: float32 [16, 32, 256, 128], P('grp', None, 'tile')
- hv_static: float32 [8, 5, 32, 256, 128], P('grp', None, None, 'tile')
The draws below stay inside these ranges and needn't reach their ends.
All inputs are finite; a program needn't handle non-finite values.
Results may differ from the reference program's by a relative error of at most 0.0003.
Values sent between devices are 32-bit elements; how exact they have to be, the bound alone decides.
No kernel may reach another device: no remote copies, remote signals or barrier semaphores. Data moves between devices by JAX's collectives and lax.ppermute only.
A program may use at most 64 MiB of HBM per device.

```python
import math
import jax
import jax.numpy as jnp
from jax import lax

NVAR = 5
NZ = 32
HX = 16
HY = 128
LGROUPS = 12
KINDS = 8
SWEEPS = 4
OBS_DEV = 4096
MEMBERS = 16
NX = 256
NY = 128
OBS = 65536
N_GRP = 8
N_TILE = 16


def touch_ends(drawn, key, smallest, top_value):
    shape = drawn.shape
    spot = [jax.random.randint(jax.random.fold_in(key, axis), (), 0, shape[axis]) for axis in range(len(shape))]
    drawn = drawn.at[tuple(spot)].set(smallest)
    longest = shape.index(max(shape))
    spot[longest] = (spot[longest] + 1) % shape[longest]
    return drawn.at[tuple(spot)].set(top_value)


def level_of(key, extent, shards, smallest, high):
    level = 1.0
    for position, parts in shards:
        draws = jax.random.uniform(jax.random.fold_in(jax.random.fold_in(key, 6), position), (parts,), jnp.float32, smallest / len(shards), high / len(shards))
        level = level * jnp.repeat(jnp.exp(draws), extent[position] // parts).reshape((-1,) + (1,) * (len(extent) - 1 - position))
    return level


def centred(stream_key, extent, scale, limit, pieces=(), kind=jnp.bfloat16):
    factor_of = level_of(stream_key, extent, pieces, -0.22, 0.18) if pieces else 1.0
    result = jax.random.normal(stream_key, extent, jnp.float32) * scale * factor_of
    return jnp.minimum(jnp.maximum(result, -limit), limit).astype(kind)


def setup_inputs(seed: int = 0) -> dict:
    arg_keys = jax.random.split(jax.random.key(seed), 13)
    return {
        "ens_control": centred(arg_keys[0], (MEMBERS, NZ, NX, NY), 1.0, 6.0, ((0, 8), (2, 16)), jnp.float32),
        "static_control": centred(arg_keys[1], (N_GRP, NVAR, NZ, NX, NY), 1.0, 6.0, ((0, 8), (3, 16)), jnp.float32),
        "member_perturb": centred(arg_keys[2], (MEMBERS, NVAR, NZ, NX, NY), 0.35, 5.0, ((0, 8), (3, 16))),
        "member_group": touch_ends(jax.random.randint(arg_keys[3], (MEMBERS,), 0, LGROUPS), jax.random.fold_in(arg_keys[3], 1), 0, LGROUPS - 1).astype(jnp.int32),
        "localize_rate": jnp.clip(jnp.exp(jax.random.uniform(arg_keys[4], (LGROUPS,), jnp.float32, math.log(0.04), math.log(0.24))), 0.04, 0.24),
        "static_rate": jnp.clip(jnp.exp(math.log(0.24) - 1.7917595 * jax.random.uniform(arg_keys[5], (N_GRP,), jnp.float32) ** level_of(arg_keys[5], (N_GRP,), ((0, 8),), -0.2, 0.2)), 0.04, 0.24),
        "static_scale": jnp.clip(jnp.exp(math.log(2.0) - 2.3025851 * jax.random.uniform(arg_keys[6], (N_GRP, NVAR, NZ), jnp.float32) ** level_of(arg_keys[6], (N_GRP, NVAR, NZ), ((0, 8),), -0.2, 0.2)), 0.2, 2.0),
        "obs_index": touch_ends(jax.random.randint(arg_keys[7], (OBS,), 0, HX * HY), jax.random.fold_in(arg_keys[7], 1), 0, (HX * HY) - 1).astype(jnp.int32),
        "obs_frac": jnp.clip(1.0 * jax.random.uniform(arg_keys[8], (OBS,), jnp.float32) ** level_of(arg_keys[8], (OBS,), ((0, 16),), -0.2, 0.2), 0.0, 1.0),
        "obs_layer": touch_ends(jax.random.randint(arg_keys[9], (OBS,), 0, NVAR * NZ), jax.random.fold_in(arg_keys[9], 1), 0, (NVAR * NZ) - 1).astype(jnp.int32),
        "obs_kind": touch_ends(jax.random.randint(arg_keys[10], (OBS,), 0, KINDS), jax.random.fold_in(arg_keys[10], 1), 0, KINDS - 1).astype(jnp.int32),
        "obs_precision": jnp.clip(jnp.exp(jax.random.uniform(arg_keys[11], (KINDS,), jnp.float32, math.log(0.5), math.log(8.0))), 0.5, 8.0),
    }


def diffuse(field, rate):
    for number in range(SWEEPS):
        padded = jnp.pad(field, [(0, 0)] * (field.ndim - 2) + [(1, 1), (1, 1)])
        beside = padded[..., 2:, 1:-1] + padded[..., :-2, 1:-1]
        beside = beside + padded[..., 1:-1, 2:] + padded[..., 1:-1, :-2]
        field = field + rate * (beside - 4.0 * field)
    return field


def reference(ens_control, static_control, member_perturb, member_group, localize_rate, static_rate, static_scale, obs_index, obs_frac, obs_layer, obs_kind, obs_precision):
    member_rate = localize_rate[member_group]
    smoothed = lax.map(lambda pair: diffuse(pair[0], pair[1]), (ens_control, member_rate))

    def add_member(total, pair):
        return total + pair[0].astype(jnp.float32) * pair[1][None], None

    increment, unused = lax.scan(add_member, jnp.zeros((NVAR, NZ, NX, NY), jnp.float32), (member_perturb, smoothed))

    def add_static(total, trio):
        return total + trio[2][:, :, None, None] * diffuse(trio[0], trio[1]), None

    increment, unused = lax.scan(add_static, increment, (static_control, static_rate, static_scale))
    tile_cells = increment.reshape(NVAR, NZ, N_TILE, HX, NY).transpose(2, 0, 1, 3, 4).reshape(N_TILE, -1)
    base = (obs_layer * (HX * HY)).astype(jnp.int32)
    next_index = ((obs_index // HY) * HY + (obs_index % HY + 1) % HY).astype(jnp.int32)
    spots = (base + obs_index).astype(jnp.int32).reshape(N_TILE, OBS_DEV)
    spots_next = (base + next_index).astype(jnp.int32).reshape(N_TILE, OBS_DEV)
    frac = obs_frac.reshape(N_TILE, OBS_DEV)
    weight = obs_precision[obs_kind].reshape(N_TILE, OBS_DEV)
    seen = (1.0 - frac) * jnp.take_along_axis(tile_cells, spots, axis=1) + frac * jnp.take_along_axis(tile_cells, spots_next, axis=1)
    tile_rows = jnp.broadcast_to(jnp.arange(N_TILE, dtype=jnp.int32)[:, None], spots.shape)
    valued = weight * seen
    placed = jnp.zeros_like(tile_cells).at[tile_rows, spots].add((1.0 - frac) * valued)
    placed = placed.at[tile_rows, spots_next].add(frac * valued)
    gradient = placed.reshape(N_TILE, NVAR, NZ, HX, NY).transpose(1, 2, 0, 3, 4).reshape(NVAR, NZ, NX, NY)
    hv_ensemble = lax.map(lambda trio: trio[1] + diffuse(jnp.sum(trio[0].astype(jnp.float32) * gradient, 0), trio[2]), (member_perturb, ens_control, member_rate))
    hv_static = lax.map(lambda trio: trio[0] + diffuse(trio[2][:, :, None, None] * gradient, trio[1]), (static_control, static_rate, static_scale))
    return hv_ensemble, hv_static
```

```python
import jax
import jax.numpy as jnp
from jax import lax
from jax.experimental import pallas as pl
from jax.experimental.pallas import tpu as pltpu
from jax.sharding import PartitionSpec as P

SWEEPS = 4
BLOCK = 256
ALIGN = 16


def sweep(planes, wanted, rows, rate, inside):
    shape = next(iter(planes.values())).shape
    cells = shape[1]
    lane = lax.broadcasted_iota(jnp.int32, shape, 1)
    factors = [(1.0 - 4.0 * rate, rate)] + [((1.0 - 4.0 * rate) * side, rate * side) for side in inside]
    swept = {}
    for x in wanted:
        keep, share = factors[1 if x < 0 else 2 if x >= rows else 0]
        here = planes.get(x)
        beside = [planes[near] for near in (x - 1, x + 1) if near in planes]
        if here is not None:
            beside.append(jnp.where(lane == 0, 0.0, pltpu.roll(here, 1, 1)))
            beside.append(jnp.where(lane == cells - 1, 0.0, pltpu.roll(here, cells - 1, 1)))
        if not beside:
            continue
        total = beside[0]
        for more in beside[1:]:
            total = total + more
        swept[x] = share * total if here is None else keep * here + share * total
    return swept


def spread(planes, first, last, rows, rate, inside):
    for left in range(SWEEPS - 1, -1, -1):
        planes = sweep(planes, range(first - left, last + left + 1), rows, rate, inside)
    return planes


def plane_rows(chunk, at, rows):
    return pl.ds(chunk * 8 * rows + at, 8, stride=rows)


def weights_of(key, frac, cells):
    cell = key & (cells - 1)
    second = (cell + 1) & (cells - 1)
    spot = lax.broadcasted_iota(jnp.int32, (cells, key.shape[1]), 0)
    return jnp.where(spot == cell, 1.0 - frac, jnp.where(spot == second, frac, 0.0))


def chosen_rows(key, start, shift):
    row = (key >> shift) - start
    spot = lax.broadcasted_iota(jnp.int32, (BLOCK, key.shape[1]), 0)
    return jnp.where(spot == row, 1.0, 0.0).astype(jnp.bfloat16)


def halves(value):
    high = value.astype(jnp.bfloat16)
    low = (value - high.astype(jnp.float32)).astype(jnp.bfloat16)
    return high, low


def further_windows(first_row, last_row, blocks, visit):
    def of_block(block, carry):
        start = first_row[block]
        count = (last_row[block] - start) // BLOCK + 1

        def of_window(window, inner):
            visit(block, start + window * BLOCK)
            return inner

        return lax.fori_loop(1, count, of_window, carry)

    lax.fori_loop(0, blocks, of_block, 0)


def forward_kernel(dims, ens, stat, perturb, scale, side_a, side_b, key, frac, rate, inside, parity, first_row, last_row, more, out, smooth, table):
    members, nvars, levels, rows, cells, blocks, copies = dims
    shift = cells.bit_length() - 1
    even = parity[0] == 1

    def halo(field, chunk, j):
        a = side_a[field, plane_rows(chunk, j, SWEEPS), :]
        b = side_b[field, plane_rows(chunk, j, SWEEPS), :]
        return jnp.where(even, b, a), jnp.where(even, a, b)

    def smooth_field(source, at, field, factor):
        def of_chunk(chunk, carry):
            planes = {x: source[at, plane_rows(chunk, x, rows), :] for x in range(rows)}
            for j in range(SWEEPS):
                planes[j - SWEEPS], planes[rows + j] = halo(field, chunk, j)
            planes = spread(planes, 0, rows - 1, rows, rate[field], (inside[0], inside[1]))
            for x in range(rows):
                value = planes[x]
                if factor:
                    value = value * scale[at, pl.ds(chunk * 8, 8), :]
                smooth[field, plane_rows(chunk, x, rows), :] = value
            return carry

        lax.fori_loop(0, levels // 8, of_chunk, 0)

    def of_member(m, carry):
        smooth_field(ens, m, m, False)
        return carry

    def of_group(v, carry):
        smooth_field(stat, v, members + v, True)
        return carry

    lax.fori_loop(0, members, of_member, 0)
    lax.fori_loop(0, nvars, of_group, 0)
    plane = levels * rows
    for v in range(nvars):
        total = smooth[members + v]
        for m in range(members):
            total = total + perturb[m, v].astype(jnp.float32) * smooth[m]
        high, low = halves(total)
        table[v * plane : (v + 1) * plane, :cells] = high
        table[v * plane : (v + 1) * plane, cells:] = low
    table[nvars * plane :, :] = jnp.zeros((BLOCK, 2 * cells), jnp.bfloat16)

    def seen_in(block, start):
        keys = key[pl.ds(block, 1), :]
        picked = lax.dot_general(
            table[pl.ds(pl.multiple_of(start, ALIGN), BLOCK), :],
            chosen_rows(keys, start, shift),
            (((0,), (0,)), ((), ())),
            preferred_element_type=jnp.float32,
        )
        picked = picked[:cells] + picked[cells:]
        return jnp.sum(picked * weights_of(keys, frac[pl.ds(block, 1), :], cells), axis=0, keepdims=True)

    for block in range(blocks):
        out[0, pl.ds(block, 1), :] = seen_in(block, first_row[block])

    @pl.when(more[0] != 0)
    def _():
        def visit(block, start):
            out[0, pl.ds(block, 1), :] = out[0, pl.ds(block, 1), :] + seen_in(block, start)

        further_windows(first_row, last_row, blocks, visit)

    for copy in range(1, copies):
        out[copy] = out[0]


def scatter_kernel(dims, parts, key, frac, weight, perturb, scale, parity, first_row, last_row, more, source, side_a, side_b, gradient, valued):
    members, nvars, levels, rows, cells, blocks, copies = dims
    shift = cells.bit_length() - 1
    seen = parts[0]
    for copy in range(1, copies):
        seen = seen + parts[copy]
    valued[...] = seen * weight[...]
    gradient[...] = jnp.zeros(gradient.shape, jnp.float32)

    def add_block(block, start):
        keys = key[pl.ds(block, 1), :]
        placed = weights_of(keys, frac[pl.ds(block, 1), :], cells) * valued[pl.ds(block, 1), :]
        high, low = halves(placed)
        both = lax.dot_general(
            chosen_rows(keys, start, shift),
            jnp.concatenate([high, low], axis=0),
            (((1,), (1,)), ((), ())),
            preferred_element_type=jnp.float32,
        )
        at = pl.ds(pl.multiple_of(start, ALIGN), BLOCK)
        gradient[at, :] = gradient[at, :] + (both[:, :cells] + both[:, cells:])

    for block in range(blocks):
        add_block(block, first_row[block])

    @pl.when(more[0] != 0)
    def _():
        further_windows(first_row, last_row, blocks, add_block)

    plane = levels * rows
    for m in range(members):
        total = perturb[m, 0].astype(jnp.float32) * gradient[:plane, :]
        for v in range(1, nvars):
            total = total + perturb[m, v].astype(jnp.float32) * gradient[v * plane : (v + 1) * plane, :]
        source[m] = total
    for v in range(nvars):
        for x in range(rows):
            at = pl.ds(x, levels, stride=rows)
            source[members + v, at, :] = gradient[pl.ds(v * plane + x, levels, stride=rows), :] * scale[v]
    even = parity[0] == 1
    begin_a = jnp.where(even, rows - SWEEPS, 0)
    begin_b = jnp.where(even, 0, rows - SWEEPS)
    for field in range(members + nvars):
        for j in range(SWEEPS):
            side_a[field, pl.ds(j, levels, stride=SWEEPS), :] = source[field, pl.ds(begin_a + j, levels, stride=rows), :]
            side_b[field, pl.ds(j, levels, stride=SWEEPS), :] = source[field, pl.ds(begin_b + j, levels, stride=rows), :]


def local_kernel(dims, source, ens, stat, rate, inside, hv_ens, hv_stat):
    members, nvars, levels, rows, cells, blocks, copies = dims

    def field_of(control, out, at, field):
        def of_chunk(chunk, carry):
            planes = {x: source[field, plane_rows(chunk, x, rows), :] for x in range(rows)}
            planes = spread(planes, 0, rows - 1, rows, rate[field], (inside[0], inside[1]))
            for x in range(rows):
                spot = plane_rows(chunk, x, rows)
                out[at, spot, :] = control[at, spot, :] + planes[x]
            return carry

        lax.fori_loop(0, levels // 8, of_chunk, 0)

    def of_member(m, carry):
        field_of(ens, hv_ens, m, m)
        return carry

    def of_group(v, carry):
        field_of(stat, hv_stat, v, members + v)
        return carry

    lax.fori_loop(0, members, of_member, 0)
    lax.fori_loop(0, nvars, of_group, 0)


def edge_kernel(dims, hv_ens_in, hv_stat_in, side_a, side_b, rate, parity, hv_ens, hv_stat):
    members, nvars, levels, rows, cells, blocks, copies = dims
    even = parity[0] == 1

    def field_of(before, out, at, field):
        def of_chunk(chunk, carry):
            lower, upper = {}, {}
            for j in range(SWEEPS):
                a = side_a[field, plane_rows(chunk, j, SWEEPS), :]
                b = side_b[field, plane_rows(chunk, j, SWEEPS), :]
                lower[j - SWEEPS] = jnp.where(even, b, a)
                upper[rows + j] = jnp.where(even, a, b)
            lower = spread(lower, 0, SWEEPS - 1, rows, rate[field], (1.0, 1.0))
            upper = spread(upper, rows - SWEEPS, rows - 1, rows, rate[field], (1.0, 1.0))
            for x in range(rows):
                spot = plane_rows(chunk, x, rows)
                value = before[at, spot, :]
                if x < SWEEPS:
                    value = value + lower[x]
                if x >= rows - SWEEPS:
                    value = value + upper[x]
                out[at, spot, :] = value
            return carry

        lax.fori_loop(0, levels // 8, of_chunk, 0)

    def of_member(m, carry):
        field_of(hv_ens_in, hv_ens, m, m)
        return carry

    def of_group(v, carry):
        field_of(hv_stat_in, hv_stat, v, members + v)
        return carry

    lax.fori_loop(0, members, of_member, 0)
    lax.fori_loop(0, nvars, of_group, 0)


def exchange(side_a, side_b):
    count = lax.axis_size("tile")
    pairs_a = [(i, i ^ 1) for i in range(count)]
    pairs_b = [(i, ((i + 1) ^ 1) - 1) for i in range(1, count - 1)]
    return lax.ppermute(side_a, "tile", pairs_a), lax.ppermute(side_b, "tile", pairs_b)


VMEM = pl.BlockSpec(memory_space=pltpu.VMEM)
SMEM = pl.BlockSpec(memory_space=pltpu.SMEM)


def call(kernel, dims, outs, ins, scalars, scratch=(), aliases={}, cost=2_000_000):
    def body(*refs):
        kernel(dims, *refs)

    return pl.pallas_call(
        body,
        out_shape=tuple(jax.ShapeDtypeStruct(shape, jnp.float32) for shape in outs),
        in_specs=[VMEM] * len(ins) + [SMEM] * len(scalars),
        out_specs=tuple([VMEM] * len(outs)),
        scratch_shapes=list(scratch),
        input_output_aliases=aliases,
        compiler_params=pltpu.CompilerParams(vmem_limit_bytes=48 * 1024 * 1024),
        cost_estimate=pl.CostEstimate(flops=cost * 10, bytes_accessed=cost, transcendentals=0),
        name=kernel.__name__,
    )(*ins, *scalars)


def per_device(
    ens_control,
    static_control,
    member_perturb,
    member_group,
    localize_rate,
    static_rate,
    static_scale,
    obs_index,
    obs_frac,
    obs_layer,
    obs_kind,
    obs_precision,
):
    members, levels, rows, cells = ens_control.shape
    nvars = static_control.shape[1]
    fields = members + nvars
    copies = lax.axis_size("grp")
    blocks = obs_index.shape[0] // BLOCK
    dims = (members, nvars, levels, rows, cells, blocks, copies)
    plane = levels * rows

    tile = lax.axis_index("tile")
    inside = jnp.stack([tile > 0, tile < lax.axis_size("tile") - 1]).astype(jnp.float32)
    even = tile % 2 == 0
    parity = even.astype(jnp.int32).reshape(1)
    begin_a = jnp.where(even, rows - SWEEPS, 0)
    begin_b = jnp.where(even, 0, rows - SWEEPS)

    def side(begin):
        parts = [
            lax.dynamic_slice_in_dim(ens_control, begin, SWEEPS, axis=2),
            lax.dynamic_slice_in_dim(static_control[0], begin, SWEEPS, axis=2),
        ]
        return jnp.concatenate(parts, 0).reshape(fields, levels * SWEEPS, cells)

    side_a, side_b = exchange(side(begin_a), side(begin_b))

    group_ids = jnp.arange(localize_rate.shape[0], dtype=jnp.int32)
    member_rate = jnp.sum(
        jnp.where(member_group[:, None] == group_ids[None, :], localize_rate[None, :], 0.0), axis=1
    )
    rate = jnp.concatenate([member_rate, jnp.broadcast_to(static_rate, (nvars,))])
    scale = jnp.broadcast_to(static_scale[0][:, :, None], (nvars, levels, cells))

    kind_ids = jnp.arange(obs_precision.shape[0], dtype=jnp.int32)
    weight = jnp.sum(
        jnp.where(obs_kind[:, None] == kind_ids[None, :], obs_precision[None, :], 0.0), axis=1
    )
    key = obs_layer * (rows * cells) + obs_index
    key, frac, weight = lax.sort((key, obs_frac, weight), num_keys=1, is_stable=False)
    key, frac, weight = (x.reshape(blocks, BLOCK) for x in (key, frac, weight))
    first_row = key[:, 0] // cells // ALIGN * ALIGN
    last_row = key[:, -1] // cells
    more = jnp.any(last_row - first_row >= BLOCK).astype(jnp.int32).reshape(1)

    ens = ens_control.reshape(members, plane, cells)
    stat = static_control.reshape(nvars, plane, cells)
    perturb = member_perturb.reshape(members, nvars, plane, cells)
    table_rows = nvars * plane + BLOCK
    (seen,) = call(
        forward_kernel,
        dims,
        [(copies, blocks, BLOCK)],
        [ens, stat, perturb, scale, side_a, side_b, key, frac],
        [rate, inside, parity, first_row, last_row, more],
        [pltpu.VMEM((fields, plane, cells), jnp.float32), pltpu.VMEM((table_rows, 2 * cells), jnp.bfloat16)],
    )
    parts = lax.all_to_all(seen, "grp", 0, 0)
    source, side_a, side_b = call(
        scatter_kernel,
        dims,
        [(fields, plane, cells), (fields, levels * SWEEPS, cells), (fields, levels * SWEEPS, cells)],
        [parts, key, frac, weight, perturb, scale],
        [parity, first_row, last_row, more],
        [pltpu.VMEM((table_rows, cells), jnp.float32), pltpu.VMEM((blocks, BLOCK), jnp.float32)],
    )
    side_a, side_b = exchange(side_a, side_b)
    shapes = [(members, plane, cells), (nvars, plane, cells)]
    hv_ens, hv_stat = call(local_kernel, dims, shapes, [source, ens, stat], [rate, inside])
    hv_ens, hv_stat = call(
        edge_kernel, dims, shapes, [hv_ens, hv_stat, side_a, side_b], [rate, parity], aliases={0: 0, 1: 1}
    )
    return hv_ens.reshape(ens_control.shape), hv_stat.reshape(static_control.shape)


def solution(mesh):
    placed = (
        P("grp", None, "tile", None),
        P("grp", None, None, "tile", None),
        P("grp", None, None, "tile", None),
        P("grp"),
        P(),
        P("grp"),
        P("grp", None, None),
        P("tile"),
        P("tile"),
        P("tile"),
        P("tile"),
        P(),
    )
    return jax.shard_map(
        per_device,
        mesh=mesh,
        in_specs=placed,
        out_specs=(P("grp", None, "tile", None), P("grp", None, None, "tile", None)),
        check_vma=False,
    )
```

```python
import jax
import jax.numpy as jnp
from jax import lax
from jax.experimental import pallas as pl
from jax.experimental.pallas import tpu as pltpu
from jax.sharding import PartitionSpec as P

SWEEPS = 4
BLOCK = 256
ALIGN = 16


def sweep(planes, wanted, rows, rate, inside):
    shape = next(iter(planes.values())).shape
    cells = shape[1]
    lane = lax.broadcasted_iota(jnp.int32, shape, 1)
    factors = [(1.0 - 4.0 * rate, rate)] + [((1.0 - 4.0 * rate) * side, rate * side) for side in inside]
    swept = {}
    for x in wanted:
        keep, share = factors[1 if x < 0 else 2 if x >= rows else 0]
        here = planes.get(x)
        beside = [planes[near] for near in (x - 1, x + 1) if near in planes]
        if here is not None:
            beside.append(jnp.where(lane == 0, 0.0, pltpu.roll(here, 1, 1)))
            beside.append(jnp.where(lane == cells - 1, 0.0, pltpu.roll(here, cells - 1, 1)))
        if not beside:
            continue
        total = beside[0]
        for more in beside[1:]:
            total = total + more
        swept[x] = share * total if here is None else keep * here + share * total
    return swept


def spread(planes, first, last, rows, rate, inside):
    for left in range(SWEEPS - 1, -1, -1):
        planes = sweep(planes, range(first - left, last + left + 1), rows, rate, inside)
    return planes


def rate_of(field, members, group, localize, static):
    if field is None:
        return static[0]
    return localize[group[field]]


def neighbours():
    tile = lax.axis_index("tile")
    last = lax.axis_size("tile") - 1
    return jnp.where(tile > 0, 1.0, 0.0), jnp.where(tile < last, 1.0, 0.0)


def is_even():
    return lax.axis_index("tile") % 2 == 0


def begins(rows):
    even = is_even()
    return jnp.where(even, rows - SWEEPS, 0), jnp.where(even, 0, rows - SWEEPS)


def sides_of(side_a, side_b, field, levels):
    even = is_even()
    lower, upper = [], []
    for j in range(SWEEPS):
        a = side_a[field, pl.ds(j * levels, levels), :]
        b = side_b[field, pl.ds(j * levels, levels), :]
        lower.append(jnp.where(even, b, a))
        upper.append(jnp.where(even, a, b))
    return lower, upper


def block_of(ref, block):
    lanes = ref.shape[1]
    parts = BLOCK // lanes
    return jnp.concatenate([ref[pl.ds(block * parts + part, 1), :] for part in range(parts)], axis=1)


def weights_of(key, frac, cells):
    cell = key & (cells - 1)
    second = (cell + 1) & (cells - 1)
    spot = lax.broadcasted_iota(jnp.int32, (cells, key.shape[1]), 0)
    return jnp.where(spot == cell, 1.0 - frac, jnp.where(spot == second, frac, 0.0))


def chosen_rows(key, start, shift):
    row = (key >> shift) - start
    spot = lax.broadcasted_iota(jnp.int32, (BLOCK, key.shape[1]), 0)
    return jnp.where(spot == row, 1.0, 0.0).astype(jnp.bfloat16)


def halves(value):
    high = value.astype(jnp.bfloat16)
    low = (value - high.astype(jnp.float32)).astype(jnp.bfloat16)
    return high, low


def window_of(bound, block, cells):
    parts = BLOCK // bound.shape[1]
    shift = cells.bit_length() - 1
    start = ((bound[block * parts, 0] >> shift) // ALIGN) * ALIGN
    last = bound[block * parts + parts - 1, bound.shape[1] - 1] >> shift
    return start, (last - start) // BLOCK + 1


def every_window(bound, blocks, cells, visit, visit_again):
    most = 1
    for block in range(blocks):
        start, count = window_of(bound, block, cells)
        most = jnp.maximum(most, count)
        visit(block, start)

    @pl.when(most > 1)
    def _():
        def of_block(block, carry):
            start, count = window_of(bound, block, cells)

            def of_window(window, inner):
                visit_again(block, start + window * BLOCK)
                return inner

            return lax.fori_loop(1, count, of_window, carry)

        lax.fori_loop(0, blocks, of_block, 0)


def each_field(members, nvars, visit):
    def of_member(m, carry):
        visit(True, m, m)
        return carry

    def of_group(v, carry):
        visit(False, v, members + v)
        return carry

    lax.fori_loop(0, members, of_member, 0)
    lax.fori_loop(0, nvars, of_group, 0)


def pack_kernel(dims, ens, stat, side_a, side_b):
    members, nvars, levels, rows, cells, blocks, copies = dims
    for begin, side in zip(begins(rows), (side_a, side_b)):
        for field in range(members + nvars):
            for j in range(SWEEPS):
                source, at = (ens, field) if field < members else (stat, field - members)
                side[field, pl.ds(j * levels, levels), :] = source[at, pl.ds(begin + j, levels, stride=rows), :]


def forward_kernel(dims, ens, stat, perturb, scale, side_a, side_b, key, frac, bound, group, localize, static, out, smooth, table):
    members, nvars, levels, rows, cells, blocks, copies = dims
    shift = cells.bit_length() - 1
    inside = neighbours()

    def of_field(member, at, field):
        source = ens if member else stat
        planes = {x: source[at, pl.ds(x, levels, stride=rows), :] for x in range(rows)}
        lower, upper = sides_of(side_a, side_b, field, levels)
        for j in range(SWEEPS):
            planes[j - SWEEPS], planes[rows + j] = lower[j], upper[j]
        rate = rate_of(field if member else None, members, group, localize, static)
        planes = spread(planes, 0, rows - 1, rows, rate, inside)
        for x in range(rows):
            value = planes[x] if member else planes[x] * scale[at]
            smooth[field, pl.ds(x, levels, stride=rows), :] = value

    each_field(members, nvars, of_field)
    plane = levels * rows
    for v in range(nvars):
        total = smooth[members + v]
        for m in range(members):
            total = total + perturb[m, v].astype(jnp.float32) * smooth[m]
        high, low = halves(total)
        table[v * plane : (v + 1) * plane, :cells] = high
        table[v * plane : (v + 1) * plane, cells:] = low
    table[nvars * plane :, :] = jnp.zeros((BLOCK, 2 * cells), jnp.bfloat16)
    lanes = key.shape[1]
    parts = BLOCK // lanes

    def seen_in(block, start):
        keys = block_of(key, block)
        picked = lax.dot_general(
            table[pl.ds(pl.multiple_of(start, ALIGN), BLOCK), :],
            chosen_rows(keys, start, shift),
            (((0,), (0,)), ((), ())),
            preferred_element_type=jnp.float32,
        )
        picked = picked[:cells] + picked[cells:]
        return jnp.sum(picked * weights_of(keys, block_of(frac, block), cells), axis=0, keepdims=True)

    def visit(block, start):
        seen = seen_in(block, start)
        for part in range(parts):
            out[0, pl.ds(block * parts + part, 1), :] = seen[:, part * lanes : (part + 1) * lanes]

    def visit_again(block, start):
        seen = seen_in(block, start)
        for part in range(parts):
            at = pl.ds(block * parts + part, 1)
            out[0, at, :] = out[0, at, :] + seen[:, part * lanes : (part + 1) * lanes]

    every_window(bound, blocks, cells, visit, visit_again)
    for copy in range(1, copies):
        out[copy] = out[0]


def scatter_kernel(dims, parts, key, frac, weight, perturb, scale, bound, source, side_a, side_b, gradient, valued):
    members, nvars, levels, rows, cells, blocks, copies = dims
    shift = cells.bit_length() - 1
    seen = parts[0]
    for copy in range(1, copies):
        seen = seen + parts[copy]
    valued[...] = seen * weight[...]
    gradient[...] = jnp.zeros(gradient.shape, jnp.float32)

    def add_block(block, start):
        keys = block_of(key, block)
        placed = weights_of(keys, block_of(frac, block), cells) * block_of(valued, block)
        high, low = halves(placed)
        both = lax.dot_general(
            chosen_rows(keys, start, shift),
            jnp.concatenate([high, low], axis=0),
            (((1,), (1,)), ((), ())),
            preferred_element_type=jnp.float32,
        )
        at = pl.ds(pl.multiple_of(start, ALIGN), BLOCK)
        gradient[at, :] = gradient[at, :] + (both[:, :cells] + both[:, cells:])

    every_window(bound, blocks, cells, add_block, add_block)

    plane = levels * rows
    for m in range(members):
        total = perturb[m, 0].astype(jnp.float32) * gradient[:plane, :]
        for v in range(1, nvars):
            total = total + perturb[m, v].astype(jnp.float32) * gradient[v * plane : (v + 1) * plane, :]
        source[m] = total
    for v in range(nvars):
        for x in range(rows):
            at = pl.ds(x, levels, stride=rows)
            source[members + v, at, :] = gradient[pl.ds(v * plane + x, levels, stride=rows), :] * scale[v]
    for begin, side in zip(begins(rows), (side_a, side_b)):
        for field in range(members + nvars):
            for j in range(SWEEPS):
                side[field, pl.ds(j * levels, levels), :] = source[field, pl.ds(begin + j, levels, stride=rows), :]


def local_kernel(dims, source, ens, stat, group, localize, static, hv):
    members, nvars, levels, rows, cells, blocks, copies = dims
    inside = neighbours()

    def of_field(member, at, field):
        control = ens if member else stat
        planes = {x: source[field, pl.ds(x, levels, stride=rows), :] for x in range(rows)}
        rate = rate_of(field if member else None, members, group, localize, static)
        planes = spread(planes, 0, rows - 1, rows, rate, inside)
        for x in range(rows):
            spot = pl.ds(x, levels, stride=rows)
            hv[field, spot, :] = control[at, spot, :] + planes[x]

    each_field(members, nvars, of_field)


def edge_kernel(dims, before, side_a, side_b, group, localize, static, hv_ens, hv_stat, after, sems):
    members, nvars, levels, rows, cells, blocks, copies = dims

    def copy_of(member, at, field):
        out = hv_ens if member else hv_stat
        return pltpu.make_async_copy(after.at[field], out.at[at], sems.at[field])

    def of_field(member, at, field):
        rate = rate_of(field if member else None, members, group, localize, static)
        lower, upper = sides_of(side_a, side_b, field, levels)
        lower = spread({j - SWEEPS: lower[j] for j in range(SWEEPS)}, 0, SWEEPS - 1, rows, rate, (1.0, 1.0))
        upper = spread({rows + j: upper[j] for j in range(SWEEPS)}, rows - SWEEPS, rows - 1, rows, rate, (1.0, 1.0))
        for x in range(rows):
            spot = pl.ds(x, levels, stride=rows)
            value = before[field, spot, :]
            if x < SWEEPS:
                value = value + lower[x]
            if x >= rows - SWEEPS:
                value = value + upper[x]
            after[field, spot, :] = value
        copy_of(member, at, field).start()

    each_field(members, nvars, of_field)
    each_field(members, nvars, lambda member, at, field: copy_of(member, at, field).wait())


def exchange(side_a, side_b):
    count = lax.axis_size("tile")
    pairs_a = [(i, i ^ 1) for i in range(count)]
    pairs_b = [(i, ((i + 1) ^ 1) - 1) for i in range(1, count - 1)]
    return lax.ppermute(side_a, "tile", pairs_a), lax.ppermute(side_b, "tile", pairs_b)


VMEM = pl.BlockSpec(memory_space=pltpu.VMEM)
SMEM = pl.BlockSpec(memory_space=pltpu.SMEM)
ANY = pl.BlockSpec(memory_space=pl.ANY)


def call(kernel, dims, outs, ins, scalars=(), scratch=(), out_spec=VMEM, cost=2_000_000):
    def body(*refs):
        kernel(dims, *refs)

    return pl.pallas_call(
        body,
        out_shape=tuple(jax.ShapeDtypeStruct(shape, jnp.float32) for shape in outs),
        in_specs=[VMEM] * len(ins) + [SMEM] * len(scalars),
        out_specs=tuple([out_spec] * len(outs)),
        scratch_shapes=list(scratch),
        compiler_params=pltpu.CompilerParams(vmem_limit_bytes=40 * 1024 * 1024),
        cost_estimate=pl.CostEstimate(flops=cost * 10, bytes_accessed=cost, transcendentals=0),
        name=kernel.__name__,
    )(*ins, *scalars)


def per_device(
    ens_control,
    static_control,
    member_perturb,
    member_group,
    localize_rate,
    static_rate,
    static_scale,
    obs_index,
    obs_frac,
    obs_layer,
    obs_kind,
    obs_precision,
):
    members, levels, rows, cells = ens_control.shape
    nvars = static_control.shape[1]
    fields = members + nvars
    copies = lax.axis_size("grp")
    blocks = obs_index.shape[0] // BLOCK
    dims = (members, nvars, levels, rows, cells, blocks, copies)
    plane = levels * rows
    strip = (fields, SWEEPS * levels, cells)

    ens = ens_control.reshape(members, plane, cells)
    stat = static_control.reshape(nvars, plane, cells)
    perturb = member_perturb.reshape(members, nvars, plane, cells)
    rates = [member_group, localize_rate, static_rate]

    side_a, side_b = exchange(*call(pack_kernel, dims, [strip, strip], [ens, stat]))

    scale = jnp.broadcast_to(static_scale[0][:, :, None], (nvars, levels, cells))
    kind_ids = jnp.arange(obs_precision.shape[0], dtype=jnp.int32)
    weight = jnp.sum(
        jnp.where(obs_kind[:, None] == kind_ids[None, :], obs_precision[None, :], 0.0), axis=1
    )
    key = obs_layer * (rows * cells) + obs_index
    key, frac, weight = lax.sort((key, obs_frac, weight), num_keys=1, is_stable=False)
    key, frac, weight = (x.reshape(-1, cells) for x in (key, frac, weight))

    table_rows = nvars * plane + BLOCK
    (seen,) = call(
        forward_kernel,
        dims,
        [(copies,) + key.shape],
        [ens, stat, perturb, scale, side_a, side_b, key, frac],
        [key] + rates,
        [pltpu.VMEM((fields, plane, cells), jnp.float32), pltpu.VMEM((table_rows, 2 * cells), jnp.bfloat16)],
    )
    parts = lax.all_to_all(seen, "grp", 0, 0)
    source, side_a, side_b = call(
        scatter_kernel,
        dims,
        [(fields, plane, cells), strip, strip],
        [parts, key, frac, weight, perturb, scale],
        [key],
        [pltpu.VMEM((table_rows, cells), jnp.float32), pltpu.VMEM(key.shape, jnp.float32)],
    )
    side_a, side_b = exchange(side_a, side_b)
    (before,) = call(local_kernel, dims, [(fields, plane, cells)], [source, ens, stat], rates)
    hv_ens, hv_stat = call(
        edge_kernel,
        dims,
        [(members, plane, cells), (nvars, plane, cells)],
        [before, side_a, side_b],
        rates,
        [pltpu.VMEM((fields, plane, cells), jnp.float32), pltpu.SemaphoreType.DMA((fields,))],
        ANY,
    )
    return hv_ens.reshape(ens_control.shape), hv_stat.reshape(static_control.shape)


def solution(mesh):
    placed = (
        P("grp", None, "tile", None),
        P("grp", None, None, "tile", None),
        P("grp", None, None, "tile", None),
        P("grp"),
        P(),
        P("grp"),
        P("grp", None, None),
        P("tile"),
        P("tile"),
        P("tile"),
        P("tile"),
        P(),
    )
    return jax.shard_map(
        per_device,
        mesh=mesh,
        in_specs=placed,
        out_specs=(P("grp", None, "tile", None), P("grp", None, None, "tile", None)),
        check_vma=False,
    )
```

```python
import math

import jax
import jax.numpy as jnp
import numpy as np
from jax import lax
from jax.experimental import pallas as pl
from jax.experimental.pallas import tpu as pltpu
from jax.sharding import PartitionSpec as P

SWEEPS = 4
BLOCK = 256
ALIGN = 16


def along_x(planes, wanted, rows, rate, inside):
    factors = [(1.0 - 4.0 * rate, rate)] + [((1.0 - 4.0 * rate) * side, rate * side) for side in inside]
    result = {}
    for x in wanted:
        keep, share = factors[1 if x < 0 else 2 if x >= rows else 0]
        total = None
        for near in (x - 1, x + 1):
            if near in planes:
                total = planes[near] if total is None else total + planes[near]
        if total is not None:
            total = share * total
        if x in planes:
            total = keep * planes[x] if total is None else keep * planes[x] + total
        if total is not None:
            result[x] = total
    return result


def powers_along_x(planes, first, last, rows, rate, inside):
    stages = [planes]
    for left in range(SWEEPS - 1, -1, -1):
        stages.append(along_x(stages[-1], range(first - left, last + left + 1), rows, rate, inside))
    return stages


def binomial(j, rate):
    factor = float(math.comb(SWEEPS, j))
    for number in range(j):
        factor = factor * rate
    return factor


def along_y(value):
    cells = value.shape[1]
    lane = lax.broadcasted_iota(jnp.int32, value.shape, 1)
    below = jnp.where(lane == 0, 0.0, pltpu.roll(value, 1, 1))
    return below + jnp.where(lane == cells - 1, 0.0, pltpu.roll(value, cells - 1, 1))


def spread_rolled(planes, first, last, rows, rate, inside):
    stages = powers_along_x(planes, first, last, rows, rate, inside)
    result = {}
    for x in range(first, last + 1):
        total = None
        for j in range(SWEEPS, -1, -1):
            if total is not None:
                total = along_y(total)
            term = stages[SWEEPS - j].get(x)
            if term is not None:
                term = term if j == 0 else binomial(j, rate) * term
                total = term if total is None else total + term
        result[x] = total
    return result


def halves(value):
    high = value.astype(jnp.bfloat16)
    low = (value - high.astype(jnp.float32)).astype(jnp.bfloat16)
    return high, low


def y_powers(cells):
    once = np.eye(cells, k=1) + np.eye(cells, k=-1)
    stack = []
    for j in range(1, SWEEPS + 1):
        stack += [np.linalg.matrix_power(once, j)] * 2
    return jnp.asarray(np.concatenate(stack), jnp.bfloat16)


GROUP = 4


def spread_product(planes, rows, rate, inside, powers):
    stages = powers_along_x(planes, 0, rows - 1, rows, rate, inside)
    levels = planes[0].shape[0]
    result = {}
    for first in range(0, rows, GROUP):
        columns = []
        for j in range(1, SWEEPS + 1):
            term = jnp.concatenate([stages[SWEEPS - j][x] for x in range(first, first + GROUP)], axis=0)
            columns += halves(binomial(j, rate) * term)
        product = jnp.dot(jnp.concatenate(columns, axis=1), powers[...], preferred_element_type=jnp.float32)
        for at in range(GROUP):
            result[first + at] = stages[SWEEPS][first + at] + product[at * levels : (at + 1) * levels]
    return result


def rate_of(field, members, group, localize, static):
    if field is None:
        return static[0]
    return localize[group[field]]


def neighbours():
    tile = lax.axis_index("tile")
    last = lax.axis_size("tile") - 1
    return jnp.where(tile > 0, 1.0, 0.0), jnp.where(tile < last, 1.0, 0.0)


def is_even():
    return lax.axis_index("tile") % 2 == 0


def begins(rows):
    even = is_even()
    return jnp.where(even, rows - SWEEPS, 0), jnp.where(even, 0, rows - SWEEPS)


def sides_of(side_a, side_b, field, levels):
    even = is_even()
    lower, upper = [], []
    for j in range(SWEEPS):
        a = side_a[field, pl.ds(j * levels, levels), :]
        b = side_b[field, pl.ds(j * levels, levels), :]
        lower.append(jnp.where(even, b, a))
        upper.append(jnp.where(even, a, b))
    return lower, upper


def block_of(ref, block):
    lanes = ref.shape[1]
    parts = BLOCK // lanes
    return jnp.concatenate([ref[pl.ds(block * parts + part, 1), :] for part in range(parts)], axis=1)


def weights_of(key, frac, cells):
    cell = key & (cells - 1)
    second = (cell + 1) & (cells - 1)
    spot = lax.broadcasted_iota(jnp.int32, (cells, key.shape[1]), 0)
    return jnp.where(spot == cell, 1.0 - frac, jnp.where(spot == second, frac, 0.0))


def chosen_rows(key, start, shift):
    row = (key >> shift) - start
    spot = lax.broadcasted_iota(jnp.int32, (BLOCK, key.shape[1]), 0)
    return jnp.where(spot == row, 1.0, 0.0).astype(jnp.bfloat16)


def window_of(bound, block, cells):
    parts = BLOCK // bound.shape[1]
    shift = cells.bit_length() - 1
    start = ((bound[block * parts, 0] >> shift) // ALIGN) * ALIGN
    last = bound[block * parts + parts - 1, bound.shape[1] - 1] >> shift
    return start, (last - start) // BLOCK + 1


def every_window(bound, blocks, cells, visit, visit_again):
    most = 1
    for block in range(blocks):
        start, count = window_of(bound, block, cells)
        most = jnp.maximum(most, count)
        visit(block, start)

    @pl.when(most > 1)
    def _():
        def of_block(block, carry):
            start, count = window_of(bound, block, cells)

            def of_window(window, inner):
                visit_again(block, start + window * BLOCK)
                return inner

            return lax.fori_loop(1, count, of_window, carry)

        lax.fori_loop(0, blocks, of_block, 0)


def each_field(members, nvars, visit):
    def of_member(m, carry):
        visit(True, m, m)
        return carry

    def of_group(v, carry):
        visit(False, v, members + v)
        return carry

    lax.fori_loop(0, members, of_member, 0)
    lax.fori_loop(0, nvars, of_group, 0)


def fetches(dims, ens, stat, into, sems):
    members, nvars = dims[:2]
    parts = [ens.at[m] for m in range(members)] + [stat.at[v] for v in range(nvars)]
    return [pltpu.make_async_copy(part, into.at[field], sems.at[field]) for field, part in enumerate(parts)]


def pack_kernel(dims, ens, stat, side_a, side_b, held, sems):
    members, nvars, levels, rows, cells, blocks, copies = dims
    loads = fetches(dims, ens, stat, held, sems)
    for load in loads:
        load.start()
    for field, load in enumerate(loads):
        load.wait()
        for begin, side in zip(begins(rows), (side_a, side_b)):
            for j in range(SWEEPS):
                side[field, pl.ds(j * levels, levels), :] = held[field, pl.ds(begin + j, levels, stride=rows), :]


def own_kernel(dims, powers, ens, stat, group, localize, static, out, held, sems):
    members, nvars, levels, rows, cells, blocks, copies = dims
    inside = neighbours()
    loads = fetches(dims, ens, stat, held, sems)
    for load in loads:
        load.start()
    for load in loads:
        load.wait()

    def of_field(member, at, field):
        planes = {x: held[field, pl.ds(x, levels, stride=rows), :] for x in range(rows)}
        rate = rate_of(field if member else None, members, group, localize, static)
        planes = spread_product(planes, rows, rate, inside, powers)
        for x in range(rows):
            out[field, pl.ds(x * levels, levels), :] = planes[x]

    each_field(members, nvars, of_field)


def with_sides(dims, own, side_a, side_b, field, rate):
    members, nvars, levels, rows, cells, blocks, copies = dims
    lower, upper = sides_of(side_a, side_b, field, levels)
    lower = spread_rolled({j - SWEEPS: lower[j] for j in range(SWEEPS)}, 0, SWEEPS - 1, rows, rate, (1.0, 1.0))
    upper = spread_rolled({rows + j: upper[j] for j in range(SWEEPS)}, rows - SWEEPS, rows - 1, rows, rate, (1.0, 1.0))
    planes = {}
    for x in range(rows):
        planes[x] = own[field, pl.ds(x * levels, levels), :]
        for extra in (lower, upper):
            if x in extra:
                planes[x] = planes[x] + extra[x]
    return planes


def forward_kernel(dims, own, scale, side_a, side_b, key, frac, perturb_far, bound, group, localize, static, out, smooth, table, perturb, sem):
    members, nvars, levels, rows, cells, blocks, copies = dims
    shift = cells.bit_length() - 1
    load = pltpu.make_async_copy(perturb_far, perturb, sem)
    load.start()

    def of_field(member, at, field):
        rate = rate_of(field if member else None, members, group, localize, static)
        planes = with_sides(dims, own, side_a, side_b, field, rate)
        for x in range(rows):
            value = planes[x] if member else planes[x] * scale[at]
            smooth[field, pl.ds(x, levels, stride=rows), :] = value

    each_field(members, nvars, of_field)
    load.wait()
    plane = levels * rows
    for v in range(nvars):
        total = smooth[members + v]
        for m in range(members):
            total = total + perturb[m, v].astype(jnp.float32) * smooth[m]
        high, low = halves(total)
        table[v * plane : (v + 1) * plane, :cells] = high
        table[v * plane : (v + 1) * plane, cells:] = low
    table[nvars * plane :, :] = jnp.zeros((BLOCK, 2 * cells), jnp.bfloat16)
    lanes = key.shape[1]
    parts = BLOCK // lanes

    def seen_in(block, start):
        keys = block_of(key, block)
        picked = lax.dot_general(
            table[pl.ds(pl.multiple_of(start, ALIGN), BLOCK), :],
            chosen_rows(keys, start, shift),
            (((0,), (0,)), ((), ())),
            preferred_element_type=jnp.float32,
        )
        picked = picked[:cells] + picked[cells:]
        return jnp.sum(picked * weights_of(keys, block_of(frac, block), cells), axis=0, keepdims=True)

    def visit(block, start):
        seen = seen_in(block, start)
        for part in range(parts):
            out[0, pl.ds(block * parts + part, 1), :] = seen[:, part * lanes : (part + 1) * lanes]

    def visit_again(block, start):
        seen = seen_in(block, start)
        for part in range(parts):
            at = pl.ds(block * parts + part, 1)
            out[0, at, :] = out[0, at, :] + seen[:, part * lanes : (part + 1) * lanes]

    every_window(bound, blocks, cells, visit, visit_again)
    for copy in range(1, copies):
        out[copy] = out[0]


def scatter_kernel(dims, parts, key, frac, weight, perturb, scale, bound, source, side_a, side_b, gradient, valued):
    members, nvars, levels, rows, cells, blocks, copies = dims
    shift = cells.bit_length() - 1
    seen = parts[0]
    for copy in range(1, copies):
        seen = seen + parts[copy]
    valued[...] = seen * weight[...]
    gradient[...] = jnp.zeros(gradient.shape, jnp.float32)

    def add_block(block, start):
        keys = block_of(key, block)
        placed = weights_of(keys, block_of(frac, block), cells) * block_of(valued, block)
        high, low = halves(placed)
        both = lax.dot_general(
            chosen_rows(keys, start, shift),
            jnp.concatenate([high, low], axis=0),
            (((1,), (1,)), ((), ())),
            preferred_element_type=jnp.float32,
        )
        at = pl.ds(pl.multiple_of(start, ALIGN), BLOCK)
        gradient[at, :] = gradient[at, :] + (both[:, :cells] + both[:, cells:])

    every_window(bound, blocks, cells, add_block, add_block)

    plane = levels * rows
    for m in range(members):
        total = perturb[m, 0].astype(jnp.float32) * gradient[:plane, :]
        for v in range(1, nvars):
            total = total + perturb[m, v].astype(jnp.float32) * gradient[v * plane : (v + 1) * plane, :]
        source[m] = total
    for v in range(nvars):
        for x in range(rows):
            at = pl.ds(x, levels, stride=rows)
            source[members + v, at, :] = gradient[pl.ds(v * plane + x, levels, stride=rows), :] * scale[v]
    for begin, side in zip(begins(rows), (side_a, side_b)):
        for field in range(members + nvars):
            for j in range(SWEEPS):
                side[field, pl.ds(j * levels, levels), :] = source[field, pl.ds(begin + j, levels, stride=rows), :]


def local_kernel(dims, powers, source, ens, stat, group, localize, static, out, held, sems):
    members, nvars, levels, rows, cells, blocks, copies = dims
    inside = neighbours()
    loads = fetches(dims, ens, stat, held, sems)
    for load in loads:
        load.start()
    for load in loads:
        load.wait()

    def of_field(member, at, field):
        planes = {x: source[field, pl.ds(x, levels, stride=rows), :] for x in range(rows)}
        rate = rate_of(field if member else None, members, group, localize, static)
        planes = spread_product(planes, rows, rate, inside, powers)
        for x in range(rows):
            out[field, pl.ds(x * levels, levels), :] = held[field, pl.ds(x, levels, stride=rows), :] + planes[x]

    each_field(members, nvars, of_field)


def edge_kernel(dims, own, side_a, side_b, group, localize, static, hv_ens, hv_stat, after, sems):
    members, nvars, levels, rows, cells, blocks, copies = dims

    def copy_of(member, at, field):
        out = hv_ens if member else hv_stat
        return pltpu.make_async_copy(after.at[field], out.at[at], sems.at[field])

    def of_field(member, at, field):
        rate = rate_of(field if member else None, members, group, localize, static)
        planes = with_sides(dims, own, side_a, side_b, field, rate)
        for x in range(rows):
            after[field, pl.ds(x, levels, stride=rows), :] = planes[x]
        copy_of(member, at, field).start()

    each_field(members, nvars, of_field)
    each_field(members, nvars, lambda member, at, field: copy_of(member, at, field).wait())


def exchange(side_a, side_b):
    count = lax.axis_size("tile")
    pairs_a = [(i, i ^ 1) for i in range(count)]
    pairs_b = [(i, ((i + 1) ^ 1) - 1) for i in range(1, count - 1)]
    return lax.ppermute(side_a, "tile", pairs_a), lax.ppermute(side_b, "tile", pairs_b)


VMEM = pl.BlockSpec(memory_space=pltpu.VMEM)
SMEM = pl.BlockSpec(memory_space=pltpu.SMEM)
HBM = pl.BlockSpec(memory_space=pltpu.HBM)


def call(kernel, dims, outs, ins, far=(), scalars=(), scratch=(), out_spec=VMEM, cost=2_000_000):
    def body(*refs):
        kernel(dims, *refs)

    far = [pltpu.with_memory_space_constraint(x, pltpu.HBM) for x in far]
    return pl.pallas_call(
        body,
        out_shape=tuple(jax.ShapeDtypeStruct(shape, jnp.float32) for shape in outs),
        in_specs=[VMEM] * len(ins) + [HBM] * len(far) + [SMEM] * len(scalars),
        out_specs=tuple([out_spec] * len(outs)),
        scratch_shapes=list(scratch),
        compiler_params=pltpu.CompilerParams(vmem_limit_bytes=40 * 1024 * 1024),
        cost_estimate=pl.CostEstimate(flops=cost * 10, bytes_accessed=cost, transcendentals=0),
        name=kernel.__name__,
    )(*ins, *far, *scalars)


def per_device(
    ens_control,
    static_control,
    member_perturb,
    member_group,
    localize_rate,
    static_rate,
    static_scale,
    obs_index,
    obs_frac,
    obs_layer,
    obs_kind,
    obs_precision,
):
    members, levels, rows, cells = ens_control.shape
    nvars = static_control.shape[1]
    fields = members + nvars
    copies = lax.axis_size("grp")
    blocks = obs_index.shape[0] // BLOCK
    dims = (members, nvars, levels, rows, cells, blocks, copies)
    plane = levels * rows
    strip = (fields, SWEEPS * levels, cells)

    ens = ens_control.reshape(members, plane, cells)
    stat = static_control.reshape(nvars, plane, cells)
    perturb = member_perturb.reshape(members, nvars, plane, cells)
    rates = [member_group, localize_rate, static_rate]

    fetched = [pltpu.VMEM((fields, plane, cells), jnp.float32), pltpu.SemaphoreType.DMA((fields,))]
    powers = y_powers(cells)

    side_a, side_b = exchange(*call(pack_kernel, dims, [strip, strip], [], [ens, stat], [], fetched))

    scale = jnp.broadcast_to(static_scale[0][:, :, None], (nvars, levels, cells))
    kind_ids = jnp.arange(obs_precision.shape[0], dtype=jnp.int32)
    weight = jnp.sum(
        jnp.where(obs_kind[:, None] == kind_ids[None, :], obs_precision[None, :], 0.0), axis=1
    )
    key = obs_layer * (rows * cells) + obs_index
    key, frac, weight = lax.sort((key, obs_frac, weight), num_keys=1, is_stable=False)
    key, frac, weight = (x.reshape(-1, cells) for x in (key, frac, weight))

    table_rows = nvars * plane + BLOCK
    (own,) = call(own_kernel, dims, [(fields, plane, cells)], [powers], [ens, stat], rates, fetched)
    (seen,) = call(
        forward_kernel,
        dims,
        [(copies,) + key.shape],
        [own, scale, side_a, side_b, key, frac],
        [perturb],
        [key] + rates,
        [
            pltpu.VMEM((fields, plane, cells), jnp.float32),
            pltpu.VMEM((table_rows, 2 * cells), jnp.bfloat16),
            pltpu.VMEM(perturb.shape, perturb.dtype),
            pltpu.SemaphoreType.DMA(()),
        ],
    )
    parts = lax.all_to_all(seen, "grp", 0, 0)
    source, side_a, side_b = call(
        scatter_kernel,
        dims,
        [(fields, plane, cells), strip, strip],
        [parts, key, frac, weight, perturb, scale],
        [],
        [key],
        [pltpu.VMEM((table_rows, cells), jnp.float32), pltpu.VMEM(key.shape, jnp.float32)],
    )
    side_a, side_b = exchange(side_a, side_b)
    (own,) = call(local_kernel, dims, [(fields, plane, cells)], [powers, source], [ens, stat], rates, fetched)
    hv_ens, hv_stat = call(
        edge_kernel,
        dims,
        [(members, plane, cells), (nvars, plane, cells)],
        [own, side_a, side_b],
        [],
        rates,
        [pltpu.VMEM((fields, plane, cells), jnp.float32), pltpu.SemaphoreType.DMA((fields,))],
        HBM,
    )
    return hv_ens.reshape(ens_control.shape), hv_stat.reshape(static_control.shape)


def solution(mesh):
    placed = (
        P("grp", None, "tile", None),
        P("grp", None, None, "tile", None),
        P("grp", None, None, "tile", None),
        P("grp"),
        P(),
        P("grp"),
        P("grp", None, None),
        P("tile"),
        P("tile"),
        P("tile"),
        P("tile"),
        P(),
    )
    return jax.shard_map(
        per_device,
        mesh=mesh,
        in_specs=placed,
        out_specs=(P("grp", None, "tile", None), P("grp", None, None, "tile", None)),
        check_vma=False,
    )
```

```python
import math

import jax
import jax.numpy as jnp
import numpy as np
from jax import lax
from jax.experimental import pallas as pl
from jax.experimental.pallas import tpu as pltpu
from jax.sharding import PartitionSpec as P

SWEEPS = 4
BLOCK = 256
ALIGN = 16


def along_x(planes, wanted, rows, rate, inside):
    factors = [(1.0 - 4.0 * rate, rate)] + [((1.0 - 4.0 * rate) * side, rate * side) for side in inside]
    result = {}
    for x in wanted:
        keep, share = factors[1 if x < 0 else 2 if x >= rows else 0]
        total = None
        for near in (x - 1, x + 1):
            if near in planes:
                total = planes[near] if total is None else total + planes[near]
        if total is not None:
            total = share * total
        if x in planes:
            total = keep * planes[x] if total is None else keep * planes[x] + total
        if total is not None:
            result[x] = total
    return result


def powers_along_x(planes, first, last, rows, rate, inside):
    stages = [planes]
    for left in range(SWEEPS - 1, -1, -1):
        stages.append(along_x(stages[-1], range(first - left, last + left + 1), rows, rate, inside))
    return stages


def binomial(j, rate):
    factor = float(math.comb(SWEEPS, j))
    for number in range(j):
        factor = factor * rate
    return factor


def along_y(value):
    cells = value.shape[1]
    lane = lax.broadcasted_iota(jnp.int32, value.shape, 1)
    below = jnp.where(lane == 0, 0.0, pltpu.roll(value, 1, 1))
    return below + jnp.where(lane == cells - 1, 0.0, pltpu.roll(value, cells - 1, 1))


def spread_rolled(planes, first, last, rows, rate, inside):
    stages = powers_along_x(planes, first, last, rows, rate, inside)
    result = {}
    for x in range(first, last + 1):
        total = None
        for j in range(SWEEPS, -1, -1):
            if total is not None:
                total = along_y(total)
            term = stages[SWEEPS - j].get(x)
            if term is not None:
                term = term if j == 0 else binomial(j, rate) * term
                total = term if total is None else total + term
        result[x] = total
    return result


def halves(value):
    high = value.astype(jnp.bfloat16)
    low = (value - high.astype(jnp.float32)).astype(jnp.bfloat16)
    return high, low


def y_powers(cells):
    once = np.eye(cells, k=1) + np.eye(cells, k=-1)
    row = np.concatenate([np.linalg.matrix_power(once, j) for j in range(1, SWEEPS + 1)], axis=1)
    return jnp.asarray(np.concatenate([row, row], axis=0), jnp.bfloat16)


GROUP = 8


def spread_product(planes, rows, rate, inside, powers):
    levels, cells = planes[0].shape
    terms = [{} for j in range(SWEEPS)]
    for first in range(0, rows, GROUP):
        both = jnp.concatenate(halves(jnp.concatenate([planes[x] for x in range(first, first + GROUP)], axis=0)), axis=1)
        product = jnp.dot(both, powers[...], preferred_element_type=jnp.float32)
        for at in range(GROUP):
            for j in range(SWEEPS):
                terms[j][first + at] = product[at * levels : (at + 1) * levels, j * cells : (j + 1) * cells]
    result = planes
    for j in range(1, SWEEPS + 1):
        left = SWEEPS - j
        result = along_x(result, range(-left, rows + left), rows, rate, inside)
        factor = binomial(j, rate)
        for x in range(rows):
            result[x] = result[x] + factor * terms[j - 1][x]
    return result


def rate_of(field, members, group, localize, static):
    member = jnp.minimum(field, members - 1)
    return jnp.where(field < members, localize[group[member]], static[0])


def neighbours():
    tile = lax.axis_index("tile")
    last = lax.axis_size("tile") - 1
    return jnp.where(tile > 0, 1.0, 0.0), jnp.where(tile < last, 1.0, 0.0)


def is_even():
    return lax.axis_index("tile") % 2 == 0


def begins(rows):
    even = is_even()
    return jnp.where(even, rows - SWEEPS, 0), jnp.where(even, 0, rows - SWEEPS)


def sides_of(side_a, side_b, field, levels):
    even = is_even()
    lower, upper = [], []
    for j in range(SWEEPS):
        a = side_a[field, pl.ds(j * levels, levels), :]
        b = side_b[field, pl.ds(j * levels, levels), :]
        lower.append(jnp.where(even, b, a))
        upper.append(jnp.where(even, a, b))
    return lower, upper


def block_of(ref, block):
    lanes = ref.shape[1]
    parts = BLOCK // lanes
    return jnp.concatenate([ref[pl.ds(block * parts + part, 1), :] for part in range(parts)], axis=1)


def weights_of(key, frac, cells):
    cell = key & (cells - 1)
    second = (cell + 1) & (cells - 1)
    spot = lax.broadcasted_iota(jnp.int32, (cells, key.shape[1]), 0)
    return jnp.where(spot == cell, 1.0 - frac, jnp.where(spot == second, frac, 0.0))


def chosen_rows(key, start, shift):
    row = (key >> shift) - start
    spot = lax.broadcasted_iota(jnp.int32, (BLOCK, key.shape[1]), 0)
    return jnp.where(spot == row, 1.0, 0.0).astype(jnp.bfloat16)


def window_of(bound, block, cells):
    parts = BLOCK // bound.shape[1]
    shift = cells.bit_length() - 1
    start = ((bound[block * parts, 0] >> shift) // ALIGN) * ALIGN
    last = bound[block * parts + parts - 1, bound.shape[1] - 1] >> shift
    return start, (last - start) // BLOCK + 1


def every_window(bound, blocks, cells, visit, visit_again):
    most = 1
    for block in range(blocks):
        start, count = window_of(bound, block, cells)
        most = jnp.maximum(most, count)
        visit(block, start)

    @pl.when(most > 1)
    def _():
        def of_block(block, carry):
            start, count = window_of(bound, block, cells)

            def of_window(window, inner):
                visit_again(block, start + window * BLOCK)
                return inner

            return lax.fori_loop(1, count, of_window, carry)

        lax.fori_loop(0, blocks, of_block, 0)


def each_field(fields, visit):
    def step(field, carry):
        visit(field)
        return carry

    lax.fori_loop(0, fields, step, 0)


def pack_kernel(dims, ens, stat, side_a, side_b, held, sems):
    members, nvars, levels, rows, cells, blocks, copies = dims
    parts = [ens.at[m] for m in range(members)] + [stat.at[v] for v in range(nvars)]
    loads = [pltpu.make_async_copy(part, held.at[field], sems.at[field]) for field, part in enumerate(parts)]
    for load in loads:
        load.start()
    for field, load in enumerate(loads):
        load.wait()
        for begin, side in zip(begins(rows), (side_a, side_b)):
            for j in range(SWEEPS):
                side[field, pl.ds(j * levels, levels), :] = held[field, pl.ds(begin + j, levels, stride=rows), :]


def own_kernel(dims, powers, held, group, localize, static, out):
    members, nvars, levels, rows, cells, blocks, copies = dims
    inside = neighbours()

    def of_field(field):
        planes = {x: held[field, pl.ds(x, levels, stride=rows), :] for x in range(rows)}
        rate = rate_of(field, members, group, localize, static)
        planes = spread_product(planes, rows, rate, inside, powers)
        for x in range(rows):
            out[field, pl.ds(x * levels, levels), :] = planes[x]

    each_field(members + nvars, of_field)


def with_sides(dims, own, side_a, side_b, field, rate):
    members, nvars, levels, rows, cells, blocks, copies = dims
    lower, upper = sides_of(side_a, side_b, field, levels)
    lower = spread_rolled({j - SWEEPS: lower[j] for j in range(SWEEPS)}, 0, SWEEPS - 1, rows, rate, (1.0, 1.0))
    upper = spread_rolled({rows + j: upper[j] for j in range(SWEEPS)}, rows - SWEEPS, rows - 1, rows, rate, (1.0, 1.0))
    planes = {}
    for x in range(rows):
        planes[x] = own[field, pl.ds(x * levels, levels), :]
        for extra in (lower, upper):
            if x in extra:
                planes[x] = planes[x] + extra[x]
    return planes


def forward_kernel(dims, own, scale, side_a, side_b, key, frac, perturb_far, bound, group, localize, static, out, smooth, table, perturb, sem):
    members, nvars, levels, rows, cells, blocks, copies = dims
    shift = cells.bit_length() - 1
    load = pltpu.make_async_copy(perturb_far, perturb, sem)
    load.start()

    def of_field(field):
        rate = rate_of(field, members, group, localize, static)
        planes = with_sides(dims, own, side_a, side_b, field, rate)
        for x in range(rows):
            smooth[field, pl.ds(x, levels, stride=rows), :] = planes[x] * scale[field]

    each_field(members + nvars, of_field)
    load.wait()
    plane = levels * rows
    for v in range(nvars):
        total = smooth[members + v]
        for m in range(members):
            total = total + perturb[m, v].astype(jnp.float32) * smooth[m]
        high, low = halves(total)
        table[v * plane : (v + 1) * plane, :cells] = high
        table[v * plane : (v + 1) * plane, cells:] = low
    table[nvars * plane :, :] = jnp.zeros((BLOCK, 2 * cells), jnp.bfloat16)
    lanes = key.shape[1]
    parts = BLOCK // lanes

    def seen_in(block, start):
        keys = block_of(key, block)
        picked = lax.dot_general(
            table[pl.ds(pl.multiple_of(start, ALIGN), BLOCK), :],
            chosen_rows(keys, start, shift),
            (((0,), (0,)), ((), ())),
            preferred_element_type=jnp.float32,
        )
        picked = picked[:cells] + picked[cells:]
        return jnp.sum(picked * weights_of(keys, block_of(frac, block), cells), axis=0, keepdims=True)

    def visit(block, start):
        seen = seen_in(block, start)
        for part in range(parts):
            out[0, pl.ds(block * parts + part, 1), :] = seen[:, part * lanes : (part + 1) * lanes]

    def visit_again(block, start):
        seen = seen_in(block, start)
        for part in range(parts):
            at = pl.ds(block * parts + part, 1)
            out[0, at, :] = out[0, at, :] + seen[:, part * lanes : (part + 1) * lanes]

    every_window(bound, blocks, cells, visit, visit_again)
    for copy in range(1, copies):
        out[copy] = out[0]


def scatter_kernel(dims, parts, key, frac, weight, perturb, scale, bound, source, side_a, side_b, gradient, valued):
    members, nvars, levels, rows, cells, blocks, copies = dims
    shift = cells.bit_length() - 1
    seen = parts[0]
    for copy in range(1, copies):
        seen = seen + parts[copy]
    valued[...] = seen * weight[...]
    gradient[...] = jnp.zeros(gradient.shape, jnp.float32)

    def add_block(block, start):
        keys = block_of(key, block)
        placed = weights_of(keys, block_of(frac, block), cells) * block_of(valued, block)
        high, low = halves(placed)
        both = lax.dot_general(
            chosen_rows(keys, start, shift),
            jnp.concatenate([high, low], axis=0),
            (((1,), (1,)), ((), ())),
            preferred_element_type=jnp.float32,
        )
        at = pl.ds(pl.multiple_of(start, ALIGN), BLOCK)
        gradient[at, :] = gradient[at, :] + (both[:, :cells] + both[:, cells:])

    every_window(bound, blocks, cells, add_block, add_block)

    plane = levels * rows
    for m in range(members):
        total = perturb[m, 0].astype(jnp.float32) * gradient[:plane, :]
        for v in range(1, nvars):
            total = total + perturb[m, v].astype(jnp.float32) * gradient[v * plane : (v + 1) * plane, :]
        source[m] = total
    for begin, side in zip(begins(rows), (side_a, side_b)):
        for field in range(members + nvars):
            for j in range(SWEEPS):
                if field < members:
                    strip = source[field, pl.ds(begin + j, levels, stride=rows), :]
                else:
                    at = (field - members) * plane + begin + j
                    strip = gradient[pl.ds(at, levels, stride=rows), :] * scale[field]
                side[field, pl.ds(j * levels, levels), :] = strip


def local_kernel(dims, powers, source, gradient, scale, held, group, localize, static, out):
    members, nvars, levels, rows, cells, blocks, copies = dims
    inside = neighbours()
    plane = levels * rows

    def of_field(field, planes):
        rate = rate_of(field, members, group, localize, static)
        planes = spread_product(planes, rows, rate, inside, powers)
        for x in range(rows):
            out[field, pl.ds(x * levels, levels), :] = held[field, pl.ds(x, levels, stride=rows), :] + planes[x]

    def of_member(m):
        of_field(m, {x: source[m, pl.ds(x, levels, stride=rows), :] for x in range(rows)})

    def of_group(v):
        field = members + v
        planes = {x: gradient[pl.ds(v * plane + x, levels, stride=rows), :] * scale[field] for x in range(rows)}
        of_field(field, planes)

    each_field(members, of_member)
    each_field(nvars, of_group)


def edge_kernel(dims, own, side_a, side_b, group, localize, static, hv_ens, hv_stat, after, sems):
    members, nvars, levels, rows, cells, blocks, copies = dims

    writes = []
    for field in range(members + nvars):
        rate = rate_of(field, members, group, localize, static)
        planes = with_sides(dims, own, side_a, side_b, field, rate)
        for x in range(rows):
            after[field, pl.ds(x, levels, stride=rows), :] = planes[x]
        out = hv_ens.at[field] if field < members else hv_stat.at[field - members]
        write = pltpu.make_async_copy(after.at[field], out, sems.at[field])
        write.start()
        writes.append(write)
    for write in writes:
        write.wait()


def exchange(side_a, side_b):
    count = lax.axis_size("tile")
    pairs_a = [(i, i ^ 1) for i in range(count)]
    pairs_b = [(i, ((i + 1) ^ 1) - 1) for i in range(1, count - 1)]
    return lax.ppermute(side_a, "tile", pairs_a), lax.ppermute(side_b, "tile", pairs_b)


VMEM = pl.BlockSpec(memory_space=pltpu.VMEM)
SMEM = pl.BlockSpec(memory_space=pltpu.SMEM)
HBM = pl.BlockSpec(memory_space=pltpu.HBM)


def call(kernel, dims, outs, ins, far=(), scalars=(), scratch=(), out_spec=VMEM, cost=2_000_000):
    def body(*refs):
        kernel(dims, *refs)

    far = [pltpu.with_memory_space_constraint(x, pltpu.HBM) for x in far]
    return pl.pallas_call(
        body,
        out_shape=tuple(jax.ShapeDtypeStruct(shape, jnp.float32) for shape in outs),
        in_specs=[VMEM] * len(ins) + [HBM] * len(far) + [SMEM] * len(scalars),
        out_specs=tuple([out_spec] * len(outs)),
        scratch_shapes=list(scratch),
        compiler_params=pltpu.CompilerParams(vmem_limit_bytes=40 * 1024 * 1024),
        cost_estimate=pl.CostEstimate(flops=cost * 10, bytes_accessed=cost, transcendentals=0),
        name=kernel.__name__,
    )(*ins, *far, *scalars)


def per_device(
    ens_control,
    static_control,
    member_perturb,
    member_group,
    localize_rate,
    static_rate,
    static_scale,
    obs_index,
    obs_frac,
    obs_layer,
    obs_kind,
    obs_precision,
):
    members, levels, rows, cells = ens_control.shape
    nvars = static_control.shape[1]
    fields = members + nvars
    copies = lax.axis_size("grp")
    blocks = obs_index.shape[0] // BLOCK
    dims = (members, nvars, levels, rows, cells, blocks, copies)
    plane = levels * rows
    strip = (fields, SWEEPS * levels, cells)

    ens = ens_control.reshape(members, plane, cells)
    stat = static_control.reshape(nvars, plane, cells)
    perturb = member_perturb.reshape(members, nvars, plane, cells)
    rates = [member_group, localize_rate, static_rate]

    whole = (fields, plane, cells)
    powers = y_powers(cells)
    copying = [pltpu.SemaphoreType.DMA((fields,))]
    side_a, side_b, held = call(pack_kernel, dims, [strip, strip, whole], [], [ens, stat], [], copying)
    side_a, side_b = exchange(side_a, side_b)

    scale = jnp.concatenate([jnp.ones((members, levels), jnp.float32), static_scale[0]])
    scale = jnp.broadcast_to(scale[:, :, None], (fields, levels, cells))
    kind_ids = jnp.arange(obs_precision.shape[0], dtype=jnp.int32)
    weight = jnp.sum(
        jnp.where(obs_kind[:, None] == kind_ids[None, :], obs_precision[None, :], 0.0), axis=1
    )
    key = obs_layer * (rows * cells) + obs_index
    key, frac, weight = lax.sort((key, obs_frac, weight), num_keys=1, is_stable=False)
    key, frac, weight = (x.reshape(-1, cells) for x in (key, frac, weight))

    table_rows = nvars * plane + BLOCK
    (own,) = call(own_kernel, dims, [whole], [powers, held], [], rates)
    (seen,) = call(
        forward_kernel,
        dims,
        [(copies,) + key.shape],
        [own, scale, side_a, side_b, key, frac],
        [perturb],
        [key] + rates,
        [
            pltpu.VMEM(whole, jnp.float32),
            pltpu.VMEM((table_rows, 2 * cells), jnp.bfloat16),
            pltpu.VMEM(perturb.shape, perturb.dtype),
            pltpu.SemaphoreType.DMA(()),
        ],
    )
    parts = lax.all_to_all(seen, "grp", 0, 0)
    source, side_a, side_b, gradient = call(
        scatter_kernel,
        dims,
        [(members, plane, cells), strip, strip, (table_rows, cells)],
        [parts, key, frac, weight, perturb, scale],
        [],
        [key],
        [pltpu.VMEM(key.shape, jnp.float32)],
    )
    side_a, side_b = exchange(side_a, side_b)
    (own,) = call(local_kernel, dims, [whole], [powers, source, gradient, scale, held], [], rates)
    hv_ens, hv_stat = call(
        edge_kernel,
        dims,
        [(members, plane, cells), (nvars, plane, cells)],
        [own, side_a, side_b],
        [],
        rates,
        [pltpu.VMEM(whole, jnp.float32), pltpu.SemaphoreType.DMA((fields,))],
        HBM,
    )
    return hv_ens.reshape(ens_control.shape), hv_stat.reshape(static_control.shape)


def solution(mesh):
    placed = (
        P("grp", None, "tile", None),
        P("grp", None, None, "tile", None),
        P("grp", None, None, "tile", None),
        P("grp"),
        P(),
        P("grp"),
        P("grp", None, None),
        P("tile"),
        P("tile"),
        P("tile"),
        P("tile"),
        P(),
    )
    return jax.shard_map(
        per_device,
        mesh=mesh,
        in_specs=placed,
        out_specs=(P("grp", None, "tile", None), P("grp", None, None, "tile", None)),
        check_vma=False,
    )
```

```python
import math

import jax
import jax.numpy as jnp
import numpy as np
from jax import lax
from jax.experimental import pallas as pl
from jax.experimental.pallas import tpu as pltpu
from jax.sharding import PartitionSpec as P

SWEEPS = 4
BLOCK = 256
ALIGN = 16


def along_x(planes, wanted, rows, rate, inside):
    factors = [(1.0 - 4.0 * rate, rate)] + [((1.0 - 4.0 * rate) * side, rate * side) for side in inside]
    result = {}
    for x in wanted:
        keep, share = factors[1 if x < 0 else 2 if x >= rows else 0]
        total = None
        for near in (x - 1, x + 1):
            if near in planes:
                total = planes[near] if total is None else total + planes[near]
        if total is not None:
            total = share * total
        if x in planes:
            total = keep * planes[x] if total is None else keep * planes[x] + total
        if total is not None:
            result[x] = total
    return result


def powers_along_x(planes, first, last, rows, rate, inside):
    stages = [planes]
    for left in range(SWEEPS - 1, -1, -1):
        stages.append(along_x(stages[-1], range(first - left, last + left + 1), rows, rate, inside))
    return stages


def binomial(j, rate):
    factor = float(math.comb(SWEEPS, j))
    for number in range(j):
        factor = factor * rate
    return factor


def along_y(value):
    cells = value.shape[1]
    lane = lax.broadcasted_iota(jnp.int32, value.shape, 1)
    below = jnp.where(lane == 0, 0.0, pltpu.roll(value, 1, 1))
    return below + jnp.where(lane == cells - 1, 0.0, pltpu.roll(value, cells - 1, 1))


def spread_rolled(planes, first, last, rows, rate, inside):
    stages = powers_along_x(planes, first, last, rows, rate, inside)
    result = {}
    for x in range(first, last + 1):
        total = None
        for j in range(SWEEPS, -1, -1):
            if total is not None:
                total = along_y(total)
            term = stages[SWEEPS - j].get(x)
            if term is not None:
                term = term if j == 0 else binomial(j, rate) * term
                total = term if total is None else total + term
        result[x] = total
    return result


def halves(value):
    high = value.astype(jnp.bfloat16)
    low = (value - high.astype(jnp.float32)).astype(jnp.bfloat16)
    return high, low


def y_powers(cells):
    once = np.eye(cells, k=1) + np.eye(cells, k=-1)
    row = np.concatenate([np.linalg.matrix_power(once, j) for j in range(1, SWEEPS + 1)], axis=1)
    return jnp.asarray(np.concatenate([row, row], axis=0), jnp.bfloat16)


GROUP = 8


def spread_product(planes, rows, rate, inside, powers):
    levels, cells = planes[0].shape
    terms = [{} for j in range(SWEEPS)]
    for first in range(0, rows, GROUP):
        both = jnp.concatenate(halves(jnp.concatenate([planes[x] for x in range(first, first + GROUP)], axis=0)), axis=1)
        product = jnp.dot(both, powers[...], preferred_element_type=jnp.float32)
        for at in range(GROUP):
            for j in range(SWEEPS):
                terms[j][first + at] = product[at * levels : (at + 1) * levels, j * cells : (j + 1) * cells]
    result = planes
    for j in range(1, SWEEPS + 1):
        left = SWEEPS - j
        result = along_x(result, range(-left, rows + left), rows, rate, inside)
        factor = binomial(j, rate)
        for x in range(rows):
            result[x] = result[x] + factor * terms[j - 1][x]
    return result


def rate_of(field, members, group, localize, static):
    member = jnp.minimum(field, members - 1)
    return jnp.where(field < members, localize[group[member]], static[0])


def neighbours():
    tile = lax.axis_index("tile")
    last = lax.axis_size("tile") - 1
    return jnp.where(tile > 0, 1.0, 0.0), jnp.where(tile < last, 1.0, 0.0)


def is_even():
    return lax.axis_index("tile") % 2 == 0


def begins(rows):
    even = is_even()
    return jnp.where(even, rows - SWEEPS, 0), jnp.where(even, 0, rows - SWEEPS)


def sides_of(side_a, side_b, field, levels):
    even = is_even()
    lower, upper = [], []
    for j in range(SWEEPS):
        a = side_a[field, pl.ds(j * levels, levels), :]
        b = side_b[field, pl.ds(j * levels, levels), :]
        lower.append(jnp.where(even, b, a))
        upper.append(jnp.where(even, a, b))
    return lower, upper


def block_of(ref, block):
    lanes = ref.shape[1]
    parts = BLOCK // lanes
    return jnp.concatenate([ref[pl.ds(block * parts + part, 1), :] for part in range(parts)], axis=1)


def weights_of(key, frac, cells):
    cell = key & (cells - 1)
    second = (cell + 1) & (cells - 1)
    spot = lax.broadcasted_iota(jnp.int32, (cells, key.shape[1]), 0)
    return jnp.where(spot == cell, 1.0 - frac, jnp.where(spot == second, frac, 0.0))


def chosen_rows(key, start, shift):
    row = (key >> shift) - start
    spot = lax.broadcasted_iota(jnp.int32, (BLOCK, key.shape[1]), 0)
    return jnp.where(spot == row, 1.0, 0.0).astype(jnp.bfloat16)


def window_of(bound, block, cells):
    parts = BLOCK // bound.shape[1]
    shift = cells.bit_length() - 1
    start = ((bound[block * parts, 0] >> shift) // ALIGN) * ALIGN
    last = bound[block * parts + parts - 1, bound.shape[1] - 1] >> shift
    return start, (last - start) // BLOCK + 1


def every_window(bound, blocks, cells, visit, visit_again):
    most = 1
    for block in range(blocks):
        start, count = window_of(bound, block, cells)
        most = jnp.maximum(most, count)
        visit(block, start)

    @pl.when(most > 1)
    def _():
        def of_block(block, carry):
            start, count = window_of(bound, block, cells)

            def of_window(window, inner):
                visit_again(block, start + window * BLOCK)
                return inner

            return lax.fori_loop(1, count, of_window, carry)

        lax.fori_loop(0, blocks, of_block, 0)


def each_field(fields, visit):
    def step(field, carry):
        visit(field)
        return carry

    lax.fori_loop(0, fields, step, 0)


def load_of(field, source, at, held, sems):
    return pltpu.make_async_copy(source.at[at], held.at[field], sems.at[field])


def start_loads(members, nvars, ens, stat, held, sems):
    for m in range(members):
        load_of(m, ens, m, held, sems).start()
    for v in range(nvars):
        load_of(members + v, stat, v, held, sems).start()


def pack_kernel(dims, ens, stat, side_a, side_b, held, sems):
    members, nvars, levels, rows, cells, blocks, copies = dims
    start_loads(members, nvars, ens, stat, held, sems)
    for field in range(members + nvars):
        load_of(field, ens, 0, held, sems).wait()
        for begin, side in zip(begins(rows), (side_a, side_b)):
            for j in range(SWEEPS):
                side[field, pl.ds(j * levels, levels), :] = held[field, pl.ds(begin + j, levels, stride=rows), :]


def own_kernel(dims, powers, ens, stat, group, localize, static, out, held, sems):
    members, nvars, levels, rows, cells, blocks, copies = dims
    inside = neighbours()
    start_loads(members, nvars, ens, stat, held, sems)

    def of_field(field):
        load_of(field, ens, 0, held, sems).wait()
        planes = {x: held[field, pl.ds(x, levels, stride=rows), :] for x in range(rows)}
        rate = rate_of(field, members, group, localize, static)
        planes = spread_product(planes, rows, rate, inside, powers)
        for x in range(rows):
            out[field, pl.ds(x * levels, levels), :] = planes[x]

    each_field(members + nvars, of_field)


def with_sides(dims, own, side_a, side_b, field, rate):
    members, nvars, levels, rows, cells, blocks, copies = dims
    lower, upper = sides_of(side_a, side_b, field, levels)
    lower = spread_rolled({j - SWEEPS: lower[j] for j in range(SWEEPS)}, 0, SWEEPS - 1, rows, rate, (1.0, 1.0))
    upper = spread_rolled({rows + j: upper[j] for j in range(SWEEPS)}, rows - SWEEPS, rows - 1, rows, rate, (1.0, 1.0))
    planes = {}
    for x in range(rows):
        planes[x] = own[field, pl.ds(x * levels, levels), :]
        for extra in (lower, upper):
            if x in extra:
                planes[x] = planes[x] + extra[x]
    return planes


def forward_kernel(dims, own, scale, side_a, side_b, key, frac, perturb_far, bound, group, localize, static, out, smooth, table, perturb, sem):
    members, nvars, levels, rows, cells, blocks, copies = dims
    shift = cells.bit_length() - 1
    load = pltpu.make_async_copy(perturb_far, perturb, sem)
    load.start()

    def of_field(field):
        rate = rate_of(field, members, group, localize, static)
        planes = with_sides(dims, own, side_a, side_b, field, rate)
        for x in range(rows):
            smooth[field, pl.ds(x, levels, stride=rows), :] = planes[x] * scale[field]

    each_field(members + nvars, of_field)
    load.wait()
    plane = levels * rows
    for v in range(nvars):
        total = smooth[members + v]
        for m in range(members):
            total = total + perturb[m, v].astype(jnp.float32) * smooth[m]
        high, low = halves(total)
        table[v * plane : (v + 1) * plane, :cells] = high
        table[v * plane : (v + 1) * plane, cells:] = low
    table[nvars * plane :, :] = jnp.zeros((BLOCK, 2 * cells), jnp.bfloat16)
    lanes = key.shape[1]
    parts = BLOCK // lanes

    def seen_in(block, start):
        keys = block_of(key, block)
        picked = lax.dot_general(
            table[pl.ds(pl.multiple_of(start, ALIGN), BLOCK), :],
            chosen_rows(keys, start, shift),
            (((0,), (0,)), ((), ())),
            preferred_element_type=jnp.float32,
        )
        picked = picked[:cells] + picked[cells:]
        return jnp.sum(picked * weights_of(keys, block_of(frac, block), cells), axis=0, keepdims=True)

    def visit(block, start):
        seen = seen_in(block, start)
        for part in range(parts):
            out[0, pl.ds(block * parts + part, 1), :] = seen[:, part * lanes : (part + 1) * lanes]

    def visit_again(block, start):
        seen = seen_in(block, start)
        for part in range(parts):
            at = pl.ds(block * parts + part, 1)
            out[0, at, :] = out[0, at, :] + seen[:, part * lanes : (part + 1) * lanes]

    every_window(bound, blocks, cells, visit, visit_again)
    for copy in range(1, copies):
        out[copy] = out[0]


def scatter_kernel(dims, parts, key, frac, weight, perturb, scale, bound, source, side_a, side_b, gradient, valued):
    members, nvars, levels, rows, cells, blocks, copies = dims
    shift = cells.bit_length() - 1
    seen = parts[0]
    for copy in range(1, copies):
        seen = seen + parts[copy]
    valued[...] = seen * weight[...]
    gradient[...] = jnp.zeros(gradient.shape, jnp.float32)

    def add_block(block, start):
        keys = block_of(key, block)
        placed = weights_of(keys, block_of(frac, block), cells) * block_of(valued, block)
        high, low = halves(placed)
        both = lax.dot_general(
            chosen_rows(keys, start, shift),
            jnp.concatenate([high, low], axis=0),
            (((1,), (1,)), ((), ())),
            preferred_element_type=jnp.float32,
        )
        at = pl.ds(pl.multiple_of(start, ALIGN), BLOCK)
        gradient[at, :] = gradient[at, :] + (both[:, :cells] + both[:, cells:])

    every_window(bound, blocks, cells, add_block, add_block)

    plane = levels * rows
    for m in range(members):
        total = perturb[m, 0].astype(jnp.float32) * gradient[:plane, :]
        for v in range(1, nvars):
            total = total + perturb[m, v].astype(jnp.float32) * gradient[v * plane : (v + 1) * plane, :]
        source[m] = total
    for begin, side in zip(begins(rows), (side_a, side_b)):
        for field in range(members + nvars):
            for j in range(SWEEPS):
                if field < members:
                    strip = source[field, pl.ds(begin + j, levels, stride=rows), :]
                else:
                    at = (field - members) * plane + begin + j
                    strip = gradient[pl.ds(at, levels, stride=rows), :] * scale[field]
                side[field, pl.ds(j * levels, levels), :] = strip


def local_kernel(dims, powers, source, gradient, scale, held, group, localize, static, out):
    members, nvars, levels, rows, cells, blocks, copies = dims
    inside = neighbours()
    plane = levels * rows

    def of_field(field, planes):
        rate = rate_of(field, members, group, localize, static)
        planes = spread_product(planes, rows, rate, inside, powers)
        for x in range(rows):
            out[field, pl.ds(x * levels, levels), :] = held[field, pl.ds(x, levels, stride=rows), :] + planes[x]

    def of_member(m):
        of_field(m, {x: source[m, pl.ds(x, levels, stride=rows), :] for x in range(rows)})

    def of_group(v):
        field = members + v
        planes = {x: gradient[pl.ds(v * plane + x, levels, stride=rows), :] * scale[field] for x in range(rows)}
        of_field(field, planes)

    each_field(members, of_member)
    each_field(nvars, of_group)


def edge_kernel(dims, own, side_a, side_b, group, localize, static, hv_ens, hv_stat, after, sems):
    members, nvars, levels, rows, cells, blocks, copies = dims

    def write_of(field, out, at):
        return pltpu.make_async_copy(after.at[field], out.at[at], sems.at[field])

    def of_field(field, out, at):
        rate = rate_of(field, members, group, localize, static)
        planes = with_sides(dims, own, side_a, side_b, field, rate)
        for x in range(rows):
            after[field, pl.ds(x, levels, stride=rows), :] = planes[x]
        write_of(field, out, at).start()

    each_field(members, lambda m: of_field(m, hv_ens, m))
    each_field(nvars, lambda v: of_field(members + v, hv_stat, v))
    each_field(members, lambda m: write_of(m, hv_ens, m).wait())
    each_field(nvars, lambda v: write_of(members + v, hv_stat, v).wait())


def exchange(side_a, side_b):
    count = lax.axis_size("tile")
    pairs_a = [(i, i ^ 1) for i in range(count)]
    pairs_b = [(i, ((i + 1) ^ 1) - 1) for i in range(1, count - 1)]
    return lax.ppermute(side_a, "tile", pairs_a), lax.ppermute(side_b, "tile", pairs_b)


VMEM = pl.BlockSpec(memory_space=pltpu.VMEM)
SMEM = pl.BlockSpec(memory_space=pltpu.SMEM)
HBM = pl.BlockSpec(memory_space=pltpu.HBM)


def call(kernel, dims, outs, ins, far=(), scalars=(), scratch=(), out_spec=VMEM, cost=2_000_000):
    def body(*refs):
        kernel(dims, *refs)

    far = [pltpu.with_memory_space_constraint(x, pltpu.HBM) for x in far]
    return pl.pallas_call(
        body,
        out_shape=tuple(jax.ShapeDtypeStruct(shape, jnp.float32) for shape in outs),
        in_specs=[VMEM] * len(ins) + [HBM] * len(far) + [SMEM] * len(scalars),
        out_specs=tuple([out_spec] * len(outs)),
        scratch_shapes=list(scratch),
        compiler_params=pltpu.CompilerParams(vmem_limit_bytes=16 * 1024 * 1024),
        cost_estimate=pl.CostEstimate(flops=cost * 10, bytes_accessed=cost, transcendentals=0),
        name=kernel.__name__,
    )(*ins, *far, *scalars)


def per_device(
    ens_control,
    static_control,
    member_perturb,
    member_group,
    localize_rate,
    static_rate,
    static_scale,
    obs_index,
    obs_frac,
    obs_layer,
    obs_kind,
    obs_precision,
):
    members, levels, rows, cells = ens_control.shape
    nvars = static_control.shape[1]
    fields = members + nvars
    copies = lax.axis_size("grp")
    blocks = obs_index.shape[0] // BLOCK
    dims = (members, nvars, levels, rows, cells, blocks, copies)
    plane = levels * rows
    strip = (fields, SWEEPS * levels, cells)

    ens = ens_control.reshape(members, plane, cells)
    stat = static_control.reshape(nvars, plane, cells)
    perturb = member_perturb.reshape(members, nvars, plane, cells)
    rates = [member_group, localize_rate, static_rate]

    whole = (fields, plane, cells)
    powers = y_powers(cells)
    copying = [pltpu.SemaphoreType.DMA((fields,))]
    side_a, side_b = call(pack_kernel, dims, [strip, strip], [], [ens, stat], [], [pltpu.VMEM(whole, jnp.float32)] + copying)
    side_a, side_b = exchange(side_a, side_b)

    scale = jnp.concatenate([jnp.ones((members, levels), jnp.float32), static_scale[0]])
    scale = jnp.broadcast_to(scale[:, :, None], (fields, levels, cells))
    kind_ids = jnp.arange(obs_precision.shape[0], dtype=jnp.int32)
    weight = jnp.sum(
        jnp.where(obs_kind[:, None] == kind_ids[None, :], obs_precision[None, :], 0.0), axis=1
    )
    key = obs_layer * (rows * cells) + obs_index
    key, frac, weight = lax.sort((key, obs_frac, weight), num_keys=1, is_stable=False)
    key, frac, weight = (x.reshape(-1, cells) for x in (key, frac, weight))

    table_rows = nvars * plane + BLOCK
    own, held = call(own_kernel, dims, [whole, whole], [powers], [ens, stat], rates, copying)
    (seen,) = call(
        forward_kernel,
        dims,
        [(copies,) + key.shape],
        [own, scale, side_a, side_b, key, frac],
        [perturb],
        [key] + rates,
        [
            pltpu.VMEM(whole, jnp.float32),
            pltpu.VMEM((table_rows, 2 * cells), jnp.bfloat16),
            pltpu.VMEM(perturb.shape, perturb.dtype),
            pltpu.SemaphoreType.DMA(()),
        ],
    )
    parts = lax.all_to_all(seen, "grp", 0, 0)
    source, side_a, side_b, gradient = call(
        scatter_kernel,
        dims,
        [(members, plane, cells), strip, strip, (table_rows, cells)],
        [parts, key, frac, weight, perturb, scale],
        [],
        [key],
        [pltpu.VMEM(key.shape, jnp.float32)],
    )
    side_a, side_b = exchange(side_a, side_b)
    (own,) = call(local_kernel, dims, [whole], [powers, source, gradient, scale, held], [], rates)
    hv_ens, hv_stat = call(
        edge_kernel,
        dims,
        [(members, plane, cells), (nvars, plane, cells)],
        [own, side_a, side_b],
        [],
        rates,
        [pltpu.VMEM(whole, jnp.float32), pltpu.SemaphoreType.DMA((fields,))],
        HBM,
    )
    return hv_ens.reshape(ens_control.shape), hv_stat.reshape(static_control.shape)


def solution(mesh):
    placed = (
        P("grp", None, "tile", None),
        P("grp", None, None, "tile", None),
        P("grp", None, None, "tile", None),
        P("grp"),
        P(),
        P("grp"),
        P("grp", None, None),
        P("tile"),
        P("tile"),
        P("tile"),
        P("tile"),
        P(),
    )
    return jax.shard_map(
        per_device,
        mesh=mesh,
        in_specs=placed,
        out_specs=(P("grp", None, "tile", None), P("grp", None, None, "tile", None)),
        check_vma=False,
    )
```

```python
import math

import jax
import jax.numpy as jnp
import numpy as np
from jax import lax
from jax.experimental import pallas as pl
from jax.experimental.pallas import tpu as pltpu
from jax.sharding import PartitionSpec as P

SWEEPS = 4
BLOCK = 256
ALIGN = 16


def along_x(planes, wanted, rows, rate, inside):
    factors = [(1.0 - 4.0 * rate, rate)] + [((1.0 - 4.0 * rate) * side, rate * side) for side in inside]
    result = {}
    for x in wanted:
        keep, share = factors[1 if x < 0 else 2 if x >= rows else 0]
        total = None
        for near in (x - 1, x + 1):
            if near in planes:
                total = planes[near] if total is None else total + planes[near]
        if total is not None:
            total = share * total
        if x in planes:
            total = keep * planes[x] if total is None else keep * planes[x] + total
        if total is not None:
            result[x] = total
    return result


def powers_along_x(planes, first, last, rows, rate, inside):
    stages = [planes]
    for left in range(SWEEPS - 1, -1, -1):
        stages.append(along_x(stages[-1], range(first - left, last + left + 1), rows, rate, inside))
    return stages


def binomial(j, rate):
    factor = float(math.comb(SWEEPS, j))
    for number in range(j):
        factor = factor * rate
    return factor


def along_y(value):
    cells = value.shape[1]
    lane = lax.broadcasted_iota(jnp.int32, value.shape, 1)
    below = jnp.where(lane == 0, 0.0, pltpu.roll(value, 1, 1))
    return below + jnp.where(lane == cells - 1, 0.0, pltpu.roll(value, cells - 1, 1))


def spread_rolled(planes, first, last, rows, rate, inside):
    stages = powers_along_x(planes, first, last, rows, rate, inside)
    result = {}
    for x in range(first, last + 1):
        total = None
        for j in range(SWEEPS, -1, -1):
            if total is not None:
                total = along_y(total)
            term = stages[SWEEPS - j].get(x)
            if term is not None:
                term = term if j == 0 else binomial(j, rate) * term
                total = term if total is None else total + term
        result[x] = total
    return result


def halves(value):
    high = value.astype(jnp.bfloat16)
    low = (value - high.astype(jnp.float32)).astype(jnp.bfloat16)
    return high, low


def y_powers(cells):
    once = np.eye(cells, k=1) + np.eye(cells, k=-1)
    row = np.concatenate([np.linalg.matrix_power(once, j) for j in range(1, SWEEPS + 1)], axis=1)
    return jnp.asarray(np.concatenate([row, row], axis=0), jnp.bfloat16)


GROUP = 8


def spread_product(planes, rows, rate, inside, powers):
    levels, cells = planes[0].shape
    terms = [{} for j in range(SWEEPS)]
    for first in range(0, rows, GROUP):
        both = jnp.concatenate(halves(jnp.concatenate([planes[x] for x in range(first, first + GROUP)], axis=0)), axis=1)
        product = jnp.dot(both, powers[...], preferred_element_type=jnp.float32)
        for at in range(GROUP):
            for j in range(SWEEPS):
                terms[j][first + at] = product[at * levels : (at + 1) * levels, j * cells : (j + 1) * cells]
    result = planes
    for j in range(1, SWEEPS + 1):
        left = SWEEPS - j
        result = along_x(result, range(-left, rows + left), rows, rate, inside)
        factor = binomial(j, rate)
        for x in range(rows):
            result[x] = result[x] + factor * terms[j - 1][x]
    return result


def rate_of(field, members, group, localize, static):
    member = jnp.minimum(field, members - 1)
    return jnp.where(field < members, localize[group[member]], static[0])


def neighbours():
    tile = lax.axis_index("tile")
    last = lax.axis_size("tile") - 1
    return jnp.where(tile > 0, 1.0, 0.0), jnp.where(tile < last, 1.0, 0.0)


def is_even():
    return lax.axis_index("tile") % 2 == 0


def begins(rows):
    even = is_even()
    return jnp.where(even, rows - SWEEPS, 0), jnp.where(even, 0, rows - SWEEPS)


def sides_of(side_a, side_b, field, levels):
    even = is_even()
    lower, upper = [], []
    for j in range(SWEEPS):
        a = side_a[field, pl.ds(j * levels, levels), :]
        b = side_b[field, pl.ds(j * levels, levels), :]
        lower.append(jnp.where(even, b, a))
        upper.append(jnp.where(even, a, b))
    return lower, upper


def block_of(ref, block):
    lanes = ref.shape[1]
    parts = BLOCK // lanes
    return jnp.concatenate([ref[pl.ds(block * parts + part, 1), :] for part in range(parts)], axis=1)


def weights_of(key, frac, cells):
    cell = key & (cells - 1)
    second = (cell + 1) & (cells - 1)
    spot = lax.broadcasted_iota(jnp.int32, (cells, key.shape[1]), 0)
    return jnp.where(spot == cell, 1.0 - frac, jnp.where(spot == second, frac, 0.0))


def chosen_rows(key, start, shift):
    row = (key >> shift) - start
    spot = lax.broadcasted_iota(jnp.int32, (BLOCK, key.shape[1]), 0)
    return jnp.where(spot == row, 1.0, 0.0).astype(jnp.bfloat16)


def window_of(bound, block, cells):
    parts = BLOCK // bound.shape[1]
    shift = cells.bit_length() - 1
    start = ((bound[block * parts, 0] >> shift) // ALIGN) * ALIGN
    last = bound[block * parts + parts - 1, bound.shape[1] - 1] >> shift
    return start, (last - start) // BLOCK + 1


def every_window(bound, blocks, cells, visit, visit_again):
    most = 1
    for block in range(blocks):
        start, count = window_of(bound, block, cells)
        most = jnp.maximum(most, count)
        visit(block, start)

    @pl.when(most > 1)
    def _():
        def of_block(block, carry):
            start, count = window_of(bound, block, cells)

            def of_window(window, inner):
                visit_again(block, start + window * BLOCK)
                return inner

            return lax.fori_loop(1, count, of_window, carry)

        lax.fori_loop(0, blocks, of_block, 0)


def each_field(fields, visit):
    def step(field, carry):
        visit(field)
        return carry

    lax.fori_loop(0, fields, step, 0)


def load_of(field, source, at, held, sems):
    return pltpu.make_async_copy(source.at[at], held.at[field], sems.at[field])


def start_loads(members, nvars, ens, stat, held, sems):
    for m in range(members):
        load_of(m, ens, m, held, sems).start()
    for v in range(nvars):
        load_of(members + v, stat, v, held, sems).start()


def pack_kernel(dims, ens, stat, side_a, side_b, held, sems):
    members, nvars, levels, rows, cells, blocks = dims
    start_loads(members, nvars, ens, stat, held, sems)
    for field in range(members + nvars):
        load_of(field, ens, 0, held, sems).wait()
        for begin, side in zip(begins(rows), (side_a, side_b)):
            for j in range(SWEEPS):
                side[field, pl.ds(j * levels, levels), :] = held[field, pl.ds(begin + j, levels, stride=rows), :]


def own_kernel(dims, powers, ens, stat, group, localize, static, out, held, sems):
    members, nvars, levels, rows, cells, blocks = dims
    inside = neighbours()
    start_loads(members, nvars, ens, stat, held, sems)

    def of_field(field):
        load_of(field, ens, 0, held, sems).wait()
        planes = {x: held[field, pl.ds(x, levels, stride=rows), :] for x in range(rows)}
        rate = rate_of(field, members, group, localize, static)
        planes = spread_product(planes, rows, rate, inside, powers)
        for x in range(rows):
            out[field, pl.ds(x * levels, levels), :] = planes[x]

    each_field(members + nvars, of_field)


def with_sides(dims, own, side_a, side_b, field, rate):
    members, nvars, levels, rows, cells, blocks = dims
    lower, upper = sides_of(side_a, side_b, field, levels)
    lower = spread_rolled({j - SWEEPS: lower[j] for j in range(SWEEPS)}, 0, SWEEPS - 1, rows, rate, (1.0, 1.0))
    upper = spread_rolled({rows + j: upper[j] for j in range(SWEEPS)}, rows - SWEEPS, rows - 1, rows, rate, (1.0, 1.0))
    planes = {}
    for x in range(rows):
        planes[x] = own[field, pl.ds(x * levels, levels), :]
        for extra in (lower, upper):
            if x in extra:
                planes[x] = planes[x] + extra[x]
    return planes


def forward_kernel(dims, own, scale, side_a, side_b, key, frac, perturb_far, bound, group, localize, static, out, smooth, table, perturb, sem):
    members, nvars, levels, rows, cells, blocks = dims
    shift = cells.bit_length() - 1
    load = pltpu.make_async_copy(perturb_far, perturb, sem)
    load.start()

    def of_field(field):
        rate = rate_of(field, members, group, localize, static)
        planes = with_sides(dims, own, side_a, side_b, field, rate)
        for x in range(rows):
            smooth[field, pl.ds(x, levels, stride=rows), :] = planes[x] * scale[field]

    each_field(members + nvars, of_field)
    load.wait()
    plane = levels * rows
    for v in range(nvars):
        total = smooth[members + v]
        for m in range(members):
            total = total + perturb[m, v].astype(jnp.float32) * smooth[m]
        high, low = halves(total)
        table[v * plane : (v + 1) * plane, :cells] = high
        table[v * plane : (v + 1) * plane, cells:] = low
    table[nvars * plane :, :] = jnp.zeros((BLOCK, 2 * cells), jnp.bfloat16)
    lanes = key.shape[1]
    parts = BLOCK // lanes

    def seen_in(block, start):
        keys = block_of(key, block)
        picked = lax.dot_general(
            table[pl.ds(pl.multiple_of(start, ALIGN), BLOCK), :],
            chosen_rows(keys, start, shift),
            (((0,), (0,)), ((), ())),
            preferred_element_type=jnp.float32,
        )
        picked = picked[:cells] + picked[cells:]
        return jnp.sum(picked * weights_of(keys, block_of(frac, block), cells), axis=0, keepdims=True)

    def visit(block, start):
        seen = seen_in(block, start)
        for part in range(parts):
            out[pl.ds(block * parts + part, 1), :] = seen[:, part * lanes : (part + 1) * lanes]

    def visit_again(block, start):
        seen = seen_in(block, start)
        for part in range(parts):
            at = pl.ds(block * parts + part, 1)
            out[at, :] = out[at, :] + seen[:, part * lanes : (part + 1) * lanes]

    every_window(bound, blocks, cells, visit, visit_again)


def scatter_kernel(dims, seen, others, key, frac, weight, perturb, scale, bound, source, side_a, side_b, gradient, valued):
    members, nvars, levels, rows, cells, blocks = dims
    shift = cells.bit_length() - 1
    valued[...] = (seen[...] + others[...]) * weight[...]
    gradient[...] = jnp.zeros(gradient.shape, jnp.float32)

    def add_block(block, start):
        keys = block_of(key, block)
        placed = weights_of(keys, block_of(frac, block), cells) * block_of(valued, block)
        high, low = halves(placed)
        both = lax.dot_general(
            chosen_rows(keys, start, shift),
            jnp.concatenate([high, low], axis=0),
            (((1,), (1,)), ((), ())),
            preferred_element_type=jnp.float32,
        )
        at = pl.ds(pl.multiple_of(start, ALIGN), BLOCK)
        gradient[at, :] = gradient[at, :] + (both[:, :cells] + both[:, cells:])

    every_window(bound, blocks, cells, add_block, add_block)

    plane = levels * rows
    for m in range(members):
        total = perturb[m, 0].astype(jnp.float32) * gradient[:plane, :]
        for v in range(1, nvars):
            total = total + perturb[m, v].astype(jnp.float32) * gradient[v * plane : (v + 1) * plane, :]
        source[m] = total
    for begin, side in zip(begins(rows), (side_a, side_b)):
        for field in range(members + nvars):
            for j in range(SWEEPS):
                if field < members:
                    strip = source[field, pl.ds(begin + j, levels, stride=rows), :]
                else:
                    at = (field - members) * plane + begin + j
                    strip = gradient[pl.ds(at, levels, stride=rows), :] * scale[field]
                side[field, pl.ds(j * levels, levels), :] = strip


def local_kernel(dims, powers, source, gradient, scale, held, group, localize, static, out):
    members, nvars, levels, rows, cells, blocks = dims
    inside = neighbours()
    plane = levels * rows

    def of_field(field, planes):
        rate = rate_of(field, members, group, localize, static)
        planes = spread_product(planes, rows, rate, inside, powers)
        for x in range(rows):
            out[field, pl.ds(x * levels, levels), :] = held[field, pl.ds(x, levels, stride=rows), :] + planes[x]

    def of_member(m):
        of_field(m, {x: source[m, pl.ds(x, levels, stride=rows), :] for x in range(rows)})

    def of_group(v):
        field = members + v
        planes = {x: gradient[pl.ds(v * plane + x, levels, stride=rows), :] * scale[field] for x in range(rows)}
        of_field(field, planes)

    each_field(members, of_member)
    each_field(nvars, of_group)


def edge_kernel(dims, own, side_a, side_b, group, localize, static, hv_ens, hv_stat, after, sems):
    members, nvars, levels, rows, cells, blocks = dims

    def write_of(field, out, at):
        return pltpu.make_async_copy(after.at[field], out.at[at], sems.at[field])

    def of_field(field, out, at):
        rate = rate_of(field, members, group, localize, static)
        planes = with_sides(dims, own, side_a, side_b, field, rate)
        for x in range(rows):
            after[field, pl.ds(x, levels, stride=rows), :] = planes[x]
        write_of(field, out, at).start()

    each_field(members, lambda m: of_field(m, hv_ens, m))
    each_field(nvars, lambda v: of_field(members + v, hv_stat, v))
    each_field(members, lambda m: write_of(m, hv_ens, m).wait())
    each_field(nvars, lambda v: write_of(members + v, hv_stat, v).wait())


def exchange(side_a, side_b):
    count = lax.axis_size("tile")
    pairs_a = [(i, i ^ 1) for i in range(count)]
    pairs_b = [(i, ((i + 1) ^ 1) - 1) for i in range(1, count - 1)]
    return lax.ppermute(side_a, "tile", pairs_a), lax.ppermute(side_b, "tile", pairs_b)


def halved_sums(value):
    count = lax.axis_size("grp")
    others = None
    for turn in (2, 6, 1) if count == 8 else [1 << bit for bit in range(count.bit_length() - 1)]:
        if others is not None:
            value = value + others
        others = lax.ppermute(value, "grp", [(i, i ^ turn) for i in range(count)])
    return value, others


VMEM = pl.BlockSpec(memory_space=pltpu.VMEM)
SMEM = pl.BlockSpec(memory_space=pltpu.SMEM)
HBM = pl.BlockSpec(memory_space=pltpu.HBM)


def call(kernel, dims, outs, ins, far=(), scalars=(), scratch=(), out_spec=VMEM, cost=2_000_000):
    def body(*refs):
        kernel(dims, *refs)

    far = [pltpu.with_memory_space_constraint(x, pltpu.HBM) for x in far]
    return pl.pallas_call(
        body,
        out_shape=tuple(jax.ShapeDtypeStruct(shape, jnp.float32) for shape in outs),
        in_specs=[VMEM] * len(ins) + [HBM] * len(far) + [SMEM] * len(scalars),
        out_specs=tuple([out_spec] * len(outs)),
        scratch_shapes=list(scratch),
        compiler_params=pltpu.CompilerParams(vmem_limit_bytes=16 * 1024 * 1024),
        cost_estimate=pl.CostEstimate(flops=cost * 10, bytes_accessed=cost, transcendentals=0),
        name=kernel.__name__,
    )(*ins, *far, *scalars)


def per_device(
    ens_control,
    static_control,
    member_perturb,
    member_group,
    localize_rate,
    static_rate,
    static_scale,
    obs_index,
    obs_frac,
    obs_layer,
    obs_kind,
    obs_precision,
):
    members, levels, rows, cells = ens_control.shape
    nvars = static_control.shape[1]
    fields = members + nvars
    blocks = obs_index.shape[0] // BLOCK
    dims = (members, nvars, levels, rows, cells, blocks)
    plane = levels * rows
    strip = (fields, SWEEPS * levels, cells)

    ens = ens_control.reshape(members, plane, cells)
    stat = static_control.reshape(nvars, plane, cells)
    perturb = member_perturb.reshape(members, nvars, plane, cells)
    rates = [member_group, localize_rate, static_rate]

    whole = (fields, plane, cells)
    powers = y_powers(cells)
    copying = [pltpu.SemaphoreType.DMA((fields,))]
    side_a, side_b = call(pack_kernel, dims, [strip, strip], [], [ens, stat], [], [pltpu.VMEM(whole, jnp.float32)] + copying)
    side_a, side_b = exchange(side_a, side_b)

    scale = jnp.concatenate([jnp.ones((members, levels), jnp.float32), static_scale[0]])
    scale = jnp.broadcast_to(scale[:, :, None], (fields, levels, cells))
    kind_ids = jnp.arange(obs_precision.shape[0], dtype=jnp.int32)
    weight = jnp.sum(
        jnp.where(obs_kind[:, None] == kind_ids[None, :], obs_precision[None, :], 0.0), axis=1
    )
    key = obs_layer * (rows * cells) + obs_index
    key, frac, weight = lax.sort((key, obs_frac, weight), num_keys=1, is_stable=False)
    key, frac, weight = (x.reshape(-1, cells) for x in (key, frac, weight))

    table_rows = nvars * plane + BLOCK
    own, held = call(own_kernel, dims, [whole, whole], [powers], [ens, stat], rates, copying)
    (seen,) = call(
        forward_kernel,
        dims,
        [key.shape],
        [own, scale, side_a, side_b, key, frac],
        [perturb],
        [key] + rates,
        [
            pltpu.VMEM(whole, jnp.float32),
            pltpu.VMEM((table_rows, 2 * cells), jnp.bfloat16),
            pltpu.VMEM(perturb.shape, perturb.dtype),
            pltpu.SemaphoreType.DMA(()),
        ],
    )
    seen, others = halved_sums(seen)
    source, side_a, side_b, gradient = call(
        scatter_kernel,
        dims,
        [(members, plane, cells), strip, strip, (table_rows, cells)],
        [seen, others, key, frac, weight, perturb, scale],
        [],
        [key],
        [pltpu.VMEM(key.shape, jnp.float32)],
    )
    side_a, side_b = exchange(side_a, side_b)
    (own,) = call(local_kernel, dims, [whole], [powers, source, gradient, scale, held], [], rates)
    hv_ens, hv_stat = call(
        edge_kernel,
        dims,
        [(members, plane, cells), (nvars, plane, cells)],
        [own, side_a, side_b],
        [],
        rates,
        [pltpu.VMEM(whole, jnp.float32), pltpu.SemaphoreType.DMA((fields,))],
        HBM,
    )
    return hv_ens.reshape(ens_control.shape), hv_stat.reshape(static_control.shape)


def solution(mesh):
    placed = (
        P("grp", None, "tile", None),
        P("grp", None, None, "tile", None),
        P("grp", None, None, "tile", None),
        P("grp"),
        P(),
        P("grp"),
        P("grp", None, None),
        P("tile"),
        P("tile"),
        P("tile"),
        P("tile"),
        P(),
    )
    return jax.shard_map(
        per_device,
        mesh=mesh,
        in_specs=placed,
        out_specs=(P("grp", None, "tile", None), P("grp", None, None, "tile", None)),
        check_vma=False,
    )
```

```python
import math

import jax
import jax.numpy as jnp
import numpy as np
from jax import lax
from jax.experimental import pallas as pl
from jax.experimental.pallas import tpu as pltpu
from jax.sharding import PartitionSpec as P

SWEEPS = 4
BLOCK = 256
ALIGN = 16


def along_x(planes, wanted, rows, rate, inside):
    factors = [(1.0 - 4.0 * rate, rate)] + [((1.0 - 4.0 * rate) * side, rate * side) for side in inside]
    result = {}
    for x in wanted:
        keep, share = factors[1 if x < 0 else 2 if x >= rows else 0]
        total = None
        for near in (x - 1, x + 1):
            if near in planes:
                total = planes[near] if total is None else total + planes[near]
        if total is not None:
            total = share * total
        if x in planes:
            total = keep * planes[x] if total is None else keep * planes[x] + total
        if total is not None:
            result[x] = total
    return result


def powers_along_x(planes, first, last, rows, rate, inside):
    stages = [planes]
    for left in range(SWEEPS - 1, -1, -1):
        stages.append(along_x(stages[-1], range(first - left, last + left + 1), rows, rate, inside))
    return stages


def binomial(j, rate):
    factor = float(math.comb(SWEEPS, j))
    for number in range(j):
        factor = factor * rate
    return factor


def along_y(value):
    cells = value.shape[1]
    lane = lax.broadcasted_iota(jnp.int32, value.shape, 1)
    below = jnp.where(lane == 0, 0.0, pltpu.roll(value, 1, 1))
    return below + jnp.where(lane == cells - 1, 0.0, pltpu.roll(value, cells - 1, 1))


def spread_rolled(planes, first, last, rows, rate, inside):
    stages = powers_along_x(planes, first, last, rows, rate, inside)
    result = {}
    for x in range(first, last + 1):
        total = None
        for j in range(SWEEPS, -1, -1):
            if total is not None:
                total = along_y(total)
            term = stages[SWEEPS - j].get(x)
            if term is not None:
                term = term if j == 0 else binomial(j, rate) * term
                total = term if total is None else total + term
        result[x] = total
    return result


def halves(value):
    high = value.astype(jnp.bfloat16)
    low = (value - high.astype(jnp.float32)).astype(jnp.bfloat16)
    return high, low


def y_powers(cells):
    once = np.eye(cells, k=1) + np.eye(cells, k=-1)
    row = np.concatenate([np.linalg.matrix_power(once, j) for j in range(1, SWEEPS + 1)], axis=1)
    return jnp.asarray(np.concatenate([row, row], axis=0), jnp.bfloat16)


GROUP = 8


def spread_product(planes, rows, rate, inside, powers):
    levels, cells = planes[0].shape
    terms = [{} for j in range(SWEEPS)]
    for first in range(0, rows, GROUP):
        both = jnp.concatenate(halves(jnp.concatenate([planes[x] for x in range(first, first + GROUP)], axis=0)), axis=1)
        product = jnp.dot(both, powers[...], preferred_element_type=jnp.float32)
        for at in range(GROUP):
            for j in range(SWEEPS):
                terms[j][first + at] = product[at * levels : (at + 1) * levels, j * cells : (j + 1) * cells]
    result = planes
    for j in range(1, SWEEPS + 1):
        left = SWEEPS - j
        result = along_x(result, range(-left, rows + left), rows, rate, inside)
        factor = binomial(j, rate)
        for x in range(rows):
            result[x] = result[x] + factor * terms[j - 1][x]
    return result


def rate_of(field, members, group, localize, static):
    member = jnp.minimum(field, members - 1)
    return jnp.where(field < members, localize[group[member]], static[0])


def neighbours():
    tile = lax.axis_index("tile")
    last = lax.axis_size("tile") - 1
    return jnp.where(tile > 0, 1.0, 0.0), jnp.where(tile < last, 1.0, 0.0)


def is_even():
    return lax.axis_index("tile") % 2 == 0


def begins(rows):
    even = is_even()
    return jnp.where(even, rows - SWEEPS, 0), jnp.where(even, 0, rows - SWEEPS)


def sides_of(side_a, side_b, field, levels):
    even = is_even()
    lower, upper = [], []
    for j in range(SWEEPS):
        a = side_a[field, pl.ds(j * levels, levels), :]
        b = side_b[field, pl.ds(j * levels, levels), :]
        lower.append(jnp.where(even, b, a))
        upper.append(jnp.where(even, a, b))
    return lower, upper


def block_of(ref, block):
    lanes = ref.shape[1]
    parts = BLOCK // lanes
    return jnp.concatenate([ref[pl.ds(block * parts + part, 1), :] for part in range(parts)], axis=1)


def weights_of(key, frac, cells):
    cell = key & (cells - 1)
    second = (cell + 1) & (cells - 1)
    spot = lax.broadcasted_iota(jnp.int32, (cells, key.shape[1]), 0)
    return jnp.where(spot == cell, 1.0 - frac, jnp.where(spot == second, frac, 0.0))


def chosen_rows(key, start, shift):
    row = (key >> shift) - start
    spot = lax.broadcasted_iota(jnp.int32, (BLOCK, key.shape[1]), 0)
    return jnp.where(spot == row, 1.0, 0.0).astype(jnp.bfloat16)


def window_of(bound, block, cells):
    parts = BLOCK // bound.shape[1]
    shift = cells.bit_length() - 1
    start = ((bound[block * parts, 0] >> shift) // ALIGN) * ALIGN
    last = bound[block * parts + parts - 1, bound.shape[1] - 1] >> shift
    return start, (last - start) // BLOCK + 1


def every_window(bound, blocks, cells, visit, visit_again):
    most = 1
    for block in range(blocks):
        start, count = window_of(bound, block, cells)
        most = jnp.maximum(most, count)
        visit(block, start)

    @pl.when(most > 1)
    def _():
        def of_block(block, carry):
            start, count = window_of(bound, block, cells)

            def of_window(window, inner):
                visit_again(block, start + window * BLOCK)
                return inner

            return lax.fori_loop(1, count, of_window, carry)

        lax.fori_loop(0, blocks, of_block, 0)


def each_field(fields, visit):
    def step(field, carry):
        visit(field)
        return carry

    lax.fori_loop(0, fields, step, 0)


def load_of(field, source, at, held, sems):
    return pltpu.make_async_copy(source.at[at], held.at[field], sems.at[field])


def start_loads(members, nvars, ens, stat, held, sems):
    for m in range(members):
        load_of(m, ens, m, held, sems).start()
    for v in range(nvars):
        load_of(members + v, stat, v, held, sems).start()


def pack_kernel(dims, ens, stat, side_a, side_b, held, sems):
    members, nvars, levels, rows, cells, blocks = dims
    start_loads(members, nvars, ens, stat, held, sems)
    for field in range(members + nvars):
        load_of(field, ens, 0, held, sems).wait()
        for begin, side in zip(begins(rows), (side_a, side_b)):
            for j in range(SWEEPS):
                side[field, pl.ds(j * levels, levels), :] = held[field, pl.ds(begin + j, levels, stride=rows), :]


def own_kernel(dims, powers, ens, stat, group, localize, static, out, held, sems):
    members, nvars, levels, rows, cells, blocks = dims
    inside = neighbours()
    start_loads(members, nvars, ens, stat, held, sems)

    def of_field(field):
        load_of(field, ens, 0, held, sems).wait()
        planes = {x: held[field, pl.ds(x, levels, stride=rows), :] for x in range(rows)}
        rate = rate_of(field, members, group, localize, static)
        planes = spread_product(planes, rows, rate, inside, powers)
        for x in range(rows):
            out[field, pl.ds(x * levels, levels), :] = planes[x]

    each_field(members + nvars, of_field)


def with_sides(dims, own, side_a, side_b, field, rate):
    members, nvars, levels, rows, cells, blocks = dims
    lower, upper = sides_of(side_a, side_b, field, levels)
    lower = spread_rolled({j - SWEEPS: lower[j] for j in range(SWEEPS)}, 0, SWEEPS - 1, rows, rate, (1.0, 1.0))
    upper = spread_rolled({rows + j: upper[j] for j in range(SWEEPS)}, rows - SWEEPS, rows - 1, rows, rate, (1.0, 1.0))
    planes = {}
    for x in range(rows):
        planes[x] = own[field, pl.ds(x * levels, levels), :]
        for extra in (lower, upper):
            if x in extra:
                planes[x] = planes[x] + extra[x]
    return planes


def forward_kernel(dims, own, scale, side_a, side_b, key, frac, perturb_far, bound, group, localize, static, out, smooth, table, perturb, sem):
    members, nvars, levels, rows, cells, blocks = dims
    shift = cells.bit_length() - 1
    load = pltpu.make_async_copy(perturb_far, perturb, sem)
    load.start()

    def of_field(field):
        rate = rate_of(field, members, group, localize, static)
        planes = with_sides(dims, own, side_a, side_b, field, rate)
        for x in range(rows):
            smooth[field, pl.ds(x, levels, stride=rows), :] = planes[x] * scale[field]

    each_field(members + nvars, of_field)
    load.wait()
    plane = levels * rows
    for v in range(nvars):
        total = smooth[members + v]
        for m in range(members):
            total = total + perturb[m, v].astype(jnp.float32) * smooth[m]
        high, low = halves(total)
        table[v * plane : (v + 1) * plane, :cells] = high
        table[v * plane : (v + 1) * plane, cells:] = low
    table[nvars * plane :, :] = jnp.zeros((BLOCK, 2 * cells), jnp.bfloat16)
    lanes = key.shape[1]
    parts = BLOCK // lanes

    def seen_in(block, start):
        keys = block_of(key, block)
        picked = lax.dot_general(
            table[pl.ds(pl.multiple_of(start, ALIGN), BLOCK), :],
            chosen_rows(keys, start, shift),
            (((0,), (0,)), ((), ())),
            preferred_element_type=jnp.float32,
        )
        picked = picked[:cells] + picked[cells:]
        return jnp.sum(picked * weights_of(keys, block_of(frac, block), cells), axis=0, keepdims=True)

    def visit(block, start):
        seen = seen_in(block, start)
        for part in range(parts):
            out[pl.ds(block * parts + part, 1), :] = seen[:, part * lanes : (part + 1) * lanes]

    def visit_again(block, start):
        seen = seen_in(block, start)
        for part in range(parts):
            at = pl.ds(block * parts + part, 1)
            out[at, :] = out[at, :] + seen[:, part * lanes : (part + 1) * lanes]

    every_window(bound, blocks, cells, visit, visit_again)


def scatter_kernel(dims, seen, key, frac, weight, perturb, scale, bound, source, side_a, side_b, gradient, valued):
    members, nvars, levels, rows, cells, blocks = dims
    shift = cells.bit_length() - 1
    valued[...] = seen[...] * weight[...]
    gradient[...] = jnp.zeros(gradient.shape, jnp.float32)

    def add_block(block, start):
        keys = block_of(key, block)
        placed = weights_of(keys, block_of(frac, block), cells) * block_of(valued, block)
        high, low = halves(placed)
        both = lax.dot_general(
            chosen_rows(keys, start, shift),
            jnp.concatenate([high, low], axis=0),
            (((1,), (1,)), ((), ())),
            preferred_element_type=jnp.float32,
        )
        at = pl.ds(pl.multiple_of(start, ALIGN), BLOCK)
        gradient[at, :] = gradient[at, :] + (both[:, :cells] + both[:, cells:])

    every_window(bound, blocks, cells, add_block, add_block)

    plane = levels * rows
    for m in range(members):
        total = perturb[m, 0].astype(jnp.float32) * gradient[:plane, :]
        for v in range(1, nvars):
            total = total + perturb[m, v].astype(jnp.float32) * gradient[v * plane : (v + 1) * plane, :]
        source[m] = total
    for begin, side in zip(begins(rows), (side_a, side_b)):
        for field in range(members + nvars):
            for j in range(SWEEPS):
                if field < members:
                    strip = source[field, pl.ds(begin + j, levels, stride=rows), :]
                else:
                    at = (field - members) * plane + begin + j
                    strip = gradient[pl.ds(at, levels, stride=rows), :] * scale[field]
                side[field, pl.ds(j * levels, levels), :] = strip


def local_kernel(dims, powers, source, gradient, scale, held, group, localize, static, out):
    members, nvars, levels, rows, cells, blocks = dims
    inside = neighbours()
    plane = levels * rows

    def of_field(field, planes):
        rate = rate_of(field, members, group, localize, static)
        planes = spread_product(planes, rows, rate, inside, powers)
        for x in range(rows):
            out[field, pl.ds(x * levels, levels), :] = held[field, pl.ds(x, levels, stride=rows), :] + planes[x]

    def of_member(m):
        of_field(m, {x: source[m, pl.ds(x, levels, stride=rows), :] for x in range(rows)})

    def of_group(v):
        field = members + v
        planes = {x: gradient[pl.ds(v * plane + x, levels, stride=rows), :] * scale[field] for x in range(rows)}
        of_field(field, planes)

    each_field(members, of_member)
    each_field(nvars, of_group)


def edge_kernel(dims, own, side_a, side_b, group, localize, static, hv_ens, hv_stat, after, sems):
    members, nvars, levels, rows, cells, blocks = dims

    def write_of(field, out, at):
        return pltpu.make_async_copy(after.at[field], out.at[at], sems.at[field])

    def of_field(field, out, at):
        rate = rate_of(field, members, group, localize, static)
        planes = with_sides(dims, own, side_a, side_b, field, rate)
        for x in range(rows):
            after[field, pl.ds(x, levels, stride=rows), :] = planes[x]
        write_of(field, out, at).start()

    each_field(members, lambda m: of_field(m, hv_ens, m))
    each_field(nvars, lambda v: of_field(members + v, hv_stat, v))
    each_field(members, lambda m: write_of(m, hv_ens, m).wait())
    each_field(nvars, lambda v: write_of(members + v, hv_stat, v).wait())


def exchange(side_a, side_b):
    count = lax.axis_size("tile")
    pairs_a = [(i, i ^ 1) for i in range(count)]
    pairs_b = [(i, ((i + 1) ^ 1) - 1) for i in range(1, count - 1)]
    return lax.ppermute(side_a, "tile", pairs_a), lax.ppermute(side_b, "tile", pairs_b)


def summed(value):
    count, tiles = lax.axis_size("grp"), lax.axis_size("tile")
    odd = lax.axis_index("tile") % 2 == 1
    other = lax.ppermute(value, "tile", [(t - 1, t) for t in range(1, tiles, 2)])
    both = jnp.concatenate([value, other])
    for turn in (2, 6, 1) if count == 8 else [1 << bit for bit in range(count.bit_length() - 1)]:
        pairs = [(g * tiles + t, (g ^ turn) * tiles + t) for g in range(count) for t in range(1, tiles, 2)]
        both = both + lax.ppermute(both, ("grp", "tile"), pairs)
    mine, theirs = both[: value.shape[0]], both[value.shape[0] :]
    back = lax.ppermute(theirs, "tile", [(t, t - 1) for t in range(1, tiles, 2)])
    return jnp.where(odd, mine, back)


VMEM = pl.BlockSpec(memory_space=pltpu.VMEM)
SMEM = pl.BlockSpec(memory_space=pltpu.SMEM)
HBM = pl.BlockSpec(memory_space=pltpu.HBM)


def call(kernel, dims, outs, ins, far=(), scalars=(), scratch=(), out_spec=VMEM, cost=2_000_000):
    def body(*refs):
        kernel(dims, *refs)

    far = [pltpu.with_memory_space_constraint(x, pltpu.HBM) for x in far]
    return pl.pallas_call(
        body,
        out_shape=tuple(jax.ShapeDtypeStruct(shape, jnp.float32) for shape in outs),
        in_specs=[VMEM] * len(ins) + [HBM] * len(far) + [SMEM] * len(scalars),
        out_specs=tuple([out_spec] * len(outs)),
        scratch_shapes=list(scratch),
        compiler_params=pltpu.CompilerParams(vmem_limit_bytes=16 * 1024 * 1024),
        cost_estimate=pl.CostEstimate(flops=cost * 10, bytes_accessed=cost, transcendentals=0),
        name=kernel.__name__,
    )(*ins, *far, *scalars)


def per_device(
    ens_control,
    static_control,
    member_perturb,
    member_group,
    localize_rate,
    static_rate,
    static_scale,
    obs_index,
    obs_frac,
    obs_layer,
    obs_kind,
    obs_precision,
):
    members, levels, rows, cells = ens_control.shape
    nvars = static_control.shape[1]
    fields = members + nvars
    blocks = obs_index.shape[0] // BLOCK
    dims = (members, nvars, levels, rows, cells, blocks)
    plane = levels * rows
    strip = (fields, SWEEPS * levels, cells)

    ens = ens_control.reshape(members, plane, cells)
    stat = static_control.reshape(nvars, plane, cells)
    perturb = member_perturb.reshape(members, nvars, plane, cells)
    rates = [member_group, localize_rate, static_rate]

    whole = (fields, plane, cells)
    powers = y_powers(cells)
    copying = [pltpu.SemaphoreType.DMA((fields,))]
    side_a, side_b = call(pack_kernel, dims, [strip, strip], [], [ens, stat], [], [pltpu.VMEM(whole, jnp.float32)] + copying)
    side_a, side_b = exchange(side_a, side_b)

    scale = jnp.concatenate([jnp.ones((members, levels), jnp.float32), static_scale[0]])
    scale = jnp.broadcast_to(scale[:, :, None], (fields, levels, cells))
    kind_ids = jnp.arange(obs_precision.shape[0], dtype=jnp.int32)
    weight = jnp.sum(
        jnp.where(obs_kind[:, None] == kind_ids[None, :], obs_precision[None, :], 0.0), axis=1
    )
    key = obs_layer * (rows * cells) + obs_index
    key, frac, weight = lax.sort((key, obs_frac, weight), num_keys=1, is_stable=False)
    key, frac, weight = (x.reshape(-1, cells) for x in (key, frac, weight))

    table_rows = nvars * plane + BLOCK
    own, held = call(own_kernel, dims, [whole, whole], [powers], [ens, stat], rates, copying)
    (seen,) = call(
        forward_kernel,
        dims,
        [key.shape],
        [own, scale, side_a, side_b, key, frac],
        [perturb],
        [key] + rates,
        [
            pltpu.VMEM(whole, jnp.float32),
            pltpu.VMEM((table_rows, 2 * cells), jnp.bfloat16),
            pltpu.VMEM(perturb.shape, perturb.dtype),
            pltpu.SemaphoreType.DMA(()),
        ],
    )
    seen = summed(seen)
    source, side_a, side_b, gradient = call(
        scatter_kernel,
        dims,
        [(members, plane, cells), strip, strip, (table_rows, cells)],
        [seen, key, frac, weight, perturb, scale],
        [],
        [key],
        [pltpu.VMEM(key.shape, jnp.float32)],
    )
    side_a, side_b = exchange(side_a, side_b)
    (own,) = call(local_kernel, dims, [whole], [powers, source, gradient, scale, held], [], rates)
    hv_ens, hv_stat = call(
        edge_kernel,
        dims,
        [(members, plane, cells), (nvars, plane, cells)],
        [own, side_a, side_b],
        [],
        rates,
        [pltpu.VMEM(whole, jnp.float32), pltpu.SemaphoreType.DMA((fields,))],
        HBM,
    )
    return hv_ens.reshape(ens_control.shape), hv_stat.reshape(static_control.shape)


def solution(mesh):
    placed = (
        P("grp", None, "tile", None),
        P("grp", None, None, "tile", None),
        P("grp", None, None, "tile", None),
        P("grp"),
        P(),
        P("grp"),
        P("grp", None, None),
        P("tile"),
        P("tile"),
        P("tile"),
        P("tile"),
        P(),
    )
    return jax.shard_map(
        per_device,
        mesh=mesh,
        in_specs=placed,
        out_specs=(P("grp", None, "tile", None), P("grp", None, None, "tile", None)),
        check_vma=False,
    )
```

```python
import math

import jax
import jax.numpy as jnp
import numpy as np
from jax import lax
from jax.experimental import pallas as pl
from jax.experimental.pallas import tpu as pltpu
from jax.sharding import PartitionSpec as P

SWEEPS = 4
BLOCK = 256
ALIGN = 16


def along_x(planes, wanted, rows, rate, inside):
    factors = [(1.0 - 4.0 * rate, rate)] + [((1.0 - 4.0 * rate) * side, rate * side) for side in inside]
    result = {}
    for x in wanted:
        keep, share = factors[1 if x < 0 else 2 if x >= rows else 0]
        total = None
        for near in (x - 1, x + 1):
            if near in planes:
                total = planes[near] if total is None else total + planes[near]
        if total is not None:
            total = share * total
        if x in planes:
            total = keep * planes[x] if total is None else keep * planes[x] + total
        if total is not None:
            result[x] = total
    return result


def powers_along_x(planes, first, last, rows, rate, inside):
    stages = [planes]
    for left in range(SWEEPS - 1, -1, -1):
        stages.append(along_x(stages[-1], range(first - left, last + left + 1), rows, rate, inside))
    return stages


def binomial(j, rate):
    factor = float(math.comb(SWEEPS, j))
    for number in range(j):
        factor = factor * rate
    return factor


def along_y(value):
    cells = value.shape[1]
    lane = lax.broadcasted_iota(jnp.int32, value.shape, 1)
    below = jnp.where(lane == 0, 0.0, pltpu.roll(value, 1, 1))
    return below + jnp.where(lane == cells - 1, 0.0, pltpu.roll(value, cells - 1, 1))


def spread_rolled(planes, first, last, rows, rate, inside):
    stages = powers_along_x(planes, first, last, rows, rate, inside)
    result = {}
    for x in range(first, last + 1):
        total = None
        for j in range(SWEEPS, -1, -1):
            if total is not None:
                total = along_y(total)
            term = stages[SWEEPS - j].get(x)
            if term is not None:
                term = term if j == 0 else binomial(j, rate) * term
                total = term if total is None else total + term
        result[x] = total
    return result


def halves(value):
    high = value.astype(jnp.bfloat16)
    low = (value - high.astype(jnp.float32)).astype(jnp.bfloat16)
    return high, low


def y_powers(cells):
    once = np.eye(cells, k=1) + np.eye(cells, k=-1)
    row = np.concatenate([np.linalg.matrix_power(once, j) for j in range(1, SWEEPS + 1)], axis=1)
    return jnp.asarray(np.concatenate([row, row], axis=0), jnp.bfloat16)


GROUP = 8


def spread_product(planes, rows, rate, inside, powers):
    levels, cells = planes[0].shape
    terms = [{} for j in range(SWEEPS)]
    for first in range(0, rows, GROUP):
        both = jnp.concatenate(halves(jnp.concatenate([planes[x] for x in range(first, first + GROUP)], axis=0)), axis=1)
        product = jnp.dot(both, powers[...], preferred_element_type=jnp.float32)
        for at in range(GROUP):
            for j in range(SWEEPS):
                terms[j][first + at] = product[at * levels : (at + 1) * levels, j * cells : (j + 1) * cells]
    result = planes
    for j in range(1, SWEEPS + 1):
        left = SWEEPS - j
        result = along_x(result, range(-left, rows + left), rows, rate, inside)
        factor = binomial(j, rate)
        for x in range(rows):
            result[x] = result[x] + factor * terms[j - 1][x]
    return result


def rate_of(field, members, group, localize, static):
    member = jnp.minimum(field, members - 1)
    return jnp.where(field < members, localize[group[member]], static[0])


def neighbours():
    tile = lax.axis_index("tile")
    last = lax.axis_size("tile") - 1
    return jnp.where(tile > 0, 1.0, 0.0), jnp.where(tile < last, 1.0, 0.0)


def is_even():
    return lax.axis_index("tile") % 2 == 0


def begins(rows):
    even = is_even()
    return jnp.where(even, rows - SWEEPS, 0), jnp.where(even, 0, rows - SWEEPS)


def sides_of(side_a, side_b, field, levels):
    even = is_even()
    below, above = neighbours()
    lower, upper = [], []
    for j in range(SWEEPS):
        a = side_a[field, pl.ds(j * levels, levels), :]
        b = side_b[field, pl.ds(j * levels, levels), :] * (below * above)
        lower.append(jnp.where(even, b, a))
        upper.append(jnp.where(even, a, b))
    return lower, upper


def block_of(ref, block):
    lanes = ref.shape[1]
    parts = BLOCK // lanes
    return jnp.concatenate([ref[pl.ds(block * parts + part, 1), :] for part in range(parts)], axis=1)


def weights_of(key, frac, cells):
    cell = key & (cells - 1)
    second = (cell + 1) & (cells - 1)
    spot = lax.broadcasted_iota(jnp.int32, (cells, key.shape[1]), 0)
    return jnp.where(spot == cell, 1.0 - frac, jnp.where(spot == second, frac, 0.0))


def chosen_rows(key, start, shift):
    row = (key >> shift) - start
    spot = lax.broadcasted_iota(jnp.int32, (BLOCK, key.shape[1]), 0)
    return jnp.where(spot == row, 1.0, 0.0).astype(jnp.bfloat16)


def window_of(bound, block, cells):
    parts = BLOCK // bound.shape[1]
    shift = cells.bit_length() - 1
    start = ((bound[block * parts, 0] >> shift) // ALIGN) * ALIGN
    last = bound[block * parts + parts - 1, bound.shape[1] - 1] >> shift
    return start, (last - start) // BLOCK + 1


def every_window(bound, blocks, cells, visit, visit_again):
    most = 1
    for block in range(blocks):
        start, count = window_of(bound, block, cells)
        most = jnp.maximum(most, count)
        visit(block, start)

    @pl.when(most > 1)
    def _():
        def of_block(block, carry):
            start, count = window_of(bound, block, cells)

            def of_window(window, inner):
                visit_again(block, start + window * BLOCK)
                return inner

            return lax.fori_loop(1, count, of_window, carry)

        lax.fori_loop(0, blocks, of_block, 0)


def each_field(fields, visit):
    def step(field, carry):
        visit(field)
        return carry

    lax.fori_loop(0, fields, step, 0)


def load_of(field, source, at, held, sems):
    return pltpu.make_async_copy(source.at[at], held.at[field], sems.at[field])


def start_loads(members, nvars, ens, stat, held, sems):
    for m in range(members):
        load_of(m, ens, m, held, sems).start()
    for v in range(nvars):
        load_of(members + v, stat, v, held, sems).start()


def pack_kernel(dims, ens, stat, side_a, side_b, held, sems):
    members, nvars, levels, rows, cells, blocks = dims
    start_loads(members, nvars, ens, stat, held, sems)
    for field in range(members + nvars):
        load_of(field, ens, 0, held, sems).wait()
        for begin, side in zip(begins(rows), (side_a, side_b)):
            for j in range(SWEEPS):
                side[field, pl.ds(j * levels, levels), :] = held[field, pl.ds(begin + j, levels, stride=rows), :]


def own_kernel(dims, powers, ens, stat, group, localize, static, out, held, sems):
    members, nvars, levels, rows, cells, blocks = dims
    inside = neighbours()
    start_loads(members, nvars, ens, stat, held, sems)

    def of_field(field):
        load_of(field, ens, 0, held, sems).wait()
        planes = {x: held[field, pl.ds(x, levels, stride=rows), :] for x in range(rows)}
        rate = rate_of(field, members, group, localize, static)
        planes = spread_product(planes, rows, rate, inside, powers)
        for x in range(rows):
            out[field, pl.ds(x * levels, levels), :] = planes[x]

    each_field(members + nvars, of_field)


def with_sides(dims, own, side_a, side_b, field, rate):
    members, nvars, levels, rows, cells, blocks = dims
    lower, upper = sides_of(side_a, side_b, field, levels)
    lower = spread_rolled({j - SWEEPS: lower[j] for j in range(SWEEPS)}, 0, SWEEPS - 1, rows, rate, (1.0, 1.0))
    upper = spread_rolled({rows + j: upper[j] for j in range(SWEEPS)}, rows - SWEEPS, rows - 1, rows, rate, (1.0, 1.0))
    planes = {}
    for x in range(rows):
        planes[x] = own[field, pl.ds(x * levels, levels), :]
        for extra in (lower, upper):
            if x in extra:
                planes[x] = planes[x] + extra[x]
    return planes


def forward_kernel(dims, own, scale, side_a, side_b, key, frac, perturb_far, bound, group, localize, static, out, smooth, table, perturb, sem):
    members, nvars, levels, rows, cells, blocks = dims
    shift = cells.bit_length() - 1
    load = pltpu.make_async_copy(perturb_far, perturb, sem)
    load.start()

    def of_field(field):
        rate = rate_of(field, members, group, localize, static)
        planes = with_sides(dims, own, side_a, side_b, field, rate)
        for x in range(rows):
            smooth[field, pl.ds(x, levels, stride=rows), :] = planes[x] * scale[field]

    each_field(members + nvars, of_field)
    load.wait()
    plane = levels * rows
    for v in range(nvars):
        total = smooth[members + v]
        for m in range(members):
            total = total + perturb[m, v].astype(jnp.float32) * smooth[m]
        high, low = halves(total)
        table[v * plane : (v + 1) * plane, :cells] = high
        table[v * plane : (v + 1) * plane, cells:] = low
    table[nvars * plane :, :] = jnp.zeros((BLOCK, 2 * cells), jnp.bfloat16)
    lanes = key.shape[1]
    parts = BLOCK // lanes

    def seen_in(block, start):
        keys = block_of(key, block)
        picked = lax.dot_general(
            table[pl.ds(pl.multiple_of(start, ALIGN), BLOCK), :],
            chosen_rows(keys, start, shift),
            (((0,), (0,)), ((), ())),
            preferred_element_type=jnp.float32,
        )
        picked = picked[:cells] + picked[cells:]
        return jnp.sum(picked * weights_of(keys, block_of(frac, block), cells), axis=0, keepdims=True)

    def visit(block, start):
        seen = seen_in(block, start)
        for part in range(parts):
            out[pl.ds(block * parts + part, 1), :] = seen[:, part * lanes : (part + 1) * lanes]

    def visit_again(block, start):
        seen = seen_in(block, start)
        for part in range(parts):
            at = pl.ds(block * parts + part, 1)
            out[at, :] = out[at, :] + seen[:, part * lanes : (part + 1) * lanes]

    every_window(bound, blocks, cells, visit, visit_again)


def scatter_kernel(dims, seen, others, key, frac, weight, perturb, scale, bound, source, side_a, side_b, gradient, valued):
    members, nvars, levels, rows, cells, blocks = dims
    shift = cells.bit_length() - 1
    valued[...] = (seen[...] + others[...]) * weight[...]
    gradient[...] = jnp.zeros(gradient.shape, jnp.float32)

    def add_block(block, start):
        keys = block_of(key, block)
        placed = weights_of(keys, block_of(frac, block), cells) * block_of(valued, block)
        high, low = halves(placed)
        both = lax.dot_general(
            chosen_rows(keys, start, shift),
            jnp.concatenate([high, low], axis=0),
            (((1,), (1,)), ((), ())),
            preferred_element_type=jnp.float32,
        )
        at = pl.ds(pl.multiple_of(start, ALIGN), BLOCK)
        gradient[at, :] = gradient[at, :] + (both[:, :cells] + both[:, cells:])

    every_window(bound, blocks, cells, add_block, add_block)

    plane = levels * rows
    for m in range(members):
        total = perturb[m, 0].astype(jnp.float32) * gradient[:plane, :]
        for v in range(1, nvars):
            total = total + perturb[m, v].astype(jnp.float32) * gradient[v * plane : (v + 1) * plane, :]
        source[m] = total
    for begin, side in zip(begins(rows), (side_a, side_b)):
        for field in range(members + nvars):
            for j in range(SWEEPS):
                if field < members:
                    strip = source[field, pl.ds(begin + j, levels, stride=rows), :]
                else:
                    at = (field - members) * plane + begin + j
                    strip = gradient[pl.ds(at, levels, stride=rows), :] * scale[field]
                side[field, pl.ds(j * levels, levels), :] = strip


def local_kernel(dims, powers, source, gradient, scale, held, group, localize, static, out):
    members, nvars, levels, rows, cells, blocks = dims
    inside = neighbours()
    plane = levels * rows

    def of_field(field, planes):
        rate = rate_of(field, members, group, localize, static)
        planes = spread_product(planes, rows, rate, inside, powers)
        for x in range(rows):
            out[field, pl.ds(x * levels, levels), :] = held[field, pl.ds(x, levels, stride=rows), :] + planes[x]

    def of_member(m):
        of_field(m, {x: source[m, pl.ds(x, levels, stride=rows), :] for x in range(rows)})

    def of_group(v):
        field = members + v
        planes = {x: gradient[pl.ds(v * plane + x, levels, stride=rows), :] * scale[field] for x in range(rows)}
        of_field(field, planes)

    each_field(members, of_member)
    each_field(nvars, of_group)


def edge_kernel(dims, own, side_a, side_b, group, localize, static, hv_ens, hv_stat, after, sems):
    members, nvars, levels, rows, cells, blocks = dims

    def write_of(field, out, at):
        return pltpu.make_async_copy(after.at[field], out.at[at], sems.at[field])

    def of_field(field, out, at):
        rate = rate_of(field, members, group, localize, static)
        planes = with_sides(dims, own, side_a, side_b, field, rate)
        for x in range(rows):
            after[field, pl.ds(x, levels, stride=rows), :] = planes[x]
        write_of(field, out, at).start()

    each_field(members, lambda m: of_field(m, hv_ens, m))
    each_field(nvars, lambda v: of_field(members + v, hv_stat, v))
    each_field(members, lambda m: write_of(m, hv_ens, m).wait())
    each_field(nvars, lambda v: write_of(members + v, hv_stat, v).wait())


def exchange(side_a, side_b):
    count = lax.axis_size("tile")
    pairs_a = [(i, i ^ 1) for i in range(count)]
    pairs_b = [(i, (((i + 1) ^ 1) - 1) % count) for i in range(count)]
    return lax.ppermute(side_a, "tile", pairs_a), lax.ppermute(side_b, "tile", pairs_b)


def halved_sums(value):
    count = lax.axis_size("grp")
    others = None
    for turn in (2, 6, 1) if count == 8 else [1 << bit for bit in range(count.bit_length() - 1)]:
        if others is not None:
            value = value + others
        others = lax.ppermute(value, "grp", [(i, i ^ turn) for i in range(count)])
    return value, others


VMEM = pl.BlockSpec(memory_space=pltpu.VMEM)
SMEM = pl.BlockSpec(memory_space=pltpu.SMEM)
HBM = pl.BlockSpec(memory_space=pltpu.HBM)


def call(kernel, dims, outs, ins, far=(), scalars=(), scratch=(), out_spec=VMEM, cost=2_000_000):
    def body(*refs):
        kernel(dims, *refs)

    far = [pltpu.with_memory_space_constraint(x, pltpu.HBM) for x in far]
    return pl.pallas_call(
        body,
        out_shape=tuple(jax.ShapeDtypeStruct(shape, jnp.float32) for shape in outs),
        in_specs=[VMEM] * len(ins) + [HBM] * len(far) + [SMEM] * len(scalars),
        out_specs=tuple([out_spec] * len(outs)),
        scratch_shapes=list(scratch),
        compiler_params=pltpu.CompilerParams(vmem_limit_bytes=16 * 1024 * 1024),
        cost_estimate=pl.CostEstimate(flops=cost * 10, bytes_accessed=cost, transcendentals=0),
        name=kernel.__name__,
    )(*ins, *far, *scalars)


def per_device(
    ens_control,
    static_control,
    member_perturb,
    member_group,
    localize_rate,
    static_rate,
    static_scale,
    obs_index,
    obs_frac,
    obs_layer,
    obs_kind,
    obs_precision,
):
    members, levels, rows, cells = ens_control.shape
    nvars = static_control.shape[1]
    fields = members + nvars
    blocks = obs_index.shape[0] // BLOCK
    dims = (members, nvars, levels, rows, cells, blocks)
    plane = levels * rows
    strip = (fields, SWEEPS * levels, cells)

    ens = ens_control.reshape(members, plane, cells)
    stat = static_control.reshape(nvars, plane, cells)
    perturb = member_perturb.reshape(members, nvars, plane, cells)
    rates = [member_group, localize_rate, static_rate]

    whole = (fields, plane, cells)
    powers = y_powers(cells)
    copying = [pltpu.SemaphoreType.DMA((fields,))]
    side_a, side_b = call(pack_kernel, dims, [strip, strip], [], [ens, stat], [], [pltpu.VMEM(whole, jnp.float32)] + copying)
    side_a, side_b = exchange(side_a, side_b)

    scale = jnp.concatenate([jnp.ones((members, levels), jnp.float32), static_scale[0]])
    scale = jnp.broadcast_to(scale[:, :, None], (fields, levels, cells))
    kind_ids = jnp.arange(obs_precision.shape[0], dtype=jnp.int32)
    weight = jnp.sum(
        jnp.where(obs_kind[:, None] == kind_ids[None, :], obs_precision[None, :], 0.0), axis=1
    )
    key = obs_layer * (rows * cells) + obs_index
    key, frac, weight = lax.sort((key, obs_frac, weight), num_keys=1, is_stable=False)
    key, frac, weight = (x.reshape(-1, cells) for x in (key, frac, weight))

    table_rows = nvars * plane + BLOCK
    own, held = call(own_kernel, dims, [whole, whole], [powers], [ens, stat], rates, copying)
    (seen,) = call(
        forward_kernel,
        dims,
        [key.shape],
        [own, scale, side_a, side_b, key, frac],
        [perturb],
        [key] + rates,
        [
            pltpu.VMEM(whole, jnp.float32),
            pltpu.VMEM((table_rows, 2 * cells), jnp.bfloat16),
            pltpu.VMEM(perturb.shape, perturb.dtype),
            pltpu.SemaphoreType.DMA(()),
        ],
    )
    seen, others = halved_sums(seen)
    source, side_a, side_b, gradient = call(
        scatter_kernel,
        dims,
        [(members, plane, cells), strip, strip, (table_rows, cells)],
        [seen, others, key, frac, weight, perturb, scale],
        [],
        [key],
        [pltpu.VMEM(key.shape, jnp.float32)],
    )
    side_a, side_b = exchange(side_a, side_b)
    (own,) = call(local_kernel, dims, [whole], [powers, source, gradient, scale, held], [], rates)
    hv_ens, hv_stat = call(
        edge_kernel,
        dims,
        [(members, plane, cells), (nvars, plane, cells)],
        [own, side_a, side_b],
        [],
        rates,
        [pltpu.VMEM(whole, jnp.float32), pltpu.SemaphoreType.DMA((fields,))],
        HBM,
    )
    return hv_ens.reshape(ens_control.shape), hv_stat.reshape(static_control.shape)


def solution(mesh):
    placed = (
        P("grp", None, "tile", None),
        P("grp", None, None, "tile", None),
        P("grp", None, None, "tile", None),
        P("grp"),
        P(),
        P("grp"),
        P("grp", None, None),
        P("tile"),
        P("tile"),
        P("tile"),
        P("tile"),
        P(),
    )
    return jax.shard_map(
        per_device,
        mesh=mesh,
        in_specs=placed,
        out_specs=(P("grp", None, "tile", None), P("grp", None, None, "tile", None)),
        check_vma=False,
    )
```

```python
import math

import jax
import jax.numpy as jnp
import numpy as np
from jax import lax
from jax.experimental import pallas as pl
from jax.experimental.pallas import tpu as pltpu
from jax.sharding import PartitionSpec as P

SWEEPS = 4
BLOCK = 256
ALIGN = 16


def along_x(planes, wanted, rows, rate, inside):
    factors = [(1.0 - 4.0 * rate, rate)] + [((1.0 - 4.0 * rate) * side, rate * side) for side in inside]
    result = {}
    for x in wanted:
        keep, share = factors[1 if x < 0 else 2 if x >= rows else 0]
        total = None
        for near in (x - 1, x + 1):
            if near in planes:
                total = planes[near] if total is None else total + planes[near]
        if total is not None:
            total = share * total
        if x in planes:
            total = keep * planes[x] if total is None else keep * planes[x] + total
        if total is not None:
            result[x] = total
    return result


def powers_along_x(planes, first, last, rows, rate, inside):
    stages = [planes]
    for left in range(SWEEPS - 1, -1, -1):
        stages.append(along_x(stages[-1], range(first - left, last + left + 1), rows, rate, inside))
    return stages


def binomial(j, rate):
    factor = float(math.comb(SWEEPS, j))
    for number in range(j):
        factor = factor * rate
    return factor


def along_y(value):
    cells = value.shape[1]
    lane = lax.broadcasted_iota(jnp.int32, value.shape, 1)
    below = jnp.where(lane == 0, 0.0, pltpu.roll(value, 1, 1))
    return below + jnp.where(lane == cells - 1, 0.0, pltpu.roll(value, cells - 1, 1))


def spread_rolled(planes, first, last, rows, rate, inside):
    stages = powers_along_x(planes, first, last, rows, rate, inside)
    result = {}
    for x in range(first, last + 1):
        total = None
        for j in range(SWEEPS, -1, -1):
            if total is not None:
                total = along_y(total)
            term = stages[SWEEPS - j].get(x)
            if term is not None:
                term = term if j == 0 else binomial(j, rate) * term
                total = term if total is None else total + term
        result[x] = total
    return result


def halves(value):
    high = value.astype(jnp.bfloat16)
    low = (value - high.astype(jnp.float32)).astype(jnp.bfloat16)
    return high, low


def y_powers(cells):
    once = np.eye(cells, k=1) + np.eye(cells, k=-1)
    row = np.concatenate([np.linalg.matrix_power(once, j) for j in range(1, SWEEPS + 1)], axis=1)
    return jnp.asarray(np.concatenate([row, row], axis=0), jnp.bfloat16)


GROUP = 8


def spread_product(planes, rows, rate, inside, powers):
    levels, cells = planes[0].shape
    terms = [{} for j in range(SWEEPS)]
    for first in range(0, rows, GROUP):
        both = jnp.concatenate(halves(jnp.concatenate([planes[x] for x in range(first, first + GROUP)], axis=0)), axis=1)
        product = jnp.dot(both, powers[...], preferred_element_type=jnp.float32)
        for at in range(GROUP):
            for j in range(SWEEPS):
                terms[j][first + at] = product[at * levels : (at + 1) * levels, j * cells : (j + 1) * cells]
    result = planes
    for j in range(1, SWEEPS + 1):
        left = SWEEPS - j
        result = along_x(result, range(-left, rows + left), rows, rate, inside)
        factor = binomial(j, rate)
        for x in range(rows):
            result[x] = result[x] + factor * terms[j - 1][x]
    return result


def rate_of(field, members, group, localize, static):
    member = jnp.minimum(field, members - 1)
    return jnp.where(field < members, localize[group[member]], static[0])


def neighbours():
    tile = lax.axis_index("tile")
    last = lax.axis_size("tile") - 1
    return jnp.where(tile > 0, 1.0, 0.0), jnp.where(tile < last, 1.0, 0.0)


def is_even():
    return lax.axis_index("tile") % 2 == 0


def begins(rows):
    even = is_even()
    return jnp.where(even, rows - SWEEPS, 0), jnp.where(even, 0, rows - SWEEPS)


def part_of_side(side, field, rate, levels, rows, upper, counts):
    planes = {}
    for away in range(1, SWEEPS + 1):
        j = jnp.where(upper, away - 1, SWEEPS - away)
        planes[-away] = side[field, pl.ds(pl.multiple_of(j * levels, levels), levels), :]
    parts = spread_rolled(planes, 0, SWEEPS - 1, rows, rate, (1.0, 1.0))
    return [part if counts is None else part * counts for part in (parts[depth] for depth in range(SWEEPS))]


def add_near(into, field, side, rate, levels, rows, scale=None):
    upper = is_even()
    for depth, part in enumerate(part_of_side(side, field, rate, levels, rows, upper, None)):
        if scale is not None:
            part = part * scale[field]
        at = pl.ds(jnp.where(upper, rows - 1 - depth, depth), levels, stride=rows)
        into[field, at, :] = into[field, at, :] + part


def add_far(into, field, side, rate, levels, rows, scale=None):
    upper = jnp.logical_not(is_even())
    below, above = neighbours()
    for depth, part in enumerate(part_of_side(side, field, rate, levels, rows, upper, below * above)):
        if scale is not None:
            part = part * scale[field]
        at = pl.ds(jnp.where(upper, rows - 1 - depth, depth), levels, stride=rows)
        into[field, at, :] = into[field, at, :] + part


def block_of(ref, block):
    lanes = ref.shape[1]
    parts = BLOCK // lanes
    return jnp.concatenate([ref[pl.ds(block * parts + part, 1), :] for part in range(parts)], axis=1)


def weights_of(key, frac, cells):
    cell = key & (cells - 1)
    second = (cell + 1) & (cells - 1)
    spot = lax.broadcasted_iota(jnp.int32, (cells, key.shape[1]), 0)
    return jnp.where(spot == cell, 1.0 - frac, jnp.where(spot == second, frac, 0.0))


def chosen_rows(key, start, shift):
    row = (key >> shift) - start
    spot = lax.broadcasted_iota(jnp.int32, (BLOCK, key.shape[1]), 0)
    return jnp.where(spot == row, 1.0, 0.0).astype(jnp.bfloat16)


def window_of(bound, block, cells):
    parts = BLOCK // bound.shape[1]
    shift = cells.bit_length() - 1
    start = ((bound[block * parts, 0] >> shift) // ALIGN) * ALIGN
    last = bound[block * parts + parts - 1, bound.shape[1] - 1] >> shift
    return start, (last - start) // BLOCK + 1


def every_window(bound, blocks, cells, visit, visit_again):
    most = 1
    for block in range(blocks):
        start, count = window_of(bound, block, cells)
        most = jnp.maximum(most, count)
        visit(block, start)

    @pl.when(most > 1)
    def _():
        def of_block(block, carry):
            start, count = window_of(bound, block, cells)

            def of_window(window, inner):
                visit_again(block, start + window * BLOCK)
                return inner

            return lax.fori_loop(1, count, of_window, carry)

        lax.fori_loop(0, blocks, of_block, 0)


def each_field(fields, visit):
    def step(field, carry):
        visit(field)
        return carry

    lax.fori_loop(0, fields, step, 0)


def load_of(field, source, at, held, sems):
    return pltpu.make_async_copy(source.at[at], held.at[field], sems.at[field])


def start_loads(members, nvars, ens, stat, held, sems):
    for m in range(members):
        load_of(m, ens, m, held, sems).start()
    for v in range(nvars):
        load_of(members + v, stat, v, held, sems).start()


def pack_kernel(dims, ens, stat, side_a, side_b, held, sems):
    members, nvars, levels, rows, cells, blocks = dims
    start_loads(members, nvars, ens, stat, held, sems)
    for field in range(members + nvars):
        load_of(field, ens, 0, held, sems).wait()
        for begin, side in zip(begins(rows), (side_a, side_b)):
            for j in range(SWEEPS):
                side[field, pl.ds(j * levels, levels), :] = held[field, pl.ds(begin + j, levels, stride=rows), :]


def own_kernel(dims, powers, held, scale, side_a, layer, index, kind, group, localize, static, precision, out, key, weight):
    members, nvars, levels, rows, cells, blocks = dims
    inside = neighbours()

    def of_field(field):
        planes = {x: held[field, pl.ds(x, levels, stride=rows), :] for x in range(rows)}
        rate = rate_of(field, members, group, localize, static)
        planes = spread_product(planes, rows, rate, inside, powers)
        for x in range(rows):
            out[field, pl.ds(x, levels, stride=rows), :] = planes[x] * scale[field]
        add_near(out, field, side_a, rate, levels, rows, scale)

    each_field(members + nvars, of_field)
    key[...] = layer[...] * (rows * cells) + index[...]
    total = jnp.zeros(kind.shape, jnp.float32)
    for k in range(precision.shape[0]):
        total = jnp.where(kind[...] == k, precision[k], total)
    weight[...] = total


def forward_kernel(dims, own, scale, side_b, key, frac, perturb_far, bound, group, localize, static, out, smooth, table, perturb, sem):
    members, nvars, levels, rows, cells, blocks = dims
    shift = cells.bit_length() - 1
    load = pltpu.make_async_copy(perturb_far, perturb, sem)
    load.start()

    def of_field(field):
        rate = rate_of(field, members, group, localize, static)
        smooth[field] = own[field]
        add_far(smooth, field, side_b, rate, levels, rows, scale)

    each_field(members + nvars, of_field)
    load.wait()
    plane = levels * rows
    for v in range(nvars):
        total = smooth[members + v]
        for m in range(members):
            total = total + perturb[m, v].astype(jnp.float32) * smooth[m]
        high, low = halves(total)
        table[v * plane : (v + 1) * plane, :cells] = high
        table[v * plane : (v + 1) * plane, cells:] = low
    table[nvars * plane :, :] = jnp.zeros((BLOCK, 2 * cells), jnp.bfloat16)
    lanes = key.shape[1]
    parts = BLOCK // lanes

    def seen_in(block, start):
        keys = block_of(key, block)
        picked = lax.dot_general(
            table[pl.ds(pl.multiple_of(start, ALIGN), BLOCK), :],
            chosen_rows(keys, start, shift),
            (((0,), (0,)), ((), ())),
            preferred_element_type=jnp.float32,
        )
        picked = picked[:cells] + picked[cells:]
        return jnp.sum(picked * weights_of(keys, block_of(frac, block), cells), axis=0, keepdims=True)

    def visit(block, start):
        seen = seen_in(block, start)
        for part in range(parts):
            out[pl.ds(block * parts + part, 1), :] = seen[:, part * lanes : (part + 1) * lanes]

    def visit_again(block, start):
        seen = seen_in(block, start)
        for part in range(parts):
            at = pl.ds(block * parts + part, 1)
            out[at, :] = out[at, :] + seen[:, part * lanes : (part + 1) * lanes]

    every_window(bound, blocks, cells, visit, visit_again)


def scatter_kernel(dims, key, frac, weight, perturb, scale, *refs):
    members, nvars, levels, rows, cells, blocks = dims
    *seen, bound, source, side_a, side_b, gradient, valued = refs
    shift = cells.bit_length() - 1
    total = seen[0][...]
    for part in seen[1:]:
        total = total + part[...]
    valued[...] = total * weight[...]
    gradient[...] = jnp.zeros(gradient.shape, jnp.float32)

    def add_block(block, start):
        keys = block_of(key, block)
        placed = weights_of(keys, block_of(frac, block), cells) * block_of(valued, block)
        high, low = halves(placed)
        both = lax.dot_general(
            chosen_rows(keys, start, shift),
            jnp.concatenate([high, low], axis=0),
            (((1,), (1,)), ((), ())),
            preferred_element_type=jnp.float32,
        )
        at = pl.ds(pl.multiple_of(start, ALIGN), BLOCK)
        gradient[at, :] = gradient[at, :] + (both[:, :cells] + both[:, cells:])

    every_window(bound, blocks, cells, add_block, add_block)

    plane = levels * rows
    for m in range(members):
        total = perturb[m, 0].astype(jnp.float32) * gradient[:plane, :]
        for v in range(1, nvars):
            total = total + perturb[m, v].astype(jnp.float32) * gradient[v * plane : (v + 1) * plane, :]
        source[m] = total
    for begin, side in zip(begins(rows), (side_a, side_b)):
        for field in range(members + nvars):
            for j in range(SWEEPS):
                if field < members:
                    strip = source[field, pl.ds(begin + j, levels, stride=rows), :]
                else:
                    at = (field - members) * plane + begin + j
                    strip = gradient[pl.ds(at, levels, stride=rows), :] * scale[field]
                side[field, pl.ds(j * levels, levels), :] = strip


def local_kernel(dims, powers, source, gradient, scale, side_a, ens, stat, group, localize, static, out, held, sems):
    members, nvars, levels, rows, cells, blocks = dims
    inside = neighbours()
    plane = levels * rows
    start_loads(members, nvars, ens, stat, held, sems)

    def of_field(field, planes):
        rate = rate_of(field, members, group, localize, static)
        planes = spread_product(planes, rows, rate, inside, powers)
        load_of(field, ens, 0, held, sems).wait()
        for x in range(rows):
            at = pl.ds(x, levels, stride=rows)
            out[field, at, :] = held[field, at, :] + planes[x]
        add_near(out, field, side_a, rate, levels, rows)

    def of_member(m):
        of_field(m, {x: source[m, pl.ds(x, levels, stride=rows), :] for x in range(rows)})

    def of_group(v):
        field = members + v
        planes = {x: gradient[pl.ds(v * plane + x, levels, stride=rows), :] * scale[field] for x in range(rows)}
        of_field(field, planes)

    each_field(members, of_member)
    each_field(nvars, of_group)


def edge_kernel(dims, own, side_b, group, localize, static, hv_ens, hv_stat, after, sems):
    members, nvars, levels, rows, cells, blocks = dims

    def write_of(field, out, at):
        return pltpu.make_async_copy(after.at[field], out.at[at], sems.at[field])

    def of_field(field, out, at):
        rate = rate_of(field, members, group, localize, static)
        after[field] = own[field]
        add_far(after, field, side_b, rate, levels, rows)
        write_of(field, out, at).start()

    each_field(members, lambda m: of_field(m, hv_ens, m))
    each_field(nvars, lambda v: of_field(members + v, hv_stat, v))
    each_field(members, lambda m: write_of(m, hv_ens, m).wait())
    each_field(nvars, lambda v: write_of(members + v, hv_stat, v).wait())


def exchange(side_a, side_b):
    count = lax.axis_size("tile")
    pairs_a = [(i, i ^ 1) for i in range(count)]
    pairs_b = [(i, (((i + 1) ^ 1) - 1) % count) for i in range(count)]
    return lax.ppermute(side_a, "tile", pairs_a), lax.ppermute(side_b, "tile", pairs_b)


def summands(value):
    count = lax.axis_size("grp")
    value = value + lax.ppermute(value, "grp", [(i, i ^ 1) for i in range(count)])
    turns = [2, 6, 4] if count == 8 else list(range(2, count, 2))
    return [value] + [lax.ppermute(value, "grp", [(i, i ^ turn) for i in range(count)]) for turn in turns]


VMEM = pl.BlockSpec(memory_space=pltpu.VMEM)
SMEM = pl.BlockSpec(memory_space=pltpu.SMEM)
HBM = pl.BlockSpec(memory_space=pltpu.HBM)


def call(kernel, dims, outs, ins, far=(), scalars=(), scratch=(), out_spec=VMEM, kinds=None, cost=2_000_000):
    def body(*refs):
        kernel(dims, *refs)

    far = [pltpu.with_memory_space_constraint(x, pltpu.HBM) for x in far]
    return pl.pallas_call(
        body,
        out_shape=tuple(jax.ShapeDtypeStruct(tuple(shape), kind) for shape, kind in zip(outs, kinds or [jnp.float32] * len(outs))),
        in_specs=[VMEM] * len(ins) + [HBM] * len(far) + [SMEM] * len(scalars),
        out_specs=tuple([out_spec] * len(outs)),
        scratch_shapes=list(scratch),
        compiler_params=pltpu.CompilerParams(vmem_limit_bytes=16 * 1024 * 1024),
        cost_estimate=pl.CostEstimate(flops=cost * 10, bytes_accessed=cost, transcendentals=0),
        name=kernel.__name__,
    )(*ins, *far, *scalars)


def per_device(
    ens_control,
    static_control,
    member_perturb,
    member_group,
    localize_rate,
    static_rate,
    static_scale,
    obs_index,
    obs_frac,
    obs_layer,
    obs_kind,
    obs_precision,
):
    members, levels, rows, cells = ens_control.shape
    nvars = static_control.shape[1]
    fields = members + nvars
    blocks = obs_index.shape[0] // BLOCK
    dims = (members, nvars, levels, rows, cells, blocks)
    plane = levels * rows
    strip = (fields, SWEEPS * levels, cells)

    ens = ens_control.reshape(members, plane, cells)
    stat = static_control.reshape(nvars, plane, cells)
    perturb = member_perturb.reshape(members, nvars, plane, cells)
    rates = [member_group, localize_rate, static_rate]

    whole = (fields, plane, cells)
    key_shape = (obs_index.shape[0] // cells, cells)
    powers = y_powers(cells)
    copying = [pltpu.SemaphoreType.DMA((fields,))]
    side_a, side_b, held = call(pack_kernel, dims, [strip, strip, whole], [], [ens, stat], [], copying)
    side_a, side_b = exchange(side_a, side_b)

    scale = jnp.concatenate([jnp.ones((members, levels), jnp.float32), static_scale[0]])
    scale = jnp.broadcast_to(scale[:, :, None], (fields, levels, cells))
    layer, index, kind = (x.reshape(-1, cells) for x in (obs_layer, obs_index, obs_kind))
    own, key, weight = call(
        own_kernel,
        dims,
        [whole, key_shape, key_shape],
        [powers, held, scale, side_a, layer, index, kind],
        [],
        rates + [obs_precision],
        kinds=[jnp.float32, jnp.int32, jnp.float32],
    )
    key, frac, weight = lax.sort((key.reshape(-1), obs_frac, weight.reshape(-1)), num_keys=1, is_stable=False)
    key, frac, weight = (x.reshape(key_shape) for x in (key, frac, weight))

    table_rows = nvars * plane + BLOCK
    (seen,) = call(
        forward_kernel,
        dims,
        [key.shape],
        [own, scale, side_b, key, frac],
        [perturb],
        [key] + rates,
        [
            pltpu.VMEM(whole, jnp.float32),
            pltpu.VMEM((table_rows, 2 * cells), jnp.bfloat16),
            pltpu.VMEM(perturb.shape, perturb.dtype),
            pltpu.SemaphoreType.DMA(()),
        ],
    )
    seen = summands(seen)
    source, side_a, side_b, gradient = call(
        scatter_kernel,
        dims,
        [(members, plane, cells), strip, strip, (table_rows, cells)],
        [key, frac, weight, perturb, scale] + seen,
        [],
        [key],
        [pltpu.VMEM(key.shape, jnp.float32)],
    )
    side_a, side_b = exchange(side_a, side_b)
    (own,) = call(local_kernel, dims, [whole], [powers, source, gradient, scale, side_a], [ens, stat], rates, [pltpu.VMEM(whole, jnp.float32)] + copying)
    hv_ens, hv_stat = call(
        edge_kernel,
        dims,
        [(members, plane, cells), (nvars, plane, cells)],
        [own, side_b],
        [],
        rates,
        [pltpu.VMEM(whole, jnp.float32), pltpu.SemaphoreType.DMA((fields,))],
        HBM,
    )
    return hv_ens.reshape(ens_control.shape), hv_stat.reshape(static_control.shape)


def solution(mesh):
    placed = (
        P("grp", None, "tile", None),
        P("grp", None, None, "tile", None),
        P("grp", None, None, "tile", None),
        P("grp"),
        P(),
        P("grp"),
        P("grp", None, None),
        P("tile"),
        P("tile"),
        P("tile"),
        P("tile"),
        P(),
    )
    return jax.shard_map(
        per_device,
        mesh=mesh,
        in_specs=placed,
        out_specs=(P("grp", None, "tile", None), P("grp", None, None, "tile", None)),
        check_vma=False,
    )
```

```python
import math

import jax
import jax.numpy as jnp
import numpy as np
from jax import lax
from jax.experimental import pallas as pl
from jax.experimental.pallas import tpu as pltpu
from jax.sharding import PartitionSpec as P

SWEEPS = 4
BLOCK = 256
ALIGN = 16


def along_x(planes, wanted, rows, rate, inside):
    factors = [(1.0 - 4.0 * rate, rate)] * 3
    if inside is not None:
        factors[1:] = [((1.0 - 4.0 * rate) * side, rate * side) for side in inside]
    result = {}
    for x in wanted:
        keep, share = factors[1 if x < 0 else 2 if x >= rows else 0]
        total = None
        for near in (x - 1, x + 1):
            if near in planes:
                total = planes[near] if total is None else total + planes[near]
        if total is not None:
            total = share * total
        if x in planes:
            total = keep * planes[x] if total is None else keep * planes[x] + total
        if total is not None:
            result[x] = total
    return result


def powers_along_x(planes, first, last, rows, rate, inside):
    stages = [planes]
    for left in range(SWEEPS - 1, -1, -1):
        stages.append(along_x(stages[-1], range(first - left, last + left + 1), rows, rate, inside))
    return stages


def binomial(j, rate):
    factor = float(math.comb(SWEEPS, j))
    for number in range(j):
        factor = factor * rate
    return factor


def along_y(value):
    cells = value.shape[1]
    lane = lax.broadcasted_iota(jnp.int32, value.shape, 1)
    below = jnp.where(lane == 0, 0.0, pltpu.roll(value, 1, 1))
    return below + jnp.where(lane == cells - 1, 0.0, pltpu.roll(value, cells - 1, 1))


def spread_rolled(planes, first, last, rows, rate, inside):
    stages = powers_along_x(planes, first, last, rows, rate, inside)
    result = {}
    for x in range(first, last + 1):
        total = None
        for j in range(SWEEPS, -1, -1):
            if total is not None:
                total = along_y(total)
            term = stages[SWEEPS - j].get(x)
            if term is not None:
                term = term if j == 0 else binomial(j, rate) * term
                total = term if total is None else total + term
        result[x] = total
    return result


def halves(value):
    high = value.astype(jnp.bfloat16)
    low = (value - high.astype(jnp.float32)).astype(jnp.bfloat16)
    return high, low


def y_powers(cells):
    once = np.eye(cells, k=1) + np.eye(cells, k=-1)
    row = np.concatenate([np.linalg.matrix_power(once, j) for j in range(1, SWEEPS + 1)], axis=1)
    return jnp.asarray(np.concatenate([row, row], axis=0), jnp.bfloat16)


GROUP = 8


def spread_product(planes, rows, rate, inside, powers):
    levels, cells = planes[0].shape
    terms = [{} for j in range(SWEEPS)]
    for first in range(0, rows, GROUP):
        both = jnp.concatenate(halves(jnp.concatenate([planes[x] for x in range(first, first + GROUP)], axis=0)), axis=1)
        product = jnp.dot(both, powers[...], preferred_element_type=jnp.float32)
        for at in range(GROUP):
            for j in range(SWEEPS):
                terms[j][first + at] = product[at * levels : (at + 1) * levels, j * cells : (j + 1) * cells]
    result = planes
    for j in range(1, SWEEPS + 1):
        left = SWEEPS - j
        result = along_x(result, range(-left, rows + left), rows, rate, inside)
        factor = binomial(j, rate)
        for x in range(rows):
            result[x] = result[x] + factor * terms[j - 1][x]
    return result


def rate_of(field, members, group, localize, static):
    member = jnp.minimum(field, members - 1)
    return jnp.where(field < members, localize[group[member]], static[0])


def rates_of(fields, members, group, localize, static):
    return [rate_of(field, members, group, localize, static) for field in range(fields)]


def neighbours():
    tile = lax.axis_index("tile")
    last = lax.axis_size("tile") - 1
    return jnp.where(tile > 0, 1.0, 0.0), jnp.where(tile < last, 1.0, 0.0)


def is_even():
    return lax.axis_index("tile") % 2 == 0


def begins(rows):
    even = is_even()
    return jnp.where(even, rows - SWEEPS, 0), jnp.where(even, 0, rows - SWEEPS)


BATCH = 4


def add_side(side, upper, rates, shape, visit, counts=None):
    levels, rows, cells = shape
    for first in range(0, len(rates), BATCH):
        fields = range(first, min(first + BATCH, len(rates)))
        rate = jnp.concatenate([jnp.full((levels, cells), rates[field], jnp.float32) for field in fields], axis=0)
        planes = {}
        for away in range(1, SWEEPS + 1):
            j = jnp.where(upper, away - 1, SWEEPS - away)
            planes[-away] = side[j, first * levels : (first + len(fields)) * levels, :]
        parts = spread_rolled(planes, 0, SWEEPS - 1, rows, rate, None)
        for at, field in enumerate(fields):
            for depth in range(SWEEPS):
                part = parts[depth][at * levels : (at + 1) * levels]
                visit(field, depth, part if counts is None else part * counts)


def adder(into, upper, shape, scale=None):
    levels, rows, cells = shape

    def visit(field, depth, part):
        at = pl.ds(jnp.where(upper, rows - 1 - depth, depth), levels, stride=rows)
        into[field, at, :] = into[field, at, :] + (part if scale is None else part * scale[field])

    return visit


def add_near(into, side, rates, shape, scale=None):
    upper = is_even()
    add_side(side, upper, rates, shape, adder(into, upper, shape, scale))


def add_far(into, side, rates, shape, scale=None):
    upper = jnp.logical_not(is_even())
    below, above = neighbours()
    add_side(side, upper, rates, shape, adder(into, upper, shape, scale), below * above)


def block_of(ref, block):
    lanes = ref.shape[1]
    parts = BLOCK // lanes
    return jnp.concatenate([ref[pl.ds(block * parts + part, 1), :] for part in range(parts)], axis=1)


def weights_of(key, frac, cells):
    cell = key & (cells - 1)
    second = (cell + 1) & (cells - 1)
    spot = lax.broadcasted_iota(jnp.int32, (cells, key.shape[1]), 0)
    return jnp.where(spot == cell, 1.0 - frac, jnp.where(spot == second, frac, 0.0))


def chosen_rows(key, start, shift):
    row = (key >> shift) - start
    spot = lax.broadcasted_iota(jnp.int32, (BLOCK, key.shape[1]), 0)
    return jnp.where(spot == row, 1.0, 0.0).astype(jnp.bfloat16)


def window_of(bound, block, cells):
    parts = BLOCK // bound.shape[1]
    shift = cells.bit_length() - 1
    start = ((bound[block * parts, 0] >> shift) // ALIGN) * ALIGN
    last = bound[block * parts + parts - 1, bound.shape[1] - 1] >> shift
    return start, (last - start) // BLOCK + 1


def every_window(bound, blocks, cells, visit, visit_again):
    most = 1
    for block in range(blocks):
        start, count = window_of(bound, block, cells)
        most = jnp.maximum(most, count)
        visit(block, start)

    @pl.when(most > 1)
    def _():
        def of_block(block, carry):
            start, count = window_of(bound, block, cells)

            def of_window(window, inner):
                visit_again(block, start + window * BLOCK)
                return inner

            return lax.fori_loop(1, count, of_window, carry)

        lax.fori_loop(0, blocks, of_block, 0)


def each_field(fields, visit):
    def step(field, carry):
        visit(field)
        return carry

    lax.fori_loop(0, fields, step, 0)


def load_of(field, source, at, held, sems):
    return pltpu.make_async_copy(source.at[at], held.at[field], sems.at[field])


def start_loads(members, nvars, ens, stat, held, sems):
    for m in range(members):
        load_of(m, ens, m, held, sems).start()
    for v in range(nvars):
        load_of(members + v, stat, v, held, sems).start()


def pack_kernel(dims, ens, stat, side_a, side_b, held, sems):
    members, nvars, levels, rows, cells, blocks = dims
    start_loads(members, nvars, ens, stat, held, sems)
    for field in range(members + nvars):
        load_of(field, ens, 0, held, sems).wait()
        for begin, side in zip(begins(rows), (side_a, side_b)):
            for j in range(SWEEPS):
                side[j, pl.ds(field * levels, levels), :] = held[field, pl.ds(begin + j, levels, stride=rows), :]


def own_kernel(dims, powers, held, scale, side_a, layer, index, kind, group, localize, static, precision, out, key, weight):
    members, nvars, levels, rows, cells, blocks = dims
    inside = neighbours()

    def of_field(field):
        planes = {x: held[field, pl.ds(x, levels, stride=rows), :] for x in range(rows)}
        rate = rate_of(field, members, group, localize, static)
        planes = spread_product(planes, rows, rate, inside, powers)
        for x in range(rows):
            out[field, pl.ds(x, levels, stride=rows), :] = planes[x] * scale[field]

    each_field(members + nvars, of_field)
    rates = rates_of(members + nvars, members, group, localize, static)
    add_near(out, side_a, rates, (levels, rows, cells), scale)
    key[...] = layer[...] * (rows * cells) + index[...]
    total = jnp.zeros(kind.shape, jnp.float32)
    for k in range(precision.shape[0]):
        total = jnp.where(kind[...] == k, precision[k], total)
    weight[...] = total


def forward_kernel(dims, own, scale, side_b, key, frac, perturb_far, bound, group, localize, static, out, smooth, table, perturb, sem):
    members, nvars, levels, rows, cells, blocks = dims
    shift = cells.bit_length() - 1
    load = pltpu.make_async_copy(perturb_far, perturb, sem)
    load.start()

    smooth[...] = own[...]
    rates = rates_of(members + nvars, members, group, localize, static)
    add_far(smooth, side_b, rates, (levels, rows, cells), scale)
    load.wait()
    plane = levels * rows
    for v in range(nvars):
        total = smooth[members + v]
        for m in range(members):
            total = total + perturb[m, v].astype(jnp.float32) * smooth[m]
        high, low = halves(total)
        table[v * plane : (v + 1) * plane, :cells] = high
        table[v * plane : (v + 1) * plane, cells:] = low
    table[nvars * plane :, :] = jnp.zeros((BLOCK, 2 * cells), jnp.bfloat16)
    lanes = key.shape[1]
    parts = BLOCK // lanes

    def seen_in(block, start):
        keys = block_of(key, block)
        picked = lax.dot_general(
            table[pl.ds(pl.multiple_of(start, ALIGN), BLOCK), :],
            chosen_rows(keys, start, shift),
            (((0,), (0,)), ((), ())),
            preferred_element_type=jnp.float32,
        )
        picked = picked[:cells] + picked[cells:]
        return jnp.sum(picked * weights_of(keys, block_of(frac, block), cells), axis=0, keepdims=True)

    def visit(block, start):
        seen = seen_in(block, start)
        for part in range(parts):
            out[pl.ds(block * parts + part, 1), :] = seen[:, part * lanes : (part + 1) * lanes]

    def visit_again(block, start):
        seen = seen_in(block, start)
        for part in range(parts):
            at = pl.ds(block * parts + part, 1)
            out[at, :] = out[at, :] + seen[:, part * lanes : (part + 1) * lanes]

    every_window(bound, blocks, cells, visit, visit_again)


def scatter_kernel(dims, key, frac, weight, perturb, scale, *refs):
    members, nvars, levels, rows, cells, blocks = dims
    *seen, bound, source, side_a, side_b, gradient, valued = refs
    shift = cells.bit_length() - 1
    total = seen[0][...]
    for part in seen[1:]:
        total = total + part[...]
    valued[...] = total * weight[...]
    gradient[...] = jnp.zeros(gradient.shape, jnp.float32)

    def add_block(block, start):
        keys = block_of(key, block)
        placed = weights_of(keys, block_of(frac, block), cells) * block_of(valued, block)
        high, low = halves(placed)
        both = lax.dot_general(
            chosen_rows(keys, start, shift),
            jnp.concatenate([high, low], axis=0),
            (((1,), (1,)), ((), ())),
            preferred_element_type=jnp.float32,
        )
        at = pl.ds(pl.multiple_of(start, ALIGN), BLOCK)
        gradient[at, :] = gradient[at, :] + (both[:, :cells] + both[:, cells:])

    every_window(bound, blocks, cells, add_block, add_block)

    plane = levels * rows
    for m in range(members):
        total = perturb[m, 0].astype(jnp.float32) * gradient[:plane, :]
        for v in range(1, nvars):
            total = total + perturb[m, v].astype(jnp.float32) * gradient[v * plane : (v + 1) * plane, :]
        source[m] = total
    for begin, side in zip(begins(rows), (side_a, side_b)):
        for field in range(members + nvars):
            for j in range(SWEEPS):
                if field < members:
                    strip = source[field, pl.ds(begin + j, levels, stride=rows), :]
                else:
                    at = (field - members) * plane + begin + j
                    strip = gradient[pl.ds(at, levels, stride=rows), :] * scale[field]
                side[j, pl.ds(field * levels, levels), :] = strip


def local_kernel(dims, powers, source, gradient, scale, side_a, ens, stat, group, localize, static, out, held, sems):
    members, nvars, levels, rows, cells, blocks = dims
    inside = neighbours()
    plane = levels * rows
    start_loads(members, nvars, ens, stat, held, sems)

    def of_field(field, planes):
        rate = rate_of(field, members, group, localize, static)
        planes = spread_product(planes, rows, rate, inside, powers)
        load_of(field, ens, 0, held, sems).wait()
        for x in range(rows):
            at = pl.ds(x, levels, stride=rows)
            out[field, at, :] = held[field, at, :] + planes[x]

    def of_member(m):
        of_field(m, {x: source[m, pl.ds(x, levels, stride=rows), :] for x in range(rows)})

    def of_group(v):
        field = members + v
        planes = {x: gradient[pl.ds(v * plane + x, levels, stride=rows), :] * scale[field] for x in range(rows)}
        of_field(field, planes)

    each_field(members, of_member)
    each_field(nvars, of_group)
    rates = rates_of(members + nvars, members, group, localize, static)
    add_near(out, side_a, rates, (levels, rows, cells))


def edge_kernel(dims, own, side_b, group, localize, static, hv_ens, hv_stat, after, sems):
    members, nvars, levels, rows, cells, blocks = dims

    writes = []
    rates = rates_of(members + nvars, members, group, localize, static)
    upper = jnp.logical_not(is_even())
    add = adder(after, upper, (levels, rows, cells))
    below, above = neighbours()

    def visit(field, depth, part):
        if depth == 0:
            after[field] = own[field]
        add(field, depth, part)
        if depth == SWEEPS - 1:
            out = hv_ens.at[field] if field < members else hv_stat.at[field - members]
            write = pltpu.make_async_copy(after.at[field], out, sems.at[field])
            write.start()
            writes.append(write)

    add_side(side_b, upper, rates, (levels, rows, cells), visit, below * above)
    for write in writes:
        write.wait()


def exchange(side_a, side_b):
    count = lax.axis_size("tile")
    pairs_a = [(i, i ^ 1) for i in range(count)]
    pairs_b = [(i, (((i + 1) ^ 1) - 1) % count) for i in range(count)]
    return lax.ppermute(side_a, "tile", pairs_a), lax.ppermute(side_b, "tile", pairs_b)


def summands(value):
    count = lax.axis_size("grp")
    value = value + lax.ppermute(value, "grp", [(i, i ^ 1) for i in range(count)])
    turns = [2, 6, 4] if count == 8 else list(range(2, count, 2))
    return [value] + [lax.ppermute(value, "grp", [(i, i ^ turn) for i in range(count)]) for turn in turns]


VMEM = pl.BlockSpec(memory_space=pltpu.VMEM)
SMEM = pl.BlockSpec(memory_space=pltpu.SMEM)
HBM = pl.BlockSpec(memory_space=pltpu.HBM)


def call(kernel, dims, outs, ins, far=(), scalars=(), scratch=(), out_spec=VMEM, kinds=None, cost=2_000_000):
    def body(*refs):
        kernel(dims, *refs)

    far = [pltpu.with_memory_space_constraint(x, pltpu.HBM) for x in far]
    return pl.pallas_call(
        body,
        out_shape=tuple(jax.ShapeDtypeStruct(tuple(shape), kind) for shape, kind in zip(outs, kinds or [jnp.float32] * len(outs))),
        in_specs=[VMEM] * len(ins) + [HBM] * len(far) + [SMEM] * len(scalars),
        out_specs=tuple([out_spec] * len(outs)),
        scratch_shapes=list(scratch),
        compiler_params=pltpu.CompilerParams(vmem_limit_bytes=16 * 1024 * 1024),
        cost_estimate=pl.CostEstimate(flops=cost * 10, bytes_accessed=cost, transcendentals=0),
        name=kernel.__name__,
    )(*ins, *far, *scalars)


def per_device(
    ens_control,
    static_control,
    member_perturb,
    member_group,
    localize_rate,
    static_rate,
    static_scale,
    obs_index,
    obs_frac,
    obs_layer,
    obs_kind,
    obs_precision,
):
    members, levels, rows, cells = ens_control.shape
    nvars = static_control.shape[1]
    fields = members + nvars
    blocks = obs_index.shape[0] // BLOCK
    dims = (members, nvars, levels, rows, cells, blocks)
    plane = levels * rows
    strip = (SWEEPS, fields * levels, cells)

    ens = ens_control.reshape(members, plane, cells)
    stat = static_control.reshape(nvars, plane, cells)
    perturb = member_perturb.reshape(members, nvars, plane, cells)
    rates = [member_group, localize_rate, static_rate]

    whole = (fields, plane, cells)
    key_shape = (obs_index.shape[0] // cells, cells)
    powers = y_powers(cells)
    copying = [pltpu.SemaphoreType.DMA((fields,))]
    side_a, side_b, held = call(pack_kernel, dims, [strip, strip, whole], [], [ens, stat], [], copying)
    side_a, side_b = exchange(side_a, side_b)

    scale = jnp.concatenate([jnp.ones((members, levels), jnp.float32), static_scale[0]])
    scale = jnp.broadcast_to(scale[:, :, None], (fields, levels, cells))
    layer, index, kind = (x.reshape(-1, cells) for x in (obs_layer, obs_index, obs_kind))
    own, key, weight = call(
        own_kernel,
        dims,
        [whole, key_shape, key_shape],
        [powers, held, scale, side_a, layer, index, kind],
        [],
        rates + [obs_precision],
        kinds=[jnp.float32, jnp.int32, jnp.float32],
    )
    key, frac, weight = lax.sort((key.reshape(-1), obs_frac, weight.reshape(-1)), num_keys=1, is_stable=False)
    key, frac, weight = (x.reshape(key_shape) for x in (key, frac, weight))

    table_rows = nvars * plane + BLOCK
    (seen,) = call(
        forward_kernel,
        dims,
        [key.shape],
        [own, scale, side_b, key, frac],
        [perturb],
        [key] + rates,
        [
            pltpu.VMEM(whole, jnp.float32),
            pltpu.VMEM((table_rows, 2 * cells), jnp.bfloat16),
            pltpu.VMEM(perturb.shape, perturb.dtype),
            pltpu.SemaphoreType.DMA(()),
        ],
    )
    seen = summands(seen)
    source, side_a, side_b, gradient = call(
        scatter_kernel,
        dims,
        [(members, plane, cells), strip, strip, (table_rows, cells)],
        [key, frac, weight, perturb, scale] + seen,
        [],
        [key],
        [pltpu.VMEM(key.shape, jnp.float32)],
    )
    side_a, side_b = exchange(side_a, side_b)
    (own,) = call(local_kernel, dims, [whole], [powers, source, gradient, scale, side_a], [ens, stat], rates, [pltpu.VMEM(whole, jnp.float32)] + copying)
    hv_ens, hv_stat = call(
        edge_kernel,
        dims,
        [(members, plane, cells), (nvars, plane, cells)],
        [own, side_b],
        [],
        rates,
        [pltpu.VMEM(whole, jnp.float32), pltpu.SemaphoreType.DMA((fields,))],
        HBM,
    )
    return hv_ens.reshape(ens_control.shape), hv_stat.reshape(static_control.shape)


def solution(mesh):
    placed = (
        P("grp", None, "tile", None),
        P("grp", None, None, "tile", None),
        P("grp", None, None, "tile", None),
        P("grp"),
        P(),
        P("grp"),
        P("grp", None, None),
        P("tile"),
        P("tile"),
        P("tile"),
        P("tile"),
        P(),
    )
    return jax.shard_map(
        per_device,
        mesh=mesh,
        in_specs=placed,
        out_specs=(P("grp", None, "tile", None), P("grp", None, None, "tile", None)),
        check_vma=False,
    )
```

```python
import math

import jax
import jax.numpy as jnp
import numpy as np
from jax import lax
from jax.experimental import pallas as pl
from jax.experimental.pallas import tpu as pltpu
from jax.sharding import PartitionSpec as P

SWEEPS = 4
BLOCK = 256
ALIGN = 16


def along_x(planes, wanted, rows, rate, inside):
    factors = [(1.0 - 4.0 * rate, rate)] * 3
    if inside is not None:
        factors[1:] = [((1.0 - 4.0 * rate) * side, rate * side) for side in inside]
    result = {}
    for x in wanted:
        keep, share = factors[1 if x < 0 else 2 if x >= rows else 0]
        total = None
        for near in (x - 1, x + 1):
            if near in planes:
                total = planes[near] if total is None else total + planes[near]
        if total is not None:
            total = share * total
        if x in planes:
            total = keep * planes[x] if total is None else keep * planes[x] + total
        if total is not None:
            result[x] = total
    return result


def powers_along_x(planes, first, last, rows, rate, inside):
    stages = [planes]
    for left in range(SWEEPS - 1, -1, -1):
        stages.append(along_x(stages[-1], range(first - left, last + left + 1), rows, rate, inside))
    return stages


def binomial(j, rate):
    factor = float(math.comb(SWEEPS, j))
    for number in range(j):
        factor = factor * rate
    return factor


def along_y(value):
    cells = value.shape[1]
    lane = lax.broadcasted_iota(jnp.int32, value.shape, 1)
    below = jnp.where(lane == 0, 0.0, pltpu.roll(value, 1, 1))
    return below + jnp.where(lane == cells - 1, 0.0, pltpu.roll(value, cells - 1, 1))


def spread_rolled(planes, first, last, rows, rate, inside):
    stages = powers_along_x(planes, first, last, rows, rate, inside)
    result = {}
    for x in range(first, last + 1):
        total = None
        for j in range(SWEEPS, -1, -1):
            if total is not None:
                total = along_y(total)
            term = stages[SWEEPS - j].get(x)
            if term is not None:
                term = term if j == 0 else binomial(j, rate) * term
                total = term if total is None else total + term
        result[x] = total
    return result


def halves(value):
    high = value.astype(jnp.bfloat16)
    low = (value - high.astype(jnp.float32)).astype(jnp.bfloat16)
    return high, low


def y_powers(cells):
    once = np.eye(cells, k=1) + np.eye(cells, k=-1)
    row = np.concatenate([np.linalg.matrix_power(once, j) for j in range(1, SWEEPS + 1)], axis=1)
    return jnp.asarray(np.concatenate([row, row], axis=0), jnp.bfloat16)


GROUP = 8


def spread_product(planes, rows, rate, inside, powers):
    levels, cells = planes[0].shape
    terms = [{} for j in range(SWEEPS)]
    for first in range(0, rows, GROUP):
        both = jnp.concatenate(halves(jnp.concatenate([planes[x] for x in range(first, first + GROUP)], axis=0)), axis=1)
        product = jnp.dot(both, powers[...], preferred_element_type=jnp.float32)
        for at in range(GROUP):
            for j in range(SWEEPS):
                terms[j][first + at] = product[at * levels : (at + 1) * levels, j * cells : (j + 1) * cells]
    result = planes
    for j in range(1, SWEEPS + 1):
        left = SWEEPS - j
        result = along_x(result, range(-left, rows + left), rows, rate, inside)
        factor = binomial(j, rate)
        for x in range(rows):
            result[x] = result[x] + factor * terms[j - 1][x]
    return result


def rate_of(field, members, group, localize, static):
    member = jnp.minimum(field, members - 1)
    return jnp.where(field < members, localize[group[member]], static[0])


def rates_of(fields, members, group, localize, static):
    return [rate_of(field, members, group, localize, static) for field in range(fields)]


def neighbours():
    tile = lax.axis_index("tile")
    last = lax.axis_size("tile") - 1
    return jnp.where(tile > 0, 1.0, 0.0), jnp.where(tile < last, 1.0, 0.0)


def is_even():
    return lax.axis_index("tile") % 2 == 0


def begins(rows):
    even = is_even()
    return jnp.where(even, rows - SWEEPS, 0), jnp.where(even, 0, rows - SWEEPS)


BATCH = 4


def add_side(side, upper, rates, shape, visit, counts=None):
    levels, rows, cells = shape
    for first in range(0, len(rates), BATCH):
        fields = range(first, min(first + BATCH, len(rates)))
        rate = jnp.concatenate([jnp.full((levels, cells), rates[field], jnp.float32) for field in fields], axis=0)
        planes = {}
        for away in range(1, SWEEPS + 1):
            j = jnp.where(upper, away - 1, SWEEPS - away)
            planes[-away] = side[j, first * levels : (first + len(fields)) * levels, :]
        parts = spread_rolled(planes, 0, SWEEPS - 1, rows, rate, None)
        for at, field in enumerate(fields):
            for depth in range(SWEEPS):
                part = parts[depth][at * levels : (at + 1) * levels]
                visit(field, depth, part if counts is None else part * counts)


def adder(into, upper, shape, scale=None):
    levels, rows, cells = shape

    def visit(field, depth, part):
        at = pl.ds(jnp.where(upper, rows - 1 - depth, depth), levels, stride=rows)
        into[field, at, :] = into[field, at, :] + (part if scale is None else part * scale[field])

    return visit


def add_near(into, side, rates, shape, scale=None):
    upper = is_even()
    add_side(side, upper, rates, shape, adder(into, upper, shape, scale))


def add_far(into, side, rates, shape, scale=None):
    upper = jnp.logical_not(is_even())
    below, above = neighbours()
    add_side(side, upper, rates, shape, adder(into, upper, shape, scale), below * above)


def block_of(ref, block):
    lanes = ref.shape[1]
    parts = BLOCK // lanes
    return jnp.concatenate([ref[pl.ds(block * parts + part, 1), :] for part in range(parts)], axis=1)


def weights_of(key, frac, cells):
    cell = key & (cells - 1)
    second = (cell + 1) & (cells - 1)
    spot = lax.broadcasted_iota(jnp.int32, (cells, key.shape[1]), 0)
    return jnp.where(spot == cell, 1.0 - frac, jnp.where(spot == second, frac, 0.0))


def chosen_rows(key, start, shift):
    row = ((key >> shift) - start).astype(jnp.int16)
    spot = lax.broadcasted_iota(jnp.int16, (BLOCK, key.shape[1]), 0)
    return jnp.where(spot == row, jnp.bfloat16(1), jnp.bfloat16(0))


def window_of(bound, block, cells):
    parts = BLOCK // bound.shape[1]
    shift = cells.bit_length() - 1
    start = ((bound[block * parts, 0] >> shift) // ALIGN) * ALIGN
    last = bound[block * parts + parts - 1, bound.shape[1] - 1] >> shift
    return start, (last - start) // BLOCK + 1


def every_window(bound, blocks, cells, visit, visit_again):
    most = 1
    for block in range(blocks):
        start, count = window_of(bound, block, cells)
        most = jnp.maximum(most, count)
        visit(block, start)

    @pl.when(most > 1)
    def _():
        def of_block(block, carry):
            start, count = window_of(bound, block, cells)

            def of_window(window, inner):
                visit_again(block, start + window * BLOCK)
                return inner

            return lax.fori_loop(1, count, of_window, carry)

        lax.fori_loop(0, blocks, of_block, 0)


def each_field(fields, visit, unroll=1):
    def step(field, carry):
        visit(field)
        return carry

    lax.fori_loop(0, fields, step, 0, unroll=unroll)


def load_of(field, source, at, held, sems):
    return pltpu.make_async_copy(source.at[at], held.at[field], sems.at[field])


def start_loads(members, nvars, ens, stat, held, sems):
    for m in range(members):
        load_of(m, ens, m, held, sems).start()
    for v in range(nvars):
        load_of(members + v, stat, v, held, sems).start()


def pack_kernel(dims, ens, stat, side_a, side_b, held, sems):
    members, nvars, levels, rows, cells, blocks = dims
    start_loads(members, nvars, ens, stat, held, sems)
    for field in range(members + nvars):
        load_of(field, ens, 0, held, sems).wait()
        for begin, side in zip(begins(rows), (side_a, side_b)):
            for j in range(SWEEPS):
                side[j, pl.ds(field * levels, levels), :] = held[field, pl.ds(begin + j, levels, stride=rows), :]


def own_kernel(dims, powers, held, scale, side_a, layer, index, kind, group, localize, static, precision, out, key, weight):
    members, nvars, levels, rows, cells, blocks = dims
    inside = neighbours()

    def of_field(field):
        planes = {x: held[field, pl.ds(x, levels, stride=rows), :] for x in range(rows)}
        rate = rate_of(field, members, group, localize, static)
        planes = spread_product(planes, rows, rate, inside, powers)
        for x in range(rows):
            out[field, pl.ds(x, levels, stride=rows), :] = planes[x] * scale[field]

    each_field(members + nvars, of_field, members + nvars)
    rates = rates_of(members + nvars, members, group, localize, static)
    add_near(out, side_a, rates, (levels, rows, cells), scale)
    key[...] = layer[...] * (rows * cells) + index[...]
    total = jnp.zeros(kind.shape, jnp.float32)
    for k in range(precision.shape[0]):
        total = jnp.where(kind[...] == k, precision[k], total)
    weight[...] = total


def forward_kernel(dims, own, scale, side_b, key, frac, perturb_far, bound, group, localize, static, out, smooth, table, perturb, sem):
    members, nvars, levels, rows, cells, blocks = dims
    shift = cells.bit_length() - 1
    loads = [pltpu.make_async_copy(perturb_far.at[m, v], perturb.at[m, v], sem.at[m, v]) for v in range(nvars) for m in range(members)]
    for load in loads:
        load.start()

    smooth[...] = own[...]
    rates = rates_of(members + nvars, members, group, localize, static)
    add_far(smooth, side_b, rates, (levels, rows, cells), scale)
    plane = levels * rows
    for v in range(nvars):
        total = smooth[members + v]
        for m in range(members):
            loads[v * members + m].wait()
            total = total + perturb[m, v].astype(jnp.float32) * smooth[m]
        high, low = halves(total)
        table[v * plane : (v + 1) * plane, :cells] = high
        table[v * plane : (v + 1) * plane, cells:] = low
    table[nvars * plane :, :] = jnp.zeros((BLOCK, 2 * cells), jnp.bfloat16)
    lanes = key.shape[1]
    parts = BLOCK // lanes

    def seen_in(block, start):
        keys = block_of(key, block)
        picked = lax.dot_general(
            table[pl.ds(pl.multiple_of(start, ALIGN), BLOCK), :],
            chosen_rows(keys, start, shift),
            (((0,), (0,)), ((), ())),
            preferred_element_type=jnp.float32,
        )
        picked = picked[:cells] + picked[cells:]
        return jnp.sum(picked * weights_of(keys, block_of(frac, block), cells), axis=0, keepdims=True)

    def visit(block, start):
        seen = seen_in(block, start)
        for part in range(parts):
            out[pl.ds(block * parts + part, 1), :] = seen[:, part * lanes : (part + 1) * lanes]

    def visit_again(block, start):
        seen = seen_in(block, start)
        for part in range(parts):
            at = pl.ds(block * parts + part, 1)
            out[at, :] = out[at, :] + seen[:, part * lanes : (part + 1) * lanes]

    every_window(bound, blocks, cells, visit, visit_again)


def scatter_kernel(dims, key, frac, weight, perturb, scale, *refs):
    members, nvars, levels, rows, cells, blocks = dims
    *seen, bound, source, side_a, side_b, gradient, valued = refs
    shift = cells.bit_length() - 1
    total = seen[0][...]
    for part in seen[1:]:
        total = total + part[...]
    valued[...] = total * weight[...]
    gradient[...] = jnp.zeros(gradient.shape, jnp.float32)

    def add_block(block, start):
        keys = block_of(key, block)
        placed = weights_of(keys, block_of(frac, block), cells) * block_of(valued, block)
        high, low = halves(placed)
        both = lax.dot_general(
            chosen_rows(keys, start, shift),
            jnp.concatenate([high, low], axis=0),
            (((1,), (1,)), ((), ())),
            preferred_element_type=jnp.float32,
        )
        at = pl.ds(pl.multiple_of(start, ALIGN), BLOCK)
        gradient[at, :] = gradient[at, :] + (both[:, :cells] + both[:, cells:])

    every_window(bound, blocks, cells, add_block, add_block)

    plane = levels * rows
    for m in range(members):
        total = perturb[m, 0].astype(jnp.float32) * gradient[:plane, :]
        for v in range(1, nvars):
            total = total + perturb[m, v].astype(jnp.float32) * gradient[v * plane : (v + 1) * plane, :]
        source[m] = total
    for begin, side in zip(begins(rows), (side_a, side_b)):
        for field in range(members + nvars):
            for j in range(SWEEPS):
                if field < members:
                    strip = source[field, pl.ds(begin + j, levels, stride=rows), :]
                else:
                    at = (field - members) * plane + begin + j
                    strip = gradient[pl.ds(at, levels, stride=rows), :] * scale[field]
                side[j, pl.ds(field * levels, levels), :] = strip


def local_kernel(dims, powers, source, gradient, scale, side_a, ens, stat, group, localize, static, out, held, sems):
    members, nvars, levels, rows, cells, blocks = dims
    inside = neighbours()
    plane = levels * rows
    start_loads(members, nvars, ens, stat, held, sems)

    def of_field(field, planes):
        rate = rate_of(field, members, group, localize, static)
        planes = spread_product(planes, rows, rate, inside, powers)
        load_of(field, ens, 0, held, sems).wait()
        for x in range(rows):
            at = pl.ds(x, levels, stride=rows)
            out[field, at, :] = held[field, at, :] + planes[x]

    def of_member(m):
        of_field(m, {x: source[m, pl.ds(x, levels, stride=rows), :] for x in range(rows)})

    def of_group(v):
        field = members + v
        planes = {x: gradient[pl.ds(v * plane + x, levels, stride=rows), :] * scale[field] for x in range(rows)}
        of_field(field, planes)

    each_field(members, of_member)
    each_field(nvars, of_group)
    rates = rates_of(members + nvars, members, group, localize, static)
    add_near(out, side_a, rates, (levels, rows, cells))


def edge_kernel(dims, own, side_b, group, localize, static, hv_ens, hv_stat, after, sems):
    members, nvars, levels, rows, cells, blocks = dims

    writes = []
    rates = rates_of(members + nvars, members, group, localize, static)
    upper = jnp.logical_not(is_even())
    add = adder(after, upper, (levels, rows, cells))
    below, above = neighbours()

    def visit(field, depth, part):
        if depth == 0:
            after[field] = own[field]
        add(field, depth, part)
        if depth == SWEEPS - 1:
            out = hv_ens.at[field] if field < members else hv_stat.at[field - members]
            write = pltpu.make_async_copy(after.at[field], out, sems.at[field])
            write.start()
            writes.append(write)

    add_side(side_b, upper, rates, (levels, rows, cells), visit, below * above)
    for write in writes:
        write.wait()


def exchange(side_a, side_b):
    count = lax.axis_size("tile")
    pairs_a = [(i, i ^ 1) for i in range(count)]
    pairs_b = [(i, (((i + 1) ^ 1) - 1) % count) for i in range(count)]
    return lax.ppermute(side_a, "tile", pairs_a), lax.ppermute(side_b, "tile", pairs_b)


def summands(value):
    count = lax.axis_size("grp")
    value = value + lax.ppermute(value, "grp", [(i, i ^ 1) for i in range(count)])
    turns = [2, 6, 4] if count == 8 else list(range(2, count, 2))
    return [value] + [lax.ppermute(value, "grp", [(i, i ^ turn) for i in range(count)]) for turn in turns]


VMEM = pl.BlockSpec(memory_space=pltpu.VMEM)
SMEM = pl.BlockSpec(memory_space=pltpu.SMEM)
HBM = pl.BlockSpec(memory_space=pltpu.HBM)


def call(kernel, dims, outs, ins, far=(), scalars=(), scratch=(), out_spec=VMEM, kinds=None, cost=2_000_000):
    def body(*refs):
        kernel(dims, *refs)

    far = [pltpu.with_memory_space_constraint(x, pltpu.HBM) for x in far]
    return pl.pallas_call(
        body,
        out_shape=tuple(jax.ShapeDtypeStruct(tuple(shape), kind) for shape, kind in zip(outs, kinds or [jnp.float32] * len(outs))),
        in_specs=[VMEM] * len(ins) + [HBM] * len(far) + [SMEM] * len(scalars),
        out_specs=tuple([out_spec] * len(outs)),
        scratch_shapes=list(scratch),
        compiler_params=pltpu.CompilerParams(vmem_limit_bytes=16 * 1024 * 1024),
        cost_estimate=pl.CostEstimate(flops=cost * 10, bytes_accessed=cost, transcendentals=0),
        name=kernel.__name__,
    )(*ins, *far, *scalars)


def per_device(
    ens_control,
    static_control,
    member_perturb,
    member_group,
    localize_rate,
    static_rate,
    static_scale,
    obs_index,
    obs_frac,
    obs_layer,
    obs_kind,
    obs_precision,
):
    members, levels, rows, cells = ens_control.shape
    nvars = static_control.shape[1]
    fields = members + nvars
    blocks = obs_index.shape[0] // BLOCK
    dims = (members, nvars, levels, rows, cells, blocks)
    plane = levels * rows
    strip = (SWEEPS, fields * levels, cells)

    ens = ens_control.reshape(members, plane, cells)
    stat = static_control.reshape(nvars, plane, cells)
    perturb = member_perturb.reshape(members, nvars, plane, cells)
    rates = [member_group, localize_rate, static_rate]

    whole = (fields, plane, cells)
    key_shape = (obs_index.shape[0] // cells, cells)
    powers = y_powers(cells)
    copying = [pltpu.SemaphoreType.DMA((fields,))]
    side_a, side_b, held = call(pack_kernel, dims, [strip, strip, whole], [], [ens, stat], [], copying)
    side_a, side_b = exchange(side_a, side_b)

    scale = jnp.concatenate([jnp.ones((members, levels), jnp.float32), static_scale[0]])
    scale = jnp.broadcast_to(scale[:, :, None], (fields, levels, cells))
    layer, index, kind = (x.reshape(-1, cells) for x in (obs_layer, obs_index, obs_kind))
    own, key, weight = call(
        own_kernel,
        dims,
        [whole, key_shape, key_shape],
        [powers, held, scale, side_a, layer, index, kind],
        [],
        rates + [obs_precision],
        kinds=[jnp.float32, jnp.int32, jnp.float32],
    )
    key, frac, weight = lax.sort((key.reshape(-1), obs_frac, weight.reshape(-1)), num_keys=1, is_stable=False)
    key, frac, weight = (x.reshape(key_shape) for x in (key, frac, weight))

    table_rows = nvars * plane + BLOCK
    (seen,) = call(
        forward_kernel,
        dims,
        [key.shape],
        [own, scale, side_b, key, frac],
        [perturb],
        [key] + rates,
        [
            pltpu.VMEM(whole, jnp.float32),
            pltpu.VMEM((table_rows, 2 * cells), jnp.bfloat16),
            pltpu.VMEM(perturb.shape, perturb.dtype),
            pltpu.SemaphoreType.DMA((members, nvars)),
        ],
    )
    seen = summands(seen)
    source, side_a, side_b, gradient = call(
        scatter_kernel,
        dims,
        [(members, plane, cells), strip, strip, (table_rows, cells)],
        [key, frac, weight, perturb, scale] + seen,
        [],
        [key],
        [pltpu.VMEM(key.shape, jnp.float32)],
    )
    side_a, side_b = exchange(side_a, side_b)
    (own,) = call(local_kernel, dims, [whole], [powers, source, gradient, scale, side_a], [ens, stat], rates, [pltpu.VMEM(whole, jnp.float32)] + copying)
    hv_ens, hv_stat = call(
        edge_kernel,
        dims,
        [(members, plane, cells), (nvars, plane, cells)],
        [own, side_b],
        [],
        rates,
        [pltpu.VMEM(whole, jnp.float32), pltpu.SemaphoreType.DMA((fields,))],
        HBM,
    )
    return hv_ens.reshape(ens_control.shape), hv_stat.reshape(static_control.shape)


def solution(mesh):
    placed = (
        P("grp", None, "tile", None),
        P("grp", None, None, "tile", None),
        P("grp", None, None, "tile", None),
        P("grp"),
        P(),
        P("grp"),
        P("grp", None, None),
        P("tile"),
        P("tile"),
        P("tile"),
        P("tile"),
        P(),
    )
    return jax.shard_map(
        per_device,
        mesh=mesh,
        in_specs=placed,
        out_specs=(P("grp", None, "tile", None), P("grp", None, None, "tile", None)),
        check_vma=False,
    )
```

```python
import math

import jax
import jax.numpy as jnp
import numpy as np
from jax import lax
from jax.experimental import pallas as pl
from jax.experimental.pallas import tpu as pltpu
from jax.sharding import PartitionSpec as P

SWEEPS = 4
BLOCK = 256
ALIGN = 16


def along_x(planes, wanted, rows, rate, inside):
    factors = [(1.0 - 4.0 * rate, rate)] * 3
    if inside is not None:
        factors[1:] = [((1.0 - 4.0 * rate) * side, rate * side) for side in inside]
    result = {}
    for x in wanted:
        keep, share = factors[1 if x < 0 else 2 if x >= rows else 0]
        total = None
        for near in (x - 1, x + 1):
            if near in planes:
                total = planes[near] if total is None else total + planes[near]
        if total is not None:
            total = share * total
        if x in planes:
            total = keep * planes[x] if total is None else keep * planes[x] + total
        if total is not None:
            result[x] = total
    return result


def powers_along_x(planes, first, last, rows, rate, inside):
    stages = [planes]
    for left in range(SWEEPS - 1, -1, -1):
        stages.append(along_x(stages[-1], range(first - left, last + left + 1), rows, rate, inside))
    return stages


def binomial(j, rate):
    factor = float(math.comb(SWEEPS, j))
    for number in range(j):
        factor = factor * rate
    return factor


def along_y(value):
    cells = value.shape[1]
    lane = lax.broadcasted_iota(jnp.int32, value.shape, 1)
    below = jnp.where(lane == 0, 0.0, pltpu.roll(value, 1, 1))
    return below + jnp.where(lane == cells - 1, 0.0, pltpu.roll(value, cells - 1, 1))


def spread_rolled(planes, first, last, rows, rate, inside):
    stages = powers_along_x(planes, first, last, rows, rate, inside)
    result = {}
    for x in range(first, last + 1):
        total = None
        for j in range(SWEEPS, -1, -1):
            if total is not None:
                total = along_y(total)
            term = stages[SWEEPS - j].get(x)
            if term is not None:
                term = term if j == 0 else binomial(j, rate) * term
                total = term if total is None else total + term
        result[x] = total
    return result


def halves(value):
    high = value.astype(jnp.bfloat16)
    low = (value - high.astype(jnp.float32)).astype(jnp.bfloat16)
    return high, low


def y_powers(cells):
    once = np.eye(cells, k=1) + np.eye(cells, k=-1)
    row = [math.comb(SWEEPS, j) * np.linalg.matrix_power(once, j) for j in range(1, SWEEPS + 1)]
    return jnp.asarray(np.concatenate([np.concatenate(row, axis=1)] * 2, axis=0), jnp.bfloat16)


GROUP = 8


def spread_product(planes, rows, rate, inside, powers, scale=None):
    levels, cells = planes[0].shape
    terms = [{} for j in range(SWEEPS)]
    for first in range(0, rows, GROUP):
        both = jnp.concatenate(halves(jnp.concatenate([planes[x] for x in range(first, first + GROUP)], axis=0)), axis=1)
        product = jnp.dot(both, powers[...], preferred_element_type=jnp.float32)
        for at in range(GROUP):
            for j in range(SWEEPS):
                terms[j][first + at] = product[at * levels : (at + 1) * levels, j * cells : (j + 1) * cells]
    own = jnp.broadcast_to(1.0 / jnp.full((8, cells), rate, jnp.float32) - 4.0, (levels // 8, 8, cells)).reshape(levels, cells)
    result = planes
    for j in range(1, SWEEPS + 1):
        left = SWEEPS - j
        before, result = result, {}
        for x in range(-left, rows + left):
            total = terms[j - 1].get(x)
            for near in (x - 1, x + 1):
                if near in before:
                    total = before[near] if total is None else total + before[near]
            if x in before:
                total = own * before[x] if total is None else total + own * before[x]
            if total is not None:
                result[x] = total * inside[0] if x < 0 else total * inside[1] if x >= rows else total
    fourth = rate * rate * (rate * rate)
    return {x: value * (fourth if scale is None else fourth * scale) for x, value in result.items()}


def rate_of(field, members, group, localize, static):
    member = jnp.minimum(field, members - 1)
    return jnp.where(field < members, localize[group[member]], static[0])


def rates_of(fields, members, group, localize, static):
    return [rate_of(field, members, group, localize, static) for field in range(fields)]


def neighbours():
    tile = lax.axis_index("tile")
    last = lax.axis_size("tile") - 1
    return jnp.where(tile > 0, 1.0, 0.0), jnp.where(tile < last, 1.0, 0.0)


def is_even():
    return lax.axis_index("tile") % 2 == 0


def begins(rows):
    even = is_even()
    return jnp.where(even, rows - SWEEPS, 0), jnp.where(even, 0, rows - SWEEPS)


def add_side(side, upper, rates, shape, visit, counts=None, batch=None):
    levels, rows, cells = shape
    batch = batch or len(rates)
    for first in range(0, len(rates), batch):
        fields = range(first, min(first + batch, len(rates)))
        rate = jnp.concatenate([jnp.full((levels, cells), rates[field], jnp.float32) for field in fields], axis=0)
        planes = {}
        for away in range(1, SWEEPS + 1):
            j = jnp.where(upper, away - 1, SWEEPS - away)
            planes[-away] = side[j, first * levels : (first + len(fields)) * levels, :]
        parts = spread_rolled(planes, 0, SWEEPS - 1, rows, rate, None)
        for at, field in enumerate(fields):
            for depth in range(SWEEPS):
                part = parts[depth][at * levels : (at + 1) * levels]
                visit(field, depth, part if counts is None else part * counts)


def adder(into, upper, shape, scale=None):
    levels, rows, cells = shape

    def visit(field, depth, part):
        at = pl.ds(jnp.where(upper, rows - 1 - depth, depth), levels, stride=rows)
        into[field, at, :] = into[field, at, :] + (part if scale is None else part * scale[field])

    return visit


def add_near(into, side, rates, shape, scale=None):
    upper = is_even()
    add_side(side, upper, rates, shape, adder(into, upper, shape, scale))


def add_far(into, side, rates, shape, scale=None):
    upper = jnp.logical_not(is_even())
    below, above = neighbours()
    add_side(side, upper, rates, shape, adder(into, upper, shape, scale), below * above)


def block_of(ref, block):
    lanes = ref.shape[1]
    parts = BLOCK // lanes
    return jnp.concatenate([ref[pl.ds(block * parts + part, 1), :] for part in range(parts)], axis=1)


def weights_of(key, frac, cells):
    cell = key & (cells - 1)
    second = (cell + 1) & (cells - 1)
    spot = lax.broadcasted_iota(jnp.int32, (cells, key.shape[1]), 0)
    return jnp.where(spot == cell, 1.0 - frac, jnp.where(spot == second, frac, 0.0))


def chosen_rows(key, start, shift):
    row = ((key >> shift) - start).astype(jnp.int16)
    spot = lax.broadcasted_iota(jnp.int16, (BLOCK, key.shape[1]), 0)
    return jnp.where(spot == row, jnp.bfloat16(1), jnp.bfloat16(0))


def window_of(bound, block, cells):
    parts = BLOCK // bound.shape[1]
    shift = cells.bit_length() - 1
    start = ((bound[block * parts, 0] >> shift) // ALIGN) * ALIGN
    last = bound[block * parts + parts - 1, bound.shape[1] - 1] >> shift
    return start, (last - start) // BLOCK + 1


def every_window(bound, blocks, cells, visit, visit_again):
    most = 1
    for block in range(blocks):
        start, count = window_of(bound, block, cells)
        most = jnp.maximum(most, count)
        visit(block, start)

    @pl.when(most > 1)
    def _():
        def of_block(block, carry):
            start, count = window_of(bound, block, cells)

            def of_window(window, inner):
                visit_again(block, start + window * BLOCK)
                return inner

            return lax.fori_loop(1, count, of_window, carry)

        lax.fori_loop(0, blocks, of_block, 0)


def each_field(fields, visit, unroll=1):
    def step(field, carry):
        visit(field)
        return carry

    lax.fori_loop(0, fields, step, 0, unroll=unroll)


def load_of(field, source, at, held, sems):
    return pltpu.make_async_copy(source.at[at], held.at[field], sems.at[field])


def start_loads(members, nvars, ens, stat, held, sems):
    for m in range(members):
        load_of(m, ens, m, held, sems).start()
    for v in range(nvars):
        load_of(members + v, stat, v, held, sems).start()


def pack_kernel(dims, ens, stat, side_a, side_b, held, sems):
    members, nvars, levels, rows, cells, blocks = dims
    start_loads(members, nvars, ens, stat, held, sems)
    for field in range(members + nvars):
        load_of(field, ens, 0, held, sems).wait()
        for begin, side in zip(begins(rows), (side_a, side_b)):
            for j in range(SWEEPS):
                side[j, pl.ds(field * levels, levels), :] = held[field, pl.ds(begin + j, levels, stride=rows), :]


def own_kernel(dims, powers, held, scale, side_a, layer, index, kind, group, localize, static, precision, out, key, weight):
    members, nvars, levels, rows, cells, blocks = dims
    inside = neighbours()

    def of_field(field):
        planes = {x: held[field, pl.ds(x, levels, stride=rows), :] for x in range(rows)}
        rate = rate_of(field, members, group, localize, static)
        planes = spread_product(planes, rows, rate, inside, powers, scale[field])
        for x in range(rows):
            out[field, pl.ds(x, levels, stride=rows), :] = planes[x]

    each_field(members + nvars, of_field, members + nvars)
    rates = rates_of(members + nvars, members, group, localize, static)
    add_near(out, side_a, rates, (levels, rows, cells), scale)
    key[...] = layer[...] * (rows * cells) + index[...]
    total = jnp.zeros(kind.shape, jnp.float32)
    for k in range(precision.shape[0]):
        total = jnp.where(kind[...] == k, precision[k], total)
    weight[...] = total


def forward_kernel(dims, own, scale, side_b, key, frac, perturb_far, bound, group, localize, static, out, smooth, table, perturb, sem):
    members, nvars, levels, rows, cells, blocks = dims
    shift = cells.bit_length() - 1
    loads = [pltpu.make_async_copy(perturb_far.at[m, v], perturb.at[m, v], sem.at[m, v]) for v in range(nvars) for m in range(members)]
    for load in loads:
        load.start()

    smooth[...] = own[...]
    rates = rates_of(members + nvars, members, group, localize, static)
    add_far(smooth, side_b, rates, (levels, rows, cells), scale)
    plane = levels * rows
    for v in range(nvars):
        total = smooth[members + v]
        for m in range(members):
            loads[v * members + m].wait()
            total = total + perturb[m, v].astype(jnp.float32) * smooth[m]
        high, low = halves(total)
        table[v * plane : (v + 1) * plane, :cells] = high
        table[v * plane : (v + 1) * plane, cells:] = low
    table[nvars * plane :, :] = jnp.zeros((BLOCK, 2 * cells), jnp.bfloat16)
    lanes = key.shape[1]
    parts = BLOCK // lanes

    def seen_in(block, start):
        keys = block_of(key, block)
        picked = lax.dot_general(
            table[pl.ds(pl.multiple_of(start, ALIGN), BLOCK), :],
            chosen_rows(keys, start, shift),
            (((0,), (0,)), ((), ())),
            preferred_element_type=jnp.float32,
        )
        picked = picked[:cells] + picked[cells:]
        return jnp.sum(picked * weights_of(keys, block_of(frac, block), cells), axis=0, keepdims=True)

    def visit(block, start):
        seen = seen_in(block, start)
        for part in range(parts):
            out[pl.ds(block * parts + part, 1), :] = seen[:, part * lanes : (part + 1) * lanes]

    def visit_again(block, start):
        seen = seen_in(block, start)
        for part in range(parts):
            at = pl.ds(block * parts + part, 1)
            out[at, :] = out[at, :] + seen[:, part * lanes : (part + 1) * lanes]

    every_window(bound, blocks, cells, visit, visit_again)


def scatter_kernel(dims, key, frac, weight, perturb, scale, *refs):
    members, nvars, levels, rows, cells, blocks = dims
    *seen, bound, source, side_a, side_b, gradient, valued = refs
    shift = cells.bit_length() - 1
    total = seen[0][...]
    for part in seen[1:]:
        total = total + part[...]
    valued[...] = total * weight[...]
    gradient[...] = jnp.zeros(gradient.shape, jnp.float32)

    def add_block(block, start):
        keys = block_of(key, block)
        placed = weights_of(keys, block_of(frac, block), cells) * block_of(valued, block)
        high, low = halves(placed)
        both = lax.dot_general(
            chosen_rows(keys, start, shift),
            jnp.concatenate([high, low], axis=0),
            (((1,), (1,)), ((), ())),
            preferred_element_type=jnp.float32,
        )
        at = pl.ds(pl.multiple_of(start, ALIGN), BLOCK)
        gradient[at, :] = gradient[at, :] + (both[:, :cells] + both[:, cells:])

    every_window(bound, blocks, cells, add_block, add_block)

    plane = levels * rows
    for m in range(members):
        total = perturb[m, 0].astype(jnp.float32) * gradient[:plane, :]
        for v in range(1, nvars):
            total = total + perturb[m, v].astype(jnp.float32) * gradient[v * plane : (v + 1) * plane, :]
        source[m] = total
    for begin, side in zip(begins(rows), (side_a, side_b)):
        for field in range(members + nvars):
            for j in range(SWEEPS):
                if field < members:
                    strip = source[field, pl.ds(begin + j, levels, stride=rows), :]
                else:
                    at = (field - members) * plane + begin + j
                    strip = gradient[pl.ds(at, levels, stride=rows), :] * scale[field]
                side[j, pl.ds(field * levels, levels), :] = strip


def local_kernel(dims, powers, source, gradient, scale, side_a, ens, stat, group, localize, static, out, held, sems):
    members, nvars, levels, rows, cells, blocks = dims
    inside = neighbours()
    plane = levels * rows
    start_loads(members, nvars, ens, stat, held, sems)

    def of_field(field, planes):
        rate = rate_of(field, members, group, localize, static)
        planes = spread_product(planes, rows, rate, inside, powers)
        load_of(field, ens, 0, held, sems).wait()
        for x in range(rows):
            at = pl.ds(x, levels, stride=rows)
            out[field, at, :] = held[field, at, :] + planes[x]

    def of_member(m):
        of_field(m, {x: source[m, pl.ds(x, levels, stride=rows), :] for x in range(rows)})

    def of_group(v):
        field = members + v
        planes = {x: gradient[pl.ds(v * plane + x, levels, stride=rows), :] * scale[field] for x in range(rows)}
        of_field(field, planes)

    each_field(members, of_member)
    each_field(nvars, of_group)
    rates = rates_of(members + nvars, members, group, localize, static)
    add_near(out, side_a, rates, (levels, rows, cells))


def edge_kernel(dims, own, side_b, group, localize, static, hv_ens, hv_stat, after, sems):
    members, nvars, levels, rows, cells, blocks = dims

    writes = []
    rates = rates_of(members + nvars, members, group, localize, static)
    upper = jnp.logical_not(is_even())
    add = adder(after, upper, (levels, rows, cells))
    below, above = neighbours()

    def visit(field, depth, part):
        if depth == 0:
            after[field] = own[field]
        add(field, depth, part)
        if depth == SWEEPS - 1:
            out = hv_ens.at[field] if field < members else hv_stat.at[field - members]
            write = pltpu.make_async_copy(after.at[field], out, sems.at[field])
            write.start()
            writes.append(write)

    add_side(side_b, upper, rates, (levels, rows, cells), visit, below * above, 4)
    for write in writes:
        write.wait()


def exchange(side_a, side_b):
    count = lax.axis_size("tile")
    pairs_a = [(i, i ^ 1) for i in range(count)]
    pairs_b = [(i, (((i + 1) ^ 1) - 1) % count) for i in range(count)]
    return lax.ppermute(side_a, "tile", pairs_a), lax.ppermute(side_b, "tile", pairs_b)


def summands(value):
    count = lax.axis_size("grp")
    value = value + lax.ppermute(value, "grp", [(i, i ^ 1) for i in range(count)])
    turns = [2, 6, 4] if count == 8 else list(range(2, count, 2))
    return [value] + [lax.ppermute(value, "grp", [(i, i ^ turn) for i in range(count)]) for turn in turns]


VMEM = pl.BlockSpec(memory_space=pltpu.VMEM)
SMEM = pl.BlockSpec(memory_space=pltpu.SMEM)
HBM = pl.BlockSpec(memory_space=pltpu.HBM)


def call(kernel, dims, outs, ins, far=(), scalars=(), scratch=(), out_spec=VMEM, kinds=None, cost=2_000_000):
    def body(*refs):
        kernel(dims, *refs)

    far = [pltpu.with_memory_space_constraint(x, pltpu.HBM) for x in far]
    return pl.pallas_call(
        body,
        out_shape=tuple(jax.ShapeDtypeStruct(tuple(shape), kind) for shape, kind in zip(outs, kinds or [jnp.float32] * len(outs))),
        in_specs=[VMEM] * len(ins) + [HBM] * len(far) + [SMEM] * len(scalars),
        out_specs=tuple([out_spec] * len(outs)),
        scratch_shapes=list(scratch),
        compiler_params=pltpu.CompilerParams(vmem_limit_bytes=16 * 1024 * 1024),
        cost_estimate=pl.CostEstimate(flops=cost * 10, bytes_accessed=cost, transcendentals=0),
        name=kernel.__name__,
    )(*ins, *far, *scalars)


def per_device(
    ens_control,
    static_control,
    member_perturb,
    member_group,
    localize_rate,
    static_rate,
    static_scale,
    obs_index,
    obs_frac,
    obs_layer,
    obs_kind,
    obs_precision,
):
    members, levels, rows, cells = ens_control.shape
    nvars = static_control.shape[1]
    fields = members + nvars
    blocks = obs_index.shape[0] // BLOCK
    dims = (members, nvars, levels, rows, cells, blocks)
    plane = levels * rows
    strip = (SWEEPS, fields * levels, cells)

    ens = ens_control.reshape(members, plane, cells)
    stat = static_control.reshape(nvars, plane, cells)
    perturb = member_perturb.reshape(members, nvars, plane, cells)
    rates = [member_group, localize_rate, static_rate]

    whole = (fields, plane, cells)
    key_shape = (obs_index.shape[0] // cells, cells)
    powers = y_powers(cells)
    copying = [pltpu.SemaphoreType.DMA((fields,))]
    side_a, side_b, held = call(pack_kernel, dims, [strip, strip, whole], [], [ens, stat], [], copying)
    side_a, side_b = exchange(side_a, side_b)

    scale = jnp.concatenate([jnp.ones((members, levels), jnp.float32), static_scale[0]])
    scale = jnp.broadcast_to(scale[:, :, None], (fields, levels, cells))
    layer, index, kind = (x.reshape(-1, cells) for x in (obs_layer, obs_index, obs_kind))
    own, key, weight = call(
        own_kernel,
        dims,
        [whole, key_shape, key_shape],
        [powers, held, scale, side_a, layer, index, kind],
        [],
        rates + [obs_precision],
        kinds=[jnp.float32, jnp.int32, jnp.float32],
    )
    key, frac, weight = lax.sort((key.reshape(-1), obs_frac, weight.reshape(-1)), num_keys=1, is_stable=False)
    key, frac, weight = (x.reshape(key_shape) for x in (key, frac, weight))

    table_rows = nvars * plane + BLOCK
    (seen,) = call(
        forward_kernel,
        dims,
        [key.shape],
        [own, scale, side_b, key, frac],
        [perturb],
        [key] + rates,
        [
            pltpu.VMEM(whole, jnp.float32),
            pltpu.VMEM((table_rows, 2 * cells), jnp.bfloat16),
            pltpu.VMEM(perturb.shape, perturb.dtype),
            pltpu.SemaphoreType.DMA((members, nvars)),
        ],
    )
    seen = summands(seen)
    source, side_a, side_b, gradient = call(
        scatter_kernel,
        dims,
        [(members, plane, cells), strip, strip, (table_rows, cells)],
        [key, frac, weight, perturb, scale] + seen,
        [],
        [key],
        [pltpu.VMEM(key.shape, jnp.float32)],
    )
    side_a, side_b = exchange(side_a, side_b)
    (own,) = call(local_kernel, dims, [whole], [powers, source, gradient, scale, side_a], [ens, stat], rates, [pltpu.VMEM(whole, jnp.float32)] + copying)
    hv_ens, hv_stat = call(
        edge_kernel,
        dims,
        [(members, plane, cells), (nvars, plane, cells)],
        [own, side_b],
        [],
        rates,
        [pltpu.VMEM(whole, jnp.float32), pltpu.SemaphoreType.DMA((fields,))],
        HBM,
    )
    return hv_ens.reshape(ens_control.shape), hv_stat.reshape(static_control.shape)


def solution(mesh):
    placed = (
        P("grp", None, "tile", None),
        P("grp", None, None, "tile", None),
        P("grp", None, None, "tile", None),
        P("grp"),
        P(),
        P("grp"),
        P("grp", None, None),
        P("tile"),
        P("tile"),
        P("tile"),
        P("tile"),
        P(),
    )
    return jax.shard_map(
        per_device,
        mesh=mesh,
        in_specs=placed,
        out_specs=(P("grp", None, "tile", None), P("grp", None, None, "tile", None)),
        check_vma=False,
    )
```

```python
import math

import jax
import jax.numpy as jnp
import numpy as np
from jax import lax
from jax.experimental import pallas as pl
from jax.experimental.pallas import tpu as pltpu
from jax.sharding import PartitionSpec as P

SWEEPS = 4
BLOCK = 256
ALIGN = 16


def along_x(planes, wanted, rows, rate, inside):
    factors = [(1.0 - 4.0 * rate, rate)] * 3
    if inside is not None:
        factors[1:] = [((1.0 - 4.0 * rate) * side, rate * side) for side in inside]
    result = {}
    for x in wanted:
        keep, share = factors[1 if x < 0 else 2 if x >= rows else 0]
        total = None
        for near in (x - 1, x + 1):
            if near in planes:
                total = planes[near] if total is None else total + planes[near]
        if total is not None:
            total = share * total
        if x in planes:
            total = keep * planes[x] if total is None else keep * planes[x] + total
        if total is not None:
            result[x] = total
    return result


def powers_along_x(planes, first, last, rows, rate, inside):
    stages = [planes]
    for left in range(SWEEPS - 1, -1, -1):
        stages.append(along_x(stages[-1], range(first - left, last + left + 1), rows, rate, inside))
    return stages


def binomial(j, rate):
    factor = float(math.comb(SWEEPS, j))
    for number in range(j):
        factor = factor * rate
    return factor


def along_y(value):
    cells = value.shape[1]
    lane = lax.broadcasted_iota(jnp.int32, value.shape, 1)
    below = jnp.where(lane == 0, 0.0, pltpu.roll(value, 1, 1))
    return below + jnp.where(lane == cells - 1, 0.0, pltpu.roll(value, cells - 1, 1))


def spread_rolled(planes, first, last, rows, rate, inside):
    stages = powers_along_x(planes, first, last, rows, rate, inside)
    result = {}
    for x in range(first, last + 1):
        total = None
        for j in range(SWEEPS, -1, -1):
            if total is not None:
                total = along_y(total)
            term = stages[SWEEPS - j].get(x)
            if term is not None:
                term = term if j == 0 else binomial(j, rate) * term
                total = term if total is None else total + term
        result[x] = total
    return result


def halves(value):
    high = value.astype(jnp.bfloat16)
    low = (value - high.astype(jnp.float32)).astype(jnp.bfloat16)
    return high, low


def y_powers(cells):
    once = np.eye(cells, k=1) + np.eye(cells, k=-1)
    row = [math.comb(SWEEPS, j) * np.linalg.matrix_power(once, j) for j in range(1, SWEEPS + 1)]
    return jnp.asarray(np.concatenate([np.concatenate(row, axis=1)] * 2, axis=0), jnp.bfloat16)


GROUP = 8


def spread_product(planes, rows, rate, inside, powers, scale=None):
    levels, cells = planes[0].shape
    terms = [{} for j in range(SWEEPS)]
    for first in range(0, rows, GROUP):
        both = jnp.concatenate(halves(jnp.concatenate([planes[x] for x in range(first, first + GROUP)], axis=0)), axis=1)
        product = jnp.dot(both, powers[...], preferred_element_type=jnp.float32)
        for at in range(GROUP):
            for j in range(SWEEPS):
                terms[j][first + at] = product[at * levels : (at + 1) * levels, j * cells : (j + 1) * cells]
    own = jnp.broadcast_to(1.0 / jnp.full((8, cells), rate, jnp.float32) - 4.0, (levels // 8, 8, cells)).reshape(levels, cells)
    result = planes
    for j in range(1, SWEEPS + 1):
        left = SWEEPS - j
        before, result = result, {}
        for x in range(-left, rows + left):
            total = terms[j - 1].get(x)
            for near in (x - 1, x + 1):
                if near in before:
                    total = before[near] if total is None else total + before[near]
            if x in before:
                total = own * before[x] if total is None else total + own * before[x]
            if total is not None:
                result[x] = total * inside[0] if x < 0 else total * inside[1] if x >= rows else total
    fourth = rate * rate * (rate * rate)
    return {x: value * (fourth if scale is None else fourth * scale) for x, value in result.items()}


def rate_of(field, members, group, localize, static):
    member = jnp.minimum(field, members - 1)
    return jnp.where(field < members, localize[group[member]], static[0])


def rates_of(fields, members, group, localize, static):
    return [rate_of(field, members, group, localize, static) for field in range(fields)]


def neighbours():
    tile = lax.axis_index("tile")
    last = lax.axis_size("tile") - 1
    return jnp.where(tile > 0, 1.0, 0.0), jnp.where(tile < last, 1.0, 0.0)


def is_even():
    return lax.axis_index("tile") % 2 == 0


def begins(rows):
    even = is_even()
    return jnp.where(even, rows - SWEEPS, 0), jnp.where(even, 0, rows - SWEEPS)


def add_side(side, upper, rates, shape, visit, counts=None, batch=None):
    levels, rows, cells = shape
    batch = batch or len(rates)
    for first in range(0, len(rates), batch):
        fields = range(first, min(first + batch, len(rates)))
        rate = jnp.concatenate([jnp.full((levels, cells), rates[field], jnp.float32) for field in fields], axis=0)
        planes = {}
        for away in range(1, SWEEPS + 1):
            j = jnp.where(upper, away - 1, SWEEPS - away)
            planes[-away] = side[j, first * levels : (first + len(fields)) * levels, :]
        parts = spread_rolled(planes, 0, SWEEPS - 1, rows, rate, None)
        for at, field in enumerate(fields):
            for depth in range(SWEEPS):
                part = parts[depth][at * levels : (at + 1) * levels]
                visit(field, depth, part if counts is None else part * counts)


def adder(into, upper, shape, scale=None):
    levels, rows, cells = shape

    def visit(field, depth, part):
        at = pl.ds(jnp.where(upper, rows - 1 - depth, depth), levels, stride=rows)
        into[field, at, :] = into[field, at, :] + (part if scale is None else part * scale[field])

    return visit


def add_near(into, side, rates, shape, scale=None):
    upper = is_even()
    add_side(side, upper, rates, shape, adder(into, upper, shape, scale))


def add_far(into, side, rates, shape, scale=None):
    upper = jnp.logical_not(is_even())
    below, above = neighbours()
    add_side(side, upper, rates, shape, adder(into, upper, shape, scale), below * above)


def block_of(ref, block):
    lanes = ref.shape[1]
    parts = BLOCK // lanes
    return jnp.concatenate([ref[pl.ds(block * parts + part, 1), :] for part in range(parts)], axis=1)


def weights_of(key, frac, cells):
    cell = key & (cells - 1)
    second = (cell + 1) & (cells - 1)
    spot = lax.broadcasted_iota(jnp.int32, (cells, key.shape[1]), 0)
    return jnp.where(spot == cell, 1.0 - frac, jnp.where(spot == second, frac, 0.0))


def chosen_rows(key, start, shift):
    row = ((key >> shift) - start).astype(jnp.int16)
    spot = lax.broadcasted_iota(jnp.int16, (BLOCK, key.shape[1]), 0)
    return jnp.where(spot == row, jnp.bfloat16(1), jnp.bfloat16(0))


def window_of(bound, block, cells):
    parts = BLOCK // bound.shape[1]
    shift = cells.bit_length() - 1
    start = ((bound[block * parts, 0] >> shift) // ALIGN) * ALIGN
    last = bound[block * parts + parts - 1, bound.shape[1] - 1] >> shift
    return start, (last - start) // BLOCK + 1


def every_window(bound, blocks, cells, visit, visit_again):
    most = 1
    for block in range(blocks):
        start, count = window_of(bound, block, cells)
        most = jnp.maximum(most, count)
        visit(block, start)

    @pl.when(most > 1)
    def _():
        def of_block(block, carry):
            start, count = window_of(bound, block, cells)

            def of_window(window, inner):
                visit_again(block, start + window * BLOCK)
                return inner

            return lax.fori_loop(1, count, of_window, carry)

        lax.fori_loop(0, blocks, of_block, 0)


def each_field(fields, visit, unroll=1):
    def step(field, carry):
        visit(field)
        return carry

    lax.fori_loop(0, fields, step, 0, unroll=unroll)


def load_of(field, source, at, held, sems):
    return pltpu.make_async_copy(source.at[at], held.at[field], sems.at[field])


def start_loads(members, nvars, ens, stat, held, sems):
    for m in range(members):
        load_of(m, ens, m, held, sems).start()
    for v in range(nvars):
        load_of(members + v, stat, v, held, sems).start()


def pack_kernel(dims, ens, stat, side_a, side_b, held, sems):
    members, nvars, levels, rows, cells, blocks = dims
    start_loads(members, nvars, ens, stat, held, sems)
    for field in range(members + nvars):
        load_of(field, ens, 0, held, sems).wait()
        for begin, side in zip(begins(rows), (side_a, side_b)):
            for j in range(SWEEPS):
                side[j, pl.ds(field * levels, levels), :] = held[field, pl.ds(begin + j, levels, stride=rows), :]


def own_kernel(dims, powers, held, scale, side_a, layer, index, kind, group, localize, static, precision, out, key, weight):
    members, nvars, levels, rows, cells, blocks = dims
    inside = neighbours()

    def of_field(field):
        planes = {x: held[field, pl.ds(x, levels, stride=rows), :] for x in range(rows)}
        rate = rate_of(field, members, group, localize, static)
        planes = spread_product(planes, rows, rate, inside, powers, scale[field])
        for x in range(rows):
            out[field, pl.ds(x, levels, stride=rows), :] = planes[x]

    each_field(members + nvars, of_field, members + nvars)
    rates = rates_of(members + nvars, members, group, localize, static)
    add_near(out, side_a, rates, (levels, rows, cells), scale)
    key[...] = layer[...] * (rows * cells) + index[...]
    total = jnp.zeros(kind.shape, jnp.float32)
    for k in range(precision.shape[0]):
        total = jnp.where(kind[...] == k, precision[k], total)
    weight[...] = total


def forward_kernel(dims, own, scale, side_b, key, frac, perturb_far, bound, group, localize, static, out, smooth, table, perturb, sem):
    members, nvars, levels, rows, cells, blocks = dims
    shift = cells.bit_length() - 1
    loads = [pltpu.make_async_copy(perturb_far.at[m, v], perturb.at[m, v], sem.at[m, v]) for v in range(nvars) for m in range(members)]
    for load in loads:
        load.start()

    smooth[...] = own[...]
    rates = rates_of(members + nvars, members, group, localize, static)
    add_far(smooth, side_b, rates, (levels, rows, cells), scale)
    plane = levels * rows
    for v in range(nvars):
        total = smooth[members + v]
        for m in range(members):
            loads[v * members + m].wait()
            total = total + perturb[m, v].astype(jnp.float32) * smooth[m]
        high, low = halves(total)
        table[v * plane : (v + 1) * plane, :cells] = high
        table[v * plane : (v + 1) * plane, cells:] = low
    table[nvars * plane :, :] = jnp.zeros((BLOCK, 2 * cells), jnp.bfloat16)
    lanes = key.shape[1]
    parts = BLOCK // lanes

    def seen_in(block, start):
        keys = block_of(key, block)
        picked = lax.dot_general(
            table[pl.ds(pl.multiple_of(start, ALIGN), BLOCK), :],
            chosen_rows(keys, start, shift),
            (((0,), (0,)), ((), ())),
            preferred_element_type=jnp.float32,
        )
        picked = picked[:cells] + picked[cells:]
        return jnp.sum(picked * weights_of(keys, block_of(frac, block), cells), axis=0, keepdims=True)

    def visit(block, start):
        seen = seen_in(block, start)
        for part in range(parts):
            out[pl.ds(block * parts + part, 1), :] = seen[:, part * lanes : (part + 1) * lanes]

    def visit_again(block, start):
        seen = seen_in(block, start)
        for part in range(parts):
            at = pl.ds(block * parts + part, 1)
            out[at, :] = out[at, :] + seen[:, part * lanes : (part + 1) * lanes]

    every_window(bound, blocks, cells, visit, visit_again)


def ready_kernel(dims, key, frac, bound, chosen, spread_out):
    members, nvars, levels, rows, cells, blocks = dims
    shift = cells.bit_length() - 1
    for block in range(blocks):
        start, count = window_of(bound, block, cells)
        keys = block_of(key, block)
        chosen[block] = chosen_rows(keys, start, shift)
        spread_out[block] = weights_of(keys, block_of(frac, block), cells)


def scatter_kernel(dims, chosen, spread_out, key, frac, weight, perturb, scale, *refs):
    members, nvars, levels, rows, cells, blocks = dims
    *seen, bound, source, side_a, side_b, gradient, valued = refs
    shift = cells.bit_length() - 1
    total = seen[0][...]
    for part in seen[1:]:
        total = total + part[...]
    valued[...] = total * weight[...]
    gradient[...] = jnp.zeros(gradient.shape, jnp.float32)

    def add_placed(block, start, taken, places):
        high, low = halves(places * block_of(valued, block))
        both = lax.dot_general(
            taken,
            jnp.concatenate([high, low], axis=0),
            (((1,), (1,)), ((), ())),
            preferred_element_type=jnp.float32,
        )
        at = pl.ds(pl.multiple_of(start, ALIGN), BLOCK)
        gradient[at, :] = gradient[at, :] + (both[:, :cells] + both[:, cells:])

    def add_first(block, start):
        add_placed(block, start, chosen[block], spread_out[block])

    def add_further(block, start):
        keys = block_of(key, block)
        add_placed(block, start, chosen_rows(keys, start, shift), weights_of(keys, block_of(frac, block), cells))

    every_window(bound, blocks, cells, add_first, add_further)

    plane = levels * rows
    for m in range(members):
        total = perturb[m, 0].astype(jnp.float32) * gradient[:plane, :]
        for v in range(1, nvars):
            total = total + perturb[m, v].astype(jnp.float32) * gradient[v * plane : (v + 1) * plane, :]
        source[m] = total
    for begin, side in zip(begins(rows), (side_a, side_b)):
        for field in range(members + nvars):
            for j in range(SWEEPS):
                if field < members:
                    strip = source[field, pl.ds(begin + j, levels, stride=rows), :]
                else:
                    at = (field - members) * plane + begin + j
                    strip = gradient[pl.ds(at, levels, stride=rows), :] * scale[field]
                side[j, pl.ds(field * levels, levels), :] = strip


def local_kernel(dims, powers, source, gradient, scale, side_a, ens, stat, group, localize, static, out, held, sems):
    members, nvars, levels, rows, cells, blocks = dims
    inside = neighbours()
    plane = levels * rows
    start_loads(members, nvars, ens, stat, held, sems)

    def of_field(field, planes):
        rate = rate_of(field, members, group, localize, static)
        planes = spread_product(planes, rows, rate, inside, powers)
        load_of(field, ens, 0, held, sems).wait()
        for x in range(rows):
            at = pl.ds(x, levels, stride=rows)
            out[field, at, :] = held[field, at, :] + planes[x]

    def of_member(m):
        of_field(m, {x: source[m, pl.ds(x, levels, stride=rows), :] for x in range(rows)})

    def of_group(v):
        field = members + v
        planes = {x: gradient[pl.ds(v * plane + x, levels, stride=rows), :] * scale[field] for x in range(rows)}
        of_field(field, planes)

    each_field(members, of_member)
    each_field(nvars, of_group)
    rates = rates_of(members + nvars, members, group, localize, static)
    add_near(out, side_a, rates, (levels, rows, cells))


def edge_kernel(dims, own, side_b, group, localize, static, hv_ens, hv_stat, after, sems):
    members, nvars, levels, rows, cells, blocks = dims

    writes = []
    rates = rates_of(members + nvars, members, group, localize, static)
    upper = jnp.logical_not(is_even())
    add = adder(after, upper, (levels, rows, cells))
    below, above = neighbours()

    def visit(field, depth, part):
        if depth == 0:
            after[field] = own[field]
        add(field, depth, part)
        if depth == SWEEPS - 1:
            out = hv_ens.at[field] if field < members else hv_stat.at[field - members]
            write = pltpu.make_async_copy(after.at[field], out, sems.at[field])
            write.start()
            writes.append(write)

    add_side(side_b, upper, rates, (levels, rows, cells), visit, below * above, 4)
    for write in writes:
        write.wait()


def exchange(side_a, side_b):
    count = lax.axis_size("tile")
    pairs_a = [(i, i ^ 1) for i in range(count)]
    pairs_b = [(i, (((i + 1) ^ 1) - 1) % count) for i in range(count)]
    return lax.ppermute(side_a, "tile", pairs_a), lax.ppermute(side_b, "tile", pairs_b)


def summands(value):
    count = lax.axis_size("grp")
    value = value + lax.ppermute(value, "grp", [(i, i ^ 1) for i in range(count)])
    turns = [2, 6, 4] if count == 8 else list(range(2, count, 2))
    return [value] + [lax.ppermute(value, "grp", [(i, i ^ turn) for i in range(count)]) for turn in turns]


VMEM = pl.BlockSpec(memory_space=pltpu.VMEM)
SMEM = pl.BlockSpec(memory_space=pltpu.SMEM)
HBM = pl.BlockSpec(memory_space=pltpu.HBM)


def call(kernel, dims, outs, ins, far=(), scalars=(), scratch=(), out_spec=VMEM, kinds=None, cost=2_000_000):
    def body(*refs):
        kernel(dims, *refs)

    far = [pltpu.with_memory_space_constraint(x, pltpu.HBM) for x in far]
    return pl.pallas_call(
        body,
        out_shape=tuple(jax.ShapeDtypeStruct(tuple(shape), kind) for shape, kind in zip(outs, kinds or [jnp.float32] * len(outs))),
        in_specs=[VMEM] * len(ins) + [HBM] * len(far) + [SMEM] * len(scalars),
        out_specs=tuple([out_spec] * len(outs)),
        scratch_shapes=list(scratch),
        compiler_params=pltpu.CompilerParams(vmem_limit_bytes=16 * 1024 * 1024),
        cost_estimate=pl.CostEstimate(flops=cost * 10, bytes_accessed=cost, transcendentals=0),
        name=kernel.__name__,
    )(*ins, *far, *scalars)


def per_device(
    ens_control,
    static_control,
    member_perturb,
    member_group,
    localize_rate,
    static_rate,
    static_scale,
    obs_index,
    obs_frac,
    obs_layer,
    obs_kind,
    obs_precision,
):
    members, levels, rows, cells = ens_control.shape
    nvars = static_control.shape[1]
    fields = members + nvars
    blocks = obs_index.shape[0] // BLOCK
    dims = (members, nvars, levels, rows, cells, blocks)
    plane = levels * rows
    strip = (SWEEPS, fields * levels, cells)

    ens = ens_control.reshape(members, plane, cells)
    stat = static_control.reshape(nvars, plane, cells)
    perturb = member_perturb.reshape(members, nvars, plane, cells)
    rates = [member_group, localize_rate, static_rate]

    whole = (fields, plane, cells)
    key_shape = (obs_index.shape[0] // cells, cells)
    powers = y_powers(cells)
    copying = [pltpu.SemaphoreType.DMA((fields,))]
    side_a, side_b, held = call(pack_kernel, dims, [strip, strip, whole], [], [ens, stat], [], copying)
    side_a, side_b = exchange(side_a, side_b)

    scale = jnp.concatenate([jnp.ones((members, levels), jnp.float32), static_scale[0]])
    scale = jnp.broadcast_to(scale[:, :, None], (fields, levels, cells))
    layer, index, kind = (x.reshape(-1, cells) for x in (obs_layer, obs_index, obs_kind))
    own, key, weight = call(
        own_kernel,
        dims,
        [whole, key_shape, key_shape],
        [powers, held, scale, side_a, layer, index, kind],
        [],
        rates + [obs_precision],
        kinds=[jnp.float32, jnp.int32, jnp.float32],
    )
    key, frac, weight = lax.sort((key.reshape(-1), obs_frac, weight.reshape(-1)), num_keys=1, is_stable=False)
    key, frac, weight = (x.reshape(key_shape) for x in (key, frac, weight))

    table_rows = nvars * plane + BLOCK
    (seen,) = call(
        forward_kernel,
        dims,
        [key.shape],
        [own, scale, side_b, key, frac],
        [perturb],
        [key] + rates,
        [
            pltpu.VMEM(whole, jnp.float32),
            pltpu.VMEM((table_rows, 2 * cells), jnp.bfloat16),
            pltpu.VMEM(perturb.shape, perturb.dtype),
            pltpu.SemaphoreType.DMA((members, nvars)),
        ],
    )
    seen = summands(seen)
    chosen, spread_out = call(
        ready_kernel,
        dims,
        [(blocks, BLOCK, BLOCK), (blocks, cells, BLOCK)],
        [key, frac],
        [],
        [key],
        kinds=[jnp.bfloat16, jnp.float32],
    )
    source, side_a, side_b, gradient = call(
        scatter_kernel,
        dims,
        [(members, plane, cells), strip, strip, (table_rows, cells)],
        [chosen, spread_out, key, frac, weight, perturb, scale] + seen,
        [],
        [key],
        [pltpu.VMEM(key.shape, jnp.float32)],
    )
    side_a, side_b = exchange(side_a, side_b)
    (own,) = call(local_kernel, dims, [whole], [powers, source, gradient, scale, side_a], [ens, stat], rates, [pltpu.VMEM(whole, jnp.float32)] + copying)
    hv_ens, hv_stat = call(
        edge_kernel,
        dims,
        [(members, plane, cells), (nvars, plane, cells)],
        [own, side_b],
        [],
        rates,
        [pltpu.VMEM(whole, jnp.float32), pltpu.SemaphoreType.DMA((fields,))],
        HBM,
    )
    return hv_ens.reshape(ens_control.shape), hv_stat.reshape(static_control.shape)


def solution(mesh):
    placed = (
        P("grp", None, "tile", None),
        P("grp", None, None, "tile", None),
        P("grp", None, None, "tile", None),
        P("grp"),
        P(),
        P("grp"),
        P("grp", None, None),
        P("tile"),
        P("tile"),
        P("tile"),
        P("tile"),
        P(),
    )
    return jax.shard_map(
        per_device,
        mesh=mesh,
        in_specs=placed,
        out_specs=(P("grp", None, "tile", None), P("grp", None, None, "tile", None)),
        check_vma=False,
    )
```

```python
import math

import jax
import jax.numpy as jnp
import numpy as np
from jax import lax
from jax.experimental import pallas as pl
from jax.experimental.pallas import tpu as pltpu
from jax.sharding import PartitionSpec as P

SWEEPS = 4
BLOCK = 256
ALIGN = 16


def along_x(planes, wanted, rows, rate, inside):
    factors = [(1.0 - 4.0 * rate, rate)] * 3
    if inside is not None:
        factors[1:] = [((1.0 - 4.0 * rate) * side, rate * side) for side in inside]
    result = {}
    for x in wanted:
        keep, share = factors[1 if x < 0 else 2 if x >= rows else 0]
        total = None
        for near in (x - 1, x + 1):
            if near in planes:
                total = planes[near] if total is None else total + planes[near]
        if total is not None:
            total = share * total
        if x in planes:
            total = keep * planes[x] if total is None else keep * planes[x] + total
        if total is not None:
            result[x] = total
    return result


def powers_along_x(planes, first, last, rows, rate, inside):
    stages = [planes]
    for left in range(SWEEPS - 1, -1, -1):
        stages.append(along_x(stages[-1], range(first - left, last + left + 1), rows, rate, inside))
    return stages


def binomial(j, rate):
    factor = float(math.comb(SWEEPS, j))
    for number in range(j):
        factor = factor * rate
    return factor


def along_y(value):
    cells = value.shape[1]
    lane = lax.broadcasted_iota(jnp.int32, value.shape, 1)
    below = jnp.where(lane == 0, 0.0, pltpu.roll(value, 1, 1))
    return below + jnp.where(lane == cells - 1, 0.0, pltpu.roll(value, cells - 1, 1))


def spread_rolled(planes, first, last, rows, rate, inside):
    stages = powers_along_x(planes, first, last, rows, rate, inside)
    result = {}
    for x in range(first, last + 1):
        total = None
        for j in range(SWEEPS, -1, -1):
            if total is not None:
                total = along_y(total)
            term = stages[SWEEPS - j].get(x)
            if term is not None:
                term = term if j == 0 else binomial(j, rate) * term
                total = term if total is None else total + term
        result[x] = total
    return result


def halves(value):
    high = value.astype(jnp.bfloat16)
    low = (value - high.astype(jnp.float32)).astype(jnp.bfloat16)
    return high, low


def y_powers(cells):
    once = np.eye(cells, k=1) + np.eye(cells, k=-1)
    row = [math.comb(SWEEPS, j) * np.linalg.matrix_power(once, j) for j in range(1, SWEEPS + 1)]
    return jnp.asarray(np.concatenate([np.concatenate(row, axis=1)] * 2, axis=0), jnp.bfloat16)


GROUP = 8


def spread_product(planes, rows, rate, inside, powers, scale=None):
    levels, cells = planes[0].shape
    terms = [{} for j in range(SWEEPS)]
    for first in range(0, rows, GROUP):
        both = jnp.concatenate(halves(jnp.concatenate([planes[x] for x in range(first, first + GROUP)], axis=0)), axis=1)
        product = jnp.dot(both, powers[...], preferred_element_type=jnp.float32)
        for at in range(GROUP):
            for j in range(SWEEPS):
                terms[j][first + at] = product[at * levels : (at + 1) * levels, j * cells : (j + 1) * cells]
    own = jnp.broadcast_to(1.0 / jnp.full((8, cells), rate, jnp.float32) - 4.0, (levels // 8, 8, cells)).reshape(levels, cells)
    result = planes
    for j in range(1, SWEEPS + 1):
        left = SWEEPS - j
        before, result = result, {}
        for x in range(-left, rows + left):
            total = terms[j - 1].get(x)
            for near in (x - 1, x + 1):
                if near in before:
                    total = before[near] if total is None else total + before[near]
            if x in before:
                total = own * before[x] if total is None else total + own * before[x]
            if total is not None:
                result[x] = total * inside[0] if x < 0 else total * inside[1] if x >= rows else total
    fourth = rate * rate * (rate * rate)
    return {x: value * (fourth if scale is None else fourth * scale) for x, value in result.items()}


def rate_of(field, members, group, localize, static):
    member = jnp.minimum(field, members - 1)
    return jnp.where(field < members, localize[group[member]], static[0])


def rates_of(fields, members, group, localize, static):
    return [rate_of(field, members, group, localize, static) for field in range(fields)]


def neighbours():
    tile = lax.axis_index("tile")
    last = lax.axis_size("tile") - 1
    return jnp.where(tile > 0, 1.0, 0.0), jnp.where(tile < last, 1.0, 0.0)


def is_even():
    return lax.axis_index("tile") % 2 == 0


def begins(rows):
    even = is_even()
    return jnp.where(even, rows - SWEEPS, 0), jnp.where(even, 0, rows - SWEEPS)


def add_side(side, upper, rates, shape, visit, counts=None, batch=None):
    levels, rows, cells = shape
    batch = batch or len(rates)
    for first in range(0, len(rates), batch):
        fields = range(first, min(first + batch, len(rates)))
        rate = jnp.concatenate([jnp.full((levels, cells), rates[field], jnp.float32) for field in fields], axis=0)
        planes = {}
        for away in range(1, SWEEPS + 1):
            j = jnp.where(upper, away - 1, SWEEPS - away)
            planes[-away] = side[j, first * levels : (first + len(fields)) * levels, :]
        parts = spread_rolled(planes, 0, SWEEPS - 1, rows, rate, None)
        for at, field in enumerate(fields):
            for depth in range(SWEEPS):
                part = parts[depth][at * levels : (at + 1) * levels]
                visit(field, depth, part if counts is None else part * counts)


def adder(into, upper, shape, scale=None):
    levels, rows, cells = shape

    def visit(field, depth, part):
        at = pl.ds(jnp.where(upper, rows - 1 - depth, depth), levels, stride=rows)
        into[field, at, :] = into[field, at, :] + (part if scale is None else part * scale[field])

    return visit


def add_near(into, side, rates, shape, scale=None):
    upper = is_even()
    add_side(side, upper, rates, shape, adder(into, upper, shape, scale))


def add_far(into, side, rates, shape, scale=None):
    upper = jnp.logical_not(is_even())
    below, above = neighbours()
    add_side(side, upper, rates, shape, adder(into, upper, shape, scale), below * above)


def block_of(ref, block):
    lanes = ref.shape[1]
    parts = BLOCK // lanes
    return jnp.concatenate([ref[pl.ds(block * parts + part, 1), :] for part in range(parts)], axis=1)


def weights_of(key, frac, cells):
    cell = key & (cells - 1)
    second = (cell + 1) & (cells - 1)
    spot = lax.broadcasted_iota(jnp.int32, (cells, key.shape[1]), 0)
    return jnp.where(spot == cell, 1.0 - frac, jnp.where(spot == second, frac, 0.0))


def chosen_rows(key, start, shift):
    row = ((key >> shift) - start).astype(jnp.int16)
    spot = lax.broadcasted_iota(jnp.int16, (BLOCK, key.shape[1]), 0)
    return jnp.where(spot == row, jnp.bfloat16(1), jnp.bfloat16(0))


def window_of(bound, block, cells):
    parts = BLOCK // bound.shape[1]
    shift = cells.bit_length() - 1
    start = ((bound[block * parts, 0] >> shift) // ALIGN) * ALIGN
    last = bound[block * parts + parts - 1, bound.shape[1] - 1] >> shift
    return start, (last - start) // BLOCK + 1


def every_window(bound, blocks, cells, visit, visit_again):
    most = 1
    for block in range(blocks):
        start, count = window_of(bound, block, cells)
        most = jnp.maximum(most, count)
        visit(block, start)

    @pl.when(most > 1)
    def _():
        def of_block(block, carry):
            start, count = window_of(bound, block, cells)

            def of_window(window, inner):
                visit_again(block, start + window * BLOCK)
                return inner

            return lax.fori_loop(1, count, of_window, carry)

        lax.fori_loop(0, blocks, of_block, 0)


def each_field(fields, visit, unroll=1):
    def step(field, carry):
        visit(field)
        return carry

    lax.fori_loop(0, fields, step, 0, unroll=unroll)


def load_of(field, source, at, held, sems):
    return pltpu.make_async_copy(source.at[at], held.at[field], sems.at[field])


def start_loads(members, nvars, ens, stat, held, sems):
    for m in range(members):
        load_of(m, ens, m, held, sems).start()
    for v in range(nvars):
        load_of(members + v, stat, v, held, sems).start()


def pack_kernel(dims, ens, stat, side_a, side_b, held, sems):
    members, nvars, levels, rows, cells, blocks = dims
    start_loads(members, nvars, ens, stat, held, sems)
    for field in range(members + nvars):
        load_of(field, ens, 0, held, sems).wait()
        for begin, side in zip(begins(rows), (side_a, side_b)):
            for j in range(SWEEPS):
                side[j, pl.ds(field * levels, levels), :] = held[field, pl.ds(begin + j, levels, stride=rows), :]


def own_kernel(dims, powers, held, scale, side_a, layer, index, kind, group, localize, static, precision, out, key, weight):
    members, nvars, levels, rows, cells, blocks = dims
    inside = neighbours()

    def of_field(field):
        planes = {x: held[field, pl.ds(x, levels, stride=rows), :] for x in range(rows)}
        rate = rate_of(field, members, group, localize, static)
        planes = spread_product(planes, rows, rate, inside, powers, scale[field])
        for x in range(rows):
            out[field, pl.ds(x, levels, stride=rows), :] = planes[x]

    each_field(members + nvars, of_field, members + nvars)
    rates = rates_of(members + nvars, members, group, localize, static)
    add_near(out, side_a, rates, (levels, rows, cells), scale)
    key[...] = layer[...] * (rows * cells) + index[...]
    total = jnp.zeros(kind.shape, jnp.float32)
    for k in range(precision.shape[0]):
        total = jnp.where(kind[...] == k, precision[k], total)
    weight[...] = total


def forward_kernel(dims, own, scale, side_b, key, frac, perturb_far, bound, group, localize, static, out, smooth, table, perturb, sem):
    members, nvars, levels, rows, cells, blocks = dims
    shift = cells.bit_length() - 1
    loads = [pltpu.make_async_copy(perturb_far.at[m, v], perturb.at[m, v], sem.at[m, v]) for v in range(nvars) for m in range(members)]
    for load in loads:
        load.start()

    smooth[...] = own[...]
    rates = rates_of(members + nvars, members, group, localize, static)
    add_far(smooth, side_b, rates, (levels, rows, cells), scale)
    plane = levels * rows
    for v in range(nvars):
        total = smooth[members + v]
        for m in range(members):
            loads[v * members + m].wait()
            total = total + perturb[m, v].astype(jnp.float32) * smooth[m]
        high, low = halves(total)
        table[v * plane : (v + 1) * plane, :cells] = high
        table[v * plane : (v + 1) * plane, cells:] = low
    table[nvars * plane :, :] = jnp.zeros((BLOCK, 2 * cells), jnp.bfloat16)
    lanes = key.shape[1]
    parts = BLOCK // lanes

    def seen_in(block, start):
        keys = block_of(key, block)
        picked = lax.dot_general(
            table[pl.ds(pl.multiple_of(start, ALIGN), BLOCK), :],
            chosen_rows(keys, start, shift),
            (((0,), (0,)), ((), ())),
            preferred_element_type=jnp.float32,
        )
        picked = picked[:cells] + picked[cells:]
        return jnp.sum(picked * weights_of(keys, block_of(frac, block), cells), axis=0, keepdims=True)

    def visit(block, start):
        seen = seen_in(block, start)
        for part in range(parts):
            out[pl.ds(block * parts + part, 1), :] = seen[:, part * lanes : (part + 1) * lanes]

    def visit_again(block, start):
        seen = seen_in(block, start)
        for part in range(parts):
            at = pl.ds(block * parts + part, 1)
            out[at, :] = out[at, :] + seen[:, part * lanes : (part + 1) * lanes]

    every_window(bound, blocks, cells, visit, visit_again)


def ready_kernel(dims, key, frac, perturb, bound, chosen, spread_out, strips, wide):
    members, nvars, levels, rows, cells, blocks = dims
    shift = cells.bit_length() - 1
    for block in range(blocks):
        start, count = window_of(bound, block, cells)
        keys = block_of(key, block)
        chosen[block] = chosen_rows(keys, start, shift)
        spread_out[block] = weights_of(keys, block_of(frac, block), cells)
    for m in range(members):
        for v in range(nvars):
            wide[m, v] = perturb[m, v].astype(jnp.float32)
            for number, begin in enumerate(begins(rows)):
                for j in range(SWEEPS):
                    strips[m, v, number * SWEEPS + j] = wide[m, v, pl.ds(begin + j, levels, stride=rows), :]


def scatter_kernel(dims, chosen, spread_out, strips, key, frac, weight, scale, *refs):
    members, nvars, levels, rows, cells, blocks = dims
    *seen, bound, side_a, side_b, gradient, valued = refs
    shift = cells.bit_length() - 1
    total = seen[0][...]
    for part in seen[1:]:
        total = total + part[...]
    valued[...] = total * weight[...]
    gradient[...] = jnp.zeros(gradient.shape, jnp.float32)

    def add_placed(block, start, taken, places):
        high, low = halves(places * block_of(valued, block))
        both = lax.dot_general(
            taken,
            jnp.concatenate([high, low], axis=0),
            (((1,), (1,)), ((), ())),
            preferred_element_type=jnp.float32,
        )
        at = pl.ds(pl.multiple_of(start, ALIGN), BLOCK)
        gradient[at, :] = gradient[at, :] + (both[:, :cells] + both[:, cells:])

    def add_first(block, start):
        add_placed(block, start, chosen[block], spread_out[block])

    def add_further(block, start):
        keys = block_of(key, block)
        add_placed(block, start, chosen_rows(keys, start, shift), weights_of(keys, block_of(frac, block), cells))

    every_window(bound, blocks, cells, add_first, add_further)

    plane = levels * rows
    for number, (begin, side) in enumerate(zip(begins(rows), (side_a, side_b))):
        for j in range(SWEEPS):
            near = [gradient[pl.ds(v * plane + begin + j, levels, stride=rows), :] for v in range(nvars)]
            for m in range(members):
                total = strips[m, 0, number * SWEEPS + j] * near[0]
                for v in range(1, nvars):
                    total = total + strips[m, v, number * SWEEPS + j] * near[v]
                side[j, pl.ds(m * levels, levels), :] = total
            for v in range(nvars):
                field = members + v
                side[j, pl.ds(field * levels, levels), :] = near[v] * scale[field]


def local_kernel(dims, powers, gradient, scale, side_a, perturb, ens, stat, group, localize, static, out, held, source, sems):
    members, nvars, levels, rows, cells, blocks = dims
    inside = neighbours()
    plane = levels * rows
    start_loads(members, nvars, ens, stat, held, sems)
    for m in range(members):
        total = perturb[m, 0].astype(jnp.float32) * gradient[:plane, :]
        for v in range(1, nvars):
            total = total + perturb[m, v].astype(jnp.float32) * gradient[v * plane : (v + 1) * plane, :]
        source[m] = total

    def of_field(field, planes):
        rate = rate_of(field, members, group, localize, static)
        planes = spread_product(planes, rows, rate, inside, powers)
        load_of(field, ens, 0, held, sems).wait()
        for x in range(rows):
            at = pl.ds(x, levels, stride=rows)
            out[field, at, :] = held[field, at, :] + planes[x]

    def of_member(m):
        of_field(m, {x: source[m, pl.ds(x, levels, stride=rows), :] for x in range(rows)})

    def of_group(v):
        field = members + v
        planes = {x: gradient[pl.ds(v * plane + x, levels, stride=rows), :] * scale[field] for x in range(rows)}
        of_field(field, planes)

    each_field(members, of_member)
    each_field(nvars, of_group)
    rates = rates_of(members + nvars, members, group, localize, static)
    add_near(out, side_a, rates, (levels, rows, cells))


def edge_kernel(dims, own, side_b, group, localize, static, hv_ens, hv_stat, after, sems):
    members, nvars, levels, rows, cells, blocks = dims

    writes = []
    rates = rates_of(members + nvars, members, group, localize, static)
    upper = jnp.logical_not(is_even())
    add = adder(after, upper, (levels, rows, cells))
    below, above = neighbours()

    def visit(field, depth, part):
        if depth == 0:
            after[field] = own[field]
        add(field, depth, part)
        if depth == SWEEPS - 1:
            out = hv_ens.at[field] if field < members else hv_stat.at[field - members]
            write = pltpu.make_async_copy(after.at[field], out, sems.at[field])
            write.start()
            writes.append(write)

    add_side(side_b, upper, rates, (levels, rows, cells), visit, below * above, 4)
    for write in writes:
        write.wait()


def exchange(side_a, side_b):
    count = lax.axis_size("tile")
    pairs_a = [(i, i ^ 1) for i in range(count)]
    pairs_b = [(i, (((i + 1) ^ 1) - 1) % count) for i in range(count)]
    return lax.ppermute(side_a, "tile", pairs_a), lax.ppermute(side_b, "tile", pairs_b)


def summands(value):
    count = lax.axis_size("grp")
    value = value + lax.ppermute(value, "grp", [(i, i ^ 1) for i in range(count)])
    turns = [2, 6, 4] if count == 8 else list(range(2, count, 2))
    return [value] + [lax.ppermute(value, "grp", [(i, i ^ turn) for i in range(count)]) for turn in turns]


VMEM = pl.BlockSpec(memory_space=pltpu.VMEM)
SMEM = pl.BlockSpec(memory_space=pltpu.SMEM)
HBM = pl.BlockSpec(memory_space=pltpu.HBM)


def call(kernel, dims, outs, ins, far=(), scalars=(), scratch=(), out_spec=VMEM, kinds=None, cost=2_000_000):
    def body(*refs):
        kernel(dims, *refs)

    far = [pltpu.with_memory_space_constraint(x, pltpu.HBM) for x in far]
    return pl.pallas_call(
        body,
        out_shape=tuple(jax.ShapeDtypeStruct(tuple(shape), kind) for shape, kind in zip(outs, kinds or [jnp.float32] * len(outs))),
        in_specs=[VMEM] * len(ins) + [HBM] * len(far) + [SMEM] * len(scalars),
        out_specs=tuple([out_spec] * len(outs)),
        scratch_shapes=list(scratch),
        compiler_params=pltpu.CompilerParams(vmem_limit_bytes=16 * 1024 * 1024),
        cost_estimate=pl.CostEstimate(flops=cost * 10, bytes_accessed=cost, transcendentals=0),
        name=kernel.__name__,
    )(*ins, *far, *scalars)


def per_device(
    ens_control,
    static_control,
    member_perturb,
    member_group,
    localize_rate,
    static_rate,
    static_scale,
    obs_index,
    obs_frac,
    obs_layer,
    obs_kind,
    obs_precision,
):
    members, levels, rows, cells = ens_control.shape
    nvars = static_control.shape[1]
    fields = members + nvars
    blocks = obs_index.shape[0] // BLOCK
    dims = (members, nvars, levels, rows, cells, blocks)
    plane = levels * rows
    strip = (SWEEPS, fields * levels, cells)

    ens = ens_control.reshape(members, plane, cells)
    stat = static_control.reshape(nvars, plane, cells)
    perturb = member_perturb.reshape(members, nvars, plane, cells)
    rates = [member_group, localize_rate, static_rate]

    whole = (fields, plane, cells)
    key_shape = (obs_index.shape[0] // cells, cells)
    powers = y_powers(cells)
    copying = [pltpu.SemaphoreType.DMA((fields,))]
    side_a, side_b, held = call(pack_kernel, dims, [strip, strip, whole], [], [ens, stat], [], copying)
    side_a, side_b = exchange(side_a, side_b)

    scale = jnp.concatenate([jnp.ones((members, levels), jnp.float32), static_scale[0]])
    scale = jnp.broadcast_to(scale[:, :, None], (fields, levels, cells))
    layer, index, kind = (x.reshape(-1, cells) for x in (obs_layer, obs_index, obs_kind))
    own, key, weight = call(
        own_kernel,
        dims,
        [whole, key_shape, key_shape],
        [powers, held, scale, side_a, layer, index, kind],
        [],
        rates + [obs_precision],
        kinds=[jnp.float32, jnp.int32, jnp.float32],
    )
    key, frac, weight = lax.sort((key.reshape(-1), obs_frac, weight.reshape(-1)), num_keys=1, is_stable=False)
    key, frac, weight = (x.reshape(key_shape) for x in (key, frac, weight))

    table_rows = nvars * plane + BLOCK
    (seen,) = call(
        forward_kernel,
        dims,
        [key.shape],
        [own, scale, side_b, key, frac],
        [perturb],
        [key] + rates,
        [
            pltpu.VMEM(whole, jnp.float32),
            pltpu.VMEM((table_rows, 2 * cells), jnp.bfloat16),
            pltpu.VMEM(perturb.shape, perturb.dtype),
            pltpu.SemaphoreType.DMA((members, nvars)),
        ],
    )
    seen = summands(seen)
    chosen, spread_out, strips = call(
        ready_kernel,
        dims,
        [(blocks, BLOCK, BLOCK), (blocks, cells, BLOCK), (members, nvars, 2 * SWEEPS, levels, cells)],
        [key, frac, perturb],
        [],
        [key],
        [pltpu.VMEM((members, nvars, plane, cells), jnp.float32)],
        kinds=[jnp.bfloat16, jnp.float32, jnp.float32],
    )
    side_a, side_b, gradient = call(
        scatter_kernel,
        dims,
        [strip, strip, (table_rows, cells)],
        [chosen, spread_out, strips, key, frac, weight, scale] + seen,
        [],
        [key],
        [pltpu.VMEM(key.shape, jnp.float32)],
    )
    side_a, side_b = exchange(side_a, side_b)
    held_source = [pltpu.VMEM(whole, jnp.float32), pltpu.VMEM((members, plane, cells), jnp.float32)]
    (own,) = call(local_kernel, dims, [whole], [powers, gradient, scale, side_a, perturb], [ens, stat], rates, held_source + copying)
    hv_ens, hv_stat = call(
        edge_kernel,
        dims,
        [(members, plane, cells), (nvars, plane, cells)],
        [own, side_b],
        [],
        rates,
        [pltpu.VMEM(whole, jnp.float32), pltpu.SemaphoreType.DMA((fields,))],
        HBM,
    )
    return hv_ens.reshape(ens_control.shape), hv_stat.reshape(static_control.shape)


def solution(mesh):
    placed = (
        P("grp", None, "tile", None),
        P("grp", None, None, "tile", None),
        P("grp", None, None, "tile", None),
        P("grp"),
        P(),
        P("grp"),
        P("grp", None, None),
        P("tile"),
        P("tile"),
        P("tile"),
        P("tile"),
        P(),
    )
    return jax.shard_map(
        per_device,
        mesh=mesh,
        in_specs=placed,
        out_specs=(P("grp", None, "tile", None), P("grp", None, None, "tile", None)),
        check_vma=False,
    )
```

```python
import math

import jax
import jax.numpy as jnp
import numpy as np
from jax import lax
from jax.experimental import pallas as pl
from jax.experimental.pallas import tpu as pltpu
from jax.sharding import PartitionSpec as P

SWEEPS = 4
BLOCK = 256
ALIGN = 16


def along_x(planes, wanted, rows, rate, inside):
    factors = [(1.0 - 4.0 * rate, rate)] * 3
    if inside is not None:
        factors[1:] = [((1.0 - 4.0 * rate) * side, rate * side) for side in inside]
    result = {}
    for x in wanted:
        keep, share = factors[1 if x < 0 else 2 if x >= rows else 0]
        total = None
        for near in (x - 1, x + 1):
            if near in planes:
                total = planes[near] if total is None else total + planes[near]
        if total is not None:
            total = share * total
        if x in planes:
            total = keep * planes[x] if total is None else keep * planes[x] + total
        if total is not None:
            result[x] = total
    return result


def powers_along_x(planes, first, last, rows, rate, inside):
    stages = [planes]
    for left in range(SWEEPS - 1, -1, -1):
        stages.append(along_x(stages[-1], range(first - left, last + left + 1), rows, rate, inside))
    return stages


def binomial(j, rate):
    factor = float(math.comb(SWEEPS, j))
    for number in range(j):
        factor = factor * rate
    return factor


def along_y(value):
    cells = value.shape[1]
    lane = lax.broadcasted_iota(jnp.int32, value.shape, 1)
    below = jnp.where(lane == 0, 0.0, pltpu.roll(value, 1, 1))
    return below + jnp.where(lane == cells - 1, 0.0, pltpu.roll(value, cells - 1, 1))


def spread_rolled(planes, first, last, rows, rate, inside):
    stages = powers_along_x(planes, first, last, rows, rate, inside)
    result = {}
    for x in range(first, last + 1):
        total = None
        for j in range(SWEEPS, -1, -1):
            if total is not None:
                total = along_y(total)
            term = stages[SWEEPS - j].get(x)
            if term is not None:
                term = term if j == 0 else binomial(j, rate) * term
                total = term if total is None else total + term
        result[x] = total
    return result


def halves(value):
    high = value.astype(jnp.bfloat16)
    low = (value - high.astype(jnp.float32)).astype(jnp.bfloat16)
    return high, low


def y_powers(cells):
    once = np.eye(cells, k=1) + np.eye(cells, k=-1)
    row = [math.comb(SWEEPS, j) * np.linalg.matrix_power(once, j) for j in range(1, SWEEPS + 1)]
    return jnp.asarray(np.concatenate([np.concatenate(row, axis=1)] * 2, axis=0), jnp.bfloat16)


GROUP = 8


def spread_product(planes, rows, rate, inside, powers, scale=None):
    levels, cells = planes[0].shape
    terms = [{} for j in range(SWEEPS)]
    for first in range(0, rows, GROUP):
        both = jnp.concatenate(halves(jnp.concatenate([planes[x] for x in range(first, first + GROUP)], axis=0)), axis=1)
        product = jnp.dot(both, powers[...], preferred_element_type=jnp.float32)
        for at in range(GROUP):
            for j in range(SWEEPS):
                terms[j][first + at] = product[at * levels : (at + 1) * levels, j * cells : (j + 1) * cells]
    own = jnp.broadcast_to(1.0 / jnp.full((8, cells), rate, jnp.float32) - 4.0, (levels // 8, 8, cells)).reshape(levels, cells)
    result = planes
    for j in range(1, SWEEPS + 1):
        left = SWEEPS - j
        before, result = result, {}
        for x in range(-left, rows + left):
            total = terms[j - 1].get(x)
            for near in (x - 1, x + 1):
                if near in before:
                    total = before[near] if total is None else total + before[near]
            if x in before:
                total = own * before[x] if total is None else total + own * before[x]
            if total is not None:
                result[x] = total * inside[0] if x < 0 else total * inside[1] if x >= rows else total
    fourth = rate * rate * (rate * rate)
    return {x: value * (fourth if scale is None else fourth * scale) for x, value in result.items()}


def rate_of(field, members, group, localize, static):
    member = jnp.minimum(field, members - 1)
    return jnp.where(field < members, localize[group[member]], static[0])


def rates_of(fields, members, group, localize, static):
    return [rate_of(field, members, group, localize, static) for field in range(fields)]


def neighbours():
    tile = lax.axis_index("tile")
    last = lax.axis_size("tile") - 1
    return jnp.where(tile > 0, 1.0, 0.0), jnp.where(tile < last, 1.0, 0.0)


def is_even():
    return lax.axis_index("tile") % 2 == 0


def begins(rows):
    even = is_even()
    return jnp.where(even, rows - SWEEPS, 0), jnp.where(even, 0, rows - SWEEPS)


def add_side(side, upper, rates, shape, visit, counts=None, batch=None):
    levels, rows, cells = shape
    batch = batch or len(rates)
    for first in range(0, len(rates), batch):
        fields = range(first, min(first + batch, len(rates)))
        rate = jnp.concatenate([jnp.full((levels, cells), rates[field], jnp.float32) for field in fields], axis=0)
        planes = {}
        for away in range(1, SWEEPS + 1):
            j = jnp.where(upper, away - 1, SWEEPS - away)
            plane = side[j, first * levels : (first + len(fields)) * levels, :]
            planes[-away] = plane if counts is None else plane * counts
        parts = spread_rolled(planes, 0, SWEEPS - 1, rows, rate, None)
        for at, field in enumerate(fields):
            for depth in range(SWEEPS):
                visit(field, depth, parts[depth][at * levels : (at + 1) * levels])


def adder(into, upper, shape, scale=None):
    levels, rows, cells = shape

    def visit(field, depth, part):
        at = pl.ds(jnp.where(upper, rows - 1 - depth, depth), levels, stride=rows)
        into[field, at, :] = into[field, at, :] + (part if scale is None else part * scale[field])

    return visit


def add_near(into, side, rates, shape, scale=None):
    upper = is_even()
    add_side(side, upper, rates, shape, adder(into, upper, shape, scale))


def block_of(ref, block):
    lanes = ref.shape[1]
    parts = BLOCK // lanes
    return jnp.concatenate([ref[pl.ds(block * parts + part, 1), :] for part in range(parts)], axis=1)


def weights_of(key, frac, cells):
    cell = key & (cells - 1)
    second = (cell + 1) & (cells - 1)
    spot = lax.broadcasted_iota(jnp.int32, (cells, key.shape[1]), 0)
    return jnp.where(spot == cell, 1.0 - frac, jnp.where(spot == second, frac, 0.0))


def chosen_rows(key, start, shift):
    row = ((key >> shift) - start).astype(jnp.int16)
    spot = lax.broadcasted_iota(jnp.int16, (BLOCK, key.shape[1]), 0)
    return jnp.where(spot == row, jnp.bfloat16(1), jnp.bfloat16(0))


def window_of(bound, block, cells):
    parts = BLOCK // bound.shape[1]
    shift = cells.bit_length() - 1
    start = ((bound[block * parts, 0] >> shift) // ALIGN) * ALIGN
    last = bound[block * parts + parts - 1, bound.shape[1] - 1] >> shift
    return start, (last - start) // BLOCK + 1


def every_window(bound, blocks, cells, visit, visit_again):
    most = 1
    for block in range(blocks):
        start, count = window_of(bound, block, cells)
        most = jnp.maximum(most, count)
        visit(block, start)

    @pl.when(most > 1)
    def _():
        def of_block(block, carry):
            start, count = window_of(bound, block, cells)

            def of_window(window, inner):
                visit_again(block, start + window * BLOCK)
                return inner

            return lax.fori_loop(1, count, of_window, carry)

        lax.fori_loop(0, blocks, of_block, 0)


def each_field(fields, visit, unroll=1):
    def step(field, carry):
        visit(field)
        return carry

    lax.fori_loop(0, fields, step, 0, unroll=unroll)


def load_of(field, source, at, held, sems):
    return pltpu.make_async_copy(source.at[at], held.at[field], sems.at[field])


def start_loads(members, nvars, ens, stat, held, sems):
    for m in range(members):
        load_of(m, ens, m, held, sems).start()
    for v in range(nvars):
        load_of(members + v, stat, v, held, sems).start()


def pack_kernel(dims, ens, stat, side_a, side_b, held, sems):
    members, nvars, levels, rows, cells, blocks = dims
    start_loads(members, nvars, ens, stat, held, sems)
    for field in range(members + nvars):
        load_of(field, ens, 0, held, sems).wait()
        for begin, side in zip(begins(rows), (side_a, side_b)):
            for j in range(SWEEPS):
                side[j, pl.ds(field * levels, levels), :] = held[field, pl.ds(begin + j, levels, stride=rows), :]


def own_kernel(dims, powers, held, scale, side_a, layer, index, kind, group, localize, static, precision, out, key, weight):
    members, nvars, levels, rows, cells, blocks = dims
    inside = neighbours()

    def of_field(field):
        planes = {x: held[field, pl.ds(x, levels, stride=rows), :] for x in range(rows)}
        rate = rate_of(field, members, group, localize, static)
        planes = spread_product(planes, rows, rate, inside, powers, scale[field])
        for x in range(rows):
            out[field, pl.ds(x, levels, stride=rows), :] = planes[x]

    each_field(members + nvars, of_field, members + nvars)
    rates = rates_of(members + nvars, members, group, localize, static)
    add_near(out, side_a, rates, (levels, rows, cells), scale)
    key[...] = layer[...] * (rows * cells) + index[...]
    total = jnp.zeros(kind.shape, jnp.float32)
    for k in range(precision.shape[0]):
        total = jnp.where(kind[...] == k, precision[k], total)
    weight[...] = total


def forward_kernel(dims, own, scale, side_b, key, frac, perturb_far, bound, group, localize, static, out, smooth, table, perturb, sem):
    members, nvars, levels, rows, cells, blocks = dims
    shift = cells.bit_length() - 1
    loads = [pltpu.make_async_copy(perturb_far.at[m, v], perturb.at[m, v], sem.at[m, v]) for v in range(nvars) for m in range(members)]
    for load in loads:
        load.start()

    rates = rates_of(members + nvars, members, group, localize, static)
    upper = jnp.logical_not(is_even())
    add = adder(smooth, upper, (levels, rows, cells), scale)
    below, above = neighbours()

    def far_part(field, depth, part):
        if depth == 0:
            smooth[field] = own[field]
        add(field, depth, part)

    add_side(side_b, upper, rates, (levels, rows, cells), far_part, below * above)
    plane = levels * rows
    for v in range(nvars):
        total = smooth[members + v]
        for m in range(members):
            loads[v * members + m].wait()
            total = total + perturb[m, v].astype(jnp.float32) * smooth[m]
        high, low = halves(total)
        table[v * plane : (v + 1) * plane, :cells] = high
        table[v * plane : (v + 1) * plane, cells:] = low
    table[nvars * plane :, :] = jnp.zeros((BLOCK, 2 * cells), jnp.bfloat16)
    lanes = key.shape[1]
    parts = BLOCK // lanes

    def seen_in(block, start):
        keys = block_of(key, block)
        picked = lax.dot_general(
            table[pl.ds(pl.multiple_of(start, ALIGN), BLOCK), :],
            chosen_rows(keys, start, shift),
            (((0,), (0,)), ((), ())),
            preferred_element_type=jnp.float32,
        )
        picked = picked[:cells] + picked[cells:]
        return jnp.sum(picked * weights_of(keys, block_of(frac, block), cells), axis=0, keepdims=True)

    def visit(block, start):
        seen = seen_in(block, start)
        for part in range(parts):
            out[pl.ds(block * parts + part, 1), :] = seen[:, part * lanes : (part + 1) * lanes]

    def visit_again(block, start):
        seen = seen_in(block, start)
        for part in range(parts):
            at = pl.ds(block * parts + part, 1)
            out[at, :] = out[at, :] + seen[:, part * lanes : (part + 1) * lanes]

    every_window(bound, blocks, cells, visit, visit_again)


def ready_kernel(dims, key, frac, perturb, bound, chosen, spread_out, strips, wide):
    members, nvars, levels, rows, cells, blocks = dims
    shift = cells.bit_length() - 1
    for block in range(blocks):
        start, count = window_of(bound, block, cells)
        keys = block_of(key, block)
        chosen[block] = chosen_rows(keys, start, shift)
        spread_out[block] = weights_of(keys, block_of(frac, block), cells)
    for m in range(members):
        for v in range(nvars):
            wide[m, v] = perturb[m, v].astype(jnp.float32)
            for number, begin in enumerate(begins(rows)):
                for j in range(SWEEPS):
                    strips[m, v, number * SWEEPS + j] = wide[m, v, pl.ds(begin + j, levels, stride=rows), :]


def scatter_kernel(dims, chosen, spread_out, strips, key, frac, weight, scale, *refs):
    members, nvars, levels, rows, cells, blocks = dims
    *seen, bound, side_a, side_b, gradient, valued = refs
    shift = cells.bit_length() - 1
    total = seen[0][...]
    for part in seen[1:]:
        total = total + part[...]
    valued[...] = total * weight[...]
    gradient[...] = jnp.zeros(gradient.shape, jnp.float32)

    def add_placed(block, start, taken, places):
        high, low = halves(places * block_of(valued, block))
        both = lax.dot_general(
            taken,
            jnp.concatenate([high, low], axis=0),
            (((1,), (1,)), ((), ())),
            preferred_element_type=jnp.float32,
        )
        at = pl.ds(pl.multiple_of(start, ALIGN), BLOCK)
        gradient[at, :] = gradient[at, :] + (both[:, :cells] + both[:, cells:])

    def add_first(block, start):
        add_placed(block, start, chosen[block], spread_out[block])

    def add_further(block, start):
        keys = block_of(key, block)
        add_placed(block, start, chosen_rows(keys, start, shift), weights_of(keys, block_of(frac, block), cells))

    every_window(bound, blocks, cells, add_first, add_further)

    plane = levels * rows
    for number, (begin, side) in enumerate(zip(begins(rows), (side_a, side_b))):
        for j in range(SWEEPS):
            near = [gradient[pl.ds(v * plane + begin + j, levels, stride=rows), :] for v in range(nvars)]
            for m in range(members):
                total = strips[m, 0, number * SWEEPS + j] * near[0]
                for v in range(1, nvars):
                    total = total + strips[m, v, number * SWEEPS + j] * near[v]
                side[j, pl.ds(m * levels, levels), :] = total
            for v in range(nvars):
                field = members + v
                side[j, pl.ds(field * levels, levels), :] = near[v] * scale[field]


def local_kernel(dims, powers, gradient, scale, side_a, perturb, ens, stat, group, localize, static, out, held, source, sems):
    members, nvars, levels, rows, cells, blocks = dims
    inside = neighbours()
    plane = levels * rows
    start_loads(members, nvars, ens, stat, held, sems)
    for m in range(members):
        total = perturb[m, 0].astype(jnp.float32) * gradient[:plane, :]
        for v in range(1, nvars):
            total = total + perturb[m, v].astype(jnp.float32) * gradient[v * plane : (v + 1) * plane, :]
        source[m] = total

    def of_field(field, planes):
        rate = rate_of(field, members, group, localize, static)
        planes = spread_product(planes, rows, rate, inside, powers)
        load_of(field, ens, 0, held, sems).wait()
        for x in range(rows):
            at = pl.ds(x, levels, stride=rows)
            out[field, at, :] = held[field, at, :] + planes[x]

    def of_member(m):
        of_field(m, {x: source[m, pl.ds(x, levels, stride=rows), :] for x in range(rows)})

    def of_group(v):
        field = members + v
        planes = {x: gradient[pl.ds(v * plane + x, levels, stride=rows), :] * scale[field] for x in range(rows)}
        of_field(field, planes)

    each_field(members, of_member)
    each_field(nvars, of_group)
    rates = rates_of(members + nvars, members, group, localize, static)
    add_near(out, side_a, rates, (levels, rows, cells))


def edge_kernel(dims, own, side_b, group, localize, static, hv_ens, hv_stat, after, sems):
    members, nvars, levels, rows, cells, blocks = dims

    writes = []
    rates = rates_of(members + nvars, members, group, localize, static)
    upper = jnp.logical_not(is_even())
    add = adder(after, upper, (levels, rows, cells))
    below, above = neighbours()

    def visit(field, depth, part):
        if depth == 0:
            after[field] = own[field]
        add(field, depth, part)
        if depth == SWEEPS - 1:
            out = hv_ens.at[field] if field < members else hv_stat.at[field - members]
            write = pltpu.make_async_copy(after.at[field], out, sems.at[field])
            write.start()
            writes.append(write)

    add_side(side_b, upper, rates, (levels, rows, cells), visit, below * above, 4)
    for write in writes:
        write.wait()


def exchange(side_a, side_b):
    count = lax.axis_size("tile")
    pairs_a = [(i, i ^ 1) for i in range(count)]
    pairs_b = [(i, (((i + 1) ^ 1) - 1) % count) for i in range(count)]
    return lax.ppermute(side_a, "tile", pairs_a), lax.ppermute(side_b, "tile", pairs_b)


def summands(value):
    count = lax.axis_size("grp")
    value = value + lax.ppermute(value, "grp", [(i, i ^ 1) for i in range(count)])
    turns = [2, 6, 4] if count == 8 else list(range(2, count, 2))
    return [value] + [lax.ppermute(value, "grp", [(i, i ^ turn) for i in range(count)]) for turn in turns]


VMEM = pl.BlockSpec(memory_space=pltpu.VMEM)
SMEM = pl.BlockSpec(memory_space=pltpu.SMEM)
HBM = pl.BlockSpec(memory_space=pltpu.HBM)


def call(kernel, dims, outs, ins, far=(), scalars=(), scratch=(), out_spec=VMEM, kinds=None, cost=2_000_000):
    def body(*refs):
        kernel(dims, *refs)

    far = [pltpu.with_memory_space_constraint(x, pltpu.HBM) for x in far]
    return pl.pallas_call(
        body,
        out_shape=tuple(jax.ShapeDtypeStruct(tuple(shape), kind) for shape, kind in zip(outs, kinds or [jnp.float32] * len(outs))),
        in_specs=[VMEM] * len(ins) + [HBM] * len(far) + [SMEM] * len(scalars),
        out_specs=tuple([out_spec] * len(outs)),
        scratch_shapes=list(scratch),
        compiler_params=pltpu.CompilerParams(vmem_limit_bytes=16 * 1024 * 1024),
        cost_estimate=pl.CostEstimate(flops=cost * 10, bytes_accessed=cost, transcendentals=0),
        name=kernel.__name__,
    )(*ins, *far, *scalars)


def per_device(
    ens_control,
    static_control,
    member_perturb,
    member_group,
    localize_rate,
    static_rate,
    static_scale,
    obs_index,
    obs_frac,
    obs_layer,
    obs_kind,
    obs_precision,
):
    members, levels, rows, cells = ens_control.shape
    nvars = static_control.shape[1]
    fields = members + nvars
    blocks = obs_index.shape[0] // BLOCK
    dims = (members, nvars, levels, rows, cells, blocks)
    plane = levels * rows
    strip = (SWEEPS, fields * levels, cells)

    ens = ens_control.reshape(members, plane, cells)
    stat = static_control.reshape(nvars, plane, cells)
    perturb = member_perturb.reshape(members, nvars, plane, cells)
    rates = [member_group, localize_rate, static_rate]

    whole = (fields, plane, cells)
    key_shape = (obs_index.shape[0] // cells, cells)
    powers = y_powers(cells)
    copying = [pltpu.SemaphoreType.DMA((fields,))]
    side_a, side_b, held = call(pack_kernel, dims, [strip, strip, whole], [], [ens, stat], [], copying)
    side_a, side_b = exchange(side_a, side_b)

    scale = jnp.concatenate([jnp.ones((members, levels), jnp.float32), static_scale[0]])
    scale = jnp.broadcast_to(scale[:, :, None], (fields, levels, cells))
    layer, index, kind = (x.reshape(-1, cells) for x in (obs_layer, obs_index, obs_kind))
    own, key, weight = call(
        own_kernel,
        dims,
        [whole, key_shape, key_shape],
        [powers, held, scale, side_a, layer, index, kind],
        [],
        rates + [obs_precision],
        kinds=[jnp.float32, jnp.int32, jnp.float32],
    )
    key, frac, weight = lax.sort((key.reshape(-1), obs_frac, weight.reshape(-1)), num_keys=1, is_stable=False)
    key, frac, weight = (x.reshape(key_shape) for x in (key, frac, weight))

    table_rows = nvars * plane + BLOCK
    (seen,) = call(
        forward_kernel,
        dims,
        [key.shape],
        [own, scale, side_b, key, frac],
        [perturb],
        [key] + rates,
        [
            pltpu.VMEM(whole, jnp.float32),
            pltpu.VMEM((table_rows, 2 * cells), jnp.bfloat16),
            pltpu.VMEM(perturb.shape, perturb.dtype),
            pltpu.SemaphoreType.DMA((members, nvars)),
        ],
    )
    seen = summands(seen)
    chosen, spread_out, strips = call(
        ready_kernel,
        dims,
        [(blocks, BLOCK, BLOCK), (blocks, cells, BLOCK), (members, nvars, 2 * SWEEPS, levels, cells)],
        [key, frac, perturb],
        [],
        [key],
        [pltpu.VMEM((members, nvars, plane, cells), jnp.float32)],
        kinds=[jnp.bfloat16, jnp.float32, jnp.float32],
    )
    side_a, side_b, gradient = call(
        scatter_kernel,
        dims,
        [strip, strip, (table_rows, cells)],
        [chosen, spread_out, strips, key, frac, weight, scale] + seen,
        [],
        [key],
        [pltpu.VMEM(key.shape, jnp.float32)],
    )
    side_a, side_b = exchange(side_a, side_b)
    held_source = [pltpu.VMEM(whole, jnp.float32), pltpu.VMEM((members, plane, cells), jnp.float32)]
    (own,) = call(local_kernel, dims, [whole], [powers, gradient, scale, side_a, perturb], [ens, stat], rates, held_source + copying)
    hv_ens, hv_stat = call(
        edge_kernel,
        dims,
        [(members, plane, cells), (nvars, plane, cells)],
        [own, side_b],
        [],
        rates,
        [pltpu.VMEM(whole, jnp.float32), pltpu.SemaphoreType.DMA((fields,))],
        HBM,
    )
    return hv_ens.reshape(ens_control.shape), hv_stat.reshape(static_control.shape)


def solution(mesh):
    placed = (
        P("grp", None, "tile", None),
        P("grp", None, None, "tile", None),
        P("grp", None, None, "tile", None),
        P("grp"),
        P(),
        P("grp"),
        P("grp", None, None),
        P("tile"),
        P("tile"),
        P("tile"),
        P("tile"),
        P(),
    )
    return jax.shard_map(
        per_device,
        mesh=mesh,
        in_specs=placed,
        out_specs=(P("grp", None, "tile", None), P("grp", None, None, "tile", None)),
        check_vma=False,
    )
```
